32 devices in a mesh: groups: 2 (over y), seq: 4 (over z), head: 2 (over x), sub: 2 (over core).
Axes of the slice: x: 2, y: 2, z: 4, core: 2. Of those that a mesh axis runs over, the one named last changes fastest.
Arguments:
- query_rows: bfloat16 [4096, 4096], P(('groups', 'seq', 'head', 'sub')), parts along dimension 0, may hold values from -6 to 6
- key_rows: bfloat16 [4096, 4096], P(('groups', 'seq', 'head', 'sub')), parts along dimension 0, may hold values from -6 to 6
- value_rows: bfloat16 [4096, 4096], P(('groups', 'seq', 'head', 'sub')), parts along dimension 0, may hold values from -6 to 6
- log_decay: float32 [32, 4096], P(('head', 'sub'), ('groups', 'seq')), parts along dimension 1, may hold values from -1 to 0
- norm_gain: float32 [32, 128], P(('head', 'sub')), may hold values from 0.25 to 1.75
- doc_lengths: int32 [64], P('groups'), parts along dimension 0, may hold values from 1 to 512, 2048 in all
Outputs:
- attended: bfloat16 [4096, 4096], P(('groups', 'seq', 'head', 'sub')), parts along dimension 0
The draws below stay inside these ranges and needn't reach their ends.
There are 2 independent parts, one for each index of `groups`. The reference program is written for one: setup_inputs(seed, part) draws one part's arguments, and reference() takes and returns one part's arrays. A program takes and returns all parts, laid end to end along the dimension named above; an argument that names none is the same for every part. Nothing has to cross between parts.
Inputs may be any that keep to these rules, and one draw needn't show every extreme that they name: `doc_lengths`: the lengths sum to 2048; the longest document has exactly 512 tokens.
All inputs are finite; a program needn't handle non-finite values.
Results may differ from the reference program's by a relative error of at most 0.0065.
Values may be sent and summed in bfloat16 or wider, within the bound.
No kernel may reach another device: no remote copies, remote signals or barrier semaphores. Data moves between devices by JAX's collectives and lax.ppermute only.
A program may use at most 64 MiB of HBM per device.

```python
import math
import jax
import jax.numpy as jnp
import numpy as np
from jax import lax

LOCAL_HEADS = 32
DH = 128
T_DEV = 128
DOCS = 32
PACKED_TOKENS = 2048


def draw_log_decay(key, part):
    random_subkeys = jax.random.split(key, 7)
    fast_share = 0.5
    fast_heads = jax.random.bernoulli(random_subkeys[0], fast_share, (LOCAL_HEADS, 1))
    fast_rate = jax.random.uniform(random_subkeys[1], (LOCAL_HEADS, 1), jnp.float32, 1.0 / 50.0, 1.0 / 30.0)
    slow_rate = jnp.exp(jax.random.uniform(random_subkeys[2], (LOCAL_HEADS, 1), jnp.float32, math.log(0.1), math.log(0.5))) / PACKED_TOKENS
    per_head_rate = jnp.where(fast_heads, fast_rate, slow_rate)
    length_factor = jnp.exp(jax.random.uniform(random_subkeys[3], (LOCAL_HEADS, PACKED_TOKENS // T_DEV), jnp.float32, math.log(0.4), math.log(2.5)))
    length_factor = jnp.repeat(length_factor, T_DEV, axis=1)
    decay_jitter = jax.random.uniform(random_subkeys[4], (LOCAL_HEADS, PACKED_TOKENS), jnp.float32, 0.5, 1.5)
    spike_positions = jax.random.randint(random_subkeys[5], (2,), 0, PACKED_TOKENS)
    spike_rows = jnp.any(jnp.arange(PACKED_TOKENS)[:, None] == spike_positions[None, :], axis=1)
    spike_decay_loss = jax.random.uniform(random_subkeys[6], (LOCAL_HEADS, PACKED_TOKENS), jnp.float32, 0.2, 0.4)
    decay_spikes = jnp.where(spike_rows[None, :], jnp.log1p(-spike_decay_loss), 0.0)
    return -per_head_rate * length_factor * decay_jitter + decay_spikes


def block_levels(stream_key, extent, cuts, least, largest):
    def one(dim, shards_of):
        steps = jax.random.uniform(jax.random.fold_in(jax.random.fold_in(stream_key, 6), dim), (shards_of,), jnp.float32, least / len(cuts), largest / len(cuts))
        return jnp.repeat(jnp.exp(steps), extent[dim] // shards_of).reshape((-1,) + (1,) * (len(extent) - dim - 1))

    gain = one(*cuts[0])
    for cut in cuts[1:]:
        gain = gain * one(*cut)
    return gain


def split_up(number_of, total, bound, lean):
    portions = [(1 << 20) // math.isqrt(rank ** lean) + 1 for rank in range(2, number_of + 1)]
    spare, counts = total - bound - (number_of - 1), [1] * (number_of - 1)
    while spare > 0:
        candidates = [i for i in range(number_of - 1) if counts[i] < bound]
        pool, budget = sum([portions[i] for i in candidates]), spare
        for i in candidates:
            addition = min(bound - counts[i], max(1, budget * portions[i] // pool), spare)
            counts[i] = counts[i] + addition
            spare = spare - addition
    return np.array([bound] + counts)


def uneven(key, number_of, total, most, skew):
    if number_of == 2:
        one = jax.random.randint(key, (), max(1, total - most), min(most, total - 1) + 1)
        return jnp.stack([one, total - one])
    sizes = jnp.asarray(split_up(number_of, total, most, skew), jnp.int32)
    pairs = (number_of - 1) // 2
    giver, receiver = sizes[1:1 + 2 * pairs:2], sizes[2:2 + 2 * pairs:2]
    slack = jnp.minimum(giver - 1, most - receiver)
    passed = jax.random.randint(jax.random.fold_in(key, 1), (pairs,), 0, 1 << 20) % (slack + 1)
    sizes = sizes.at[1:1 + 2 * pairs:2].set(giver - passed).at[2:2 + 2 * pairs:2].set(receiver + passed)
    return sizes[jax.random.permutation(jax.random.fold_in(key, 2), number_of)]


def normal_values(stream_key, dims, width, bound, cuts=(), kind=jnp.bfloat16):
    entries = width * jax.random.normal(stream_key, dims, jnp.float32)
    if cuts:
        entries = entries * block_levels(stream_key, dims, cuts, -0.22, 0.18)
    return jnp.clip(entries, -bound, bound).astype(kind)


def setup_inputs(seed: int = 0, part: int = 0) -> dict:
    streams_of = jax.random.split(jax.random.key(seed), 7)
    part_splits = jax.random.split(jax.random.fold_in(streams_of[6], part), 7)
    return {
        "query_rows": normal_values(part_splits[0], (PACKED_TOKENS, LOCAL_HEADS * DH), 1.0, 6.0, ((0, 16),)),
        "key_rows": normal_values(part_splits[1], (PACKED_TOKENS, LOCAL_HEADS * DH), 1.0, 6.0, ((0, 16),)),
        "value_rows": normal_values(part_splits[2], (PACKED_TOKENS, LOCAL_HEADS * DH), 1.0, 6.0, ((0, 16),)),
        "log_decay": draw_log_decay(jax.random.fold_in(jax.random.fold_in(streams_of[6], part), 71), part),
        "norm_gain": jnp.clip(1.0 + 0.15 * jax.random.normal(streams_of[4], (LOCAL_HEADS, DH), jnp.float32), 0.25, 1.75),
        "doc_lengths": uneven(part_splits[5], DOCS, PACKED_TOKENS, PACKED_TOKENS // 4, 2).astype(jnp.int32),
    }


def doc_index(doc_lengths, positions):
    doc_ends = jnp.cumsum(doc_lengths).astype(jnp.int32)
    doc_starts = doc_ends - doc_lengths.astype(jnp.int32)
    return lax.optimization_barrier(jnp.sum((doc_starts[None, :] <= positions[:, None]).astype(jnp.int32), axis=1)) - 1

def attend_head(query_head, key_head, value_head, decay_head, doc_now, doc_before, block_rows):
    head_width = query_head.shape[1]
    blocks = query_head.shape[0] // block_rows

    def advance(carry_state, inputs):
        query_blk, key_blk, value_blk, decay_blk, doc_blk, prior_blk = inputs
        running = jnp.cumsum(decay_blk)
        entry_doc = prior_blk[0]
        indices = jnp.arange(block_rows, dtype=jnp.int32)
        linked = (doc_blk[:, None] == doc_blk[None, :]) & (indices[:, None] >= indices[None, :])
        damping = jnp.exp(jnp.where(linked, running[:, None] - running[None, :], -1e+30))
        scores = jnp.dot(query_blk, key_blk.T, preferred_element_type=jnp.float32) * damping
        weights = scores.astype(jnp.bfloat16)
        carried = jnp.where(doc_blk == entry_doc, jnp.exp(running), 0.0)
        result = jnp.dot(weights, value_blk, preferred_element_type=jnp.float32)
        result = result + carried[:, None] * jnp.dot(query_blk.astype(jnp.float32), carry_state, precision=lax.Precision.HIGHEST)
        final_doc = doc_blk[-1]
        retain = jnp.where(final_doc == entry_doc, jnp.exp(running[-1]), 0.0)
        weight_rows = jnp.where(doc_blk == final_doc, jnp.exp(running[-1] - running), 0.0)
        weighted_keys = (key_blk.astype(jnp.float32) * weight_rows[:, None]).astype(jnp.bfloat16)
        update = jnp.dot(weighted_keys.T, value_blk, preferred_element_type=jnp.float32)
        return (retain * carry_state + update, result)
    shaped = (query_head.reshape(blocks, block_rows, head_width), key_head.reshape(blocks, block_rows, head_width), value_head.reshape(blocks, block_rows, head_width), decay_head.reshape(blocks, block_rows), doc_now.reshape(blocks, block_rows), doc_before.reshape(blocks, block_rows))
    final_state, results = lax.scan(advance, jnp.zeros((head_width, head_width), jnp.float32), shaped)
    return (results.reshape(-1, head_width), final_state)

def reference(query_rows, key_rows, value_rows, log_decay, norm_gain, doc_lengths):
    token_count = query_rows.shape[0]
    positions = jnp.arange(token_count, dtype=jnp.int32)
    doc_now = doc_index(doc_lengths, positions)
    doc_before = doc_index(doc_lengths, positions - 1)
    block_rows = min(256, token_count)
    queries = query_rows.reshape(token_count, LOCAL_HEADS, DH).transpose(1, 0, 2)
    keys_all = key_rows.reshape(token_count, LOCAL_HEADS, DH).transpose(1, 0, 2)
    values_all = value_rows.reshape(token_count, LOCAL_HEADS, DH).transpose(1, 0, 2)

    def per_head(inputs):
        query_head, key_head, value_head, decay_head = inputs
        result, final_state = attend_head(query_head, key_head, value_head, decay_head, doc_now, doc_before, block_rows)
        return result
    attended = lax.map(per_head, (queries, keys_all, values_all, log_decay))
    mean_square = lax.optimization_barrier(jnp.mean(attended * attended, axis=2, keepdims=True))
    normed = attended * lax.rsqrt(mean_square + 1e-06) * norm_gain[:, None, :]
    return normed.astype(jnp.bfloat16).transpose(1, 0, 2).reshape(token_count, LOCAL_HEADS * DH)
```

```python
import functools

import jax
import jax.numpy as jnp
from jax import lax
from jax.experimental import pallas as pl
from jax.experimental.pallas import tpu as pltpu
from jax.sharding import PartitionSpec as P

BF16 = jnp.bfloat16
F32 = jnp.float32
ANY = pl.BlockSpec(memory_space=pl.ANY)


def whole(*shape):
    zeros = (0,) * len(shape)
    return pl.BlockSpec(shape, lambda *_: zeros)


def rotate(x, axis, step):
    size = lax.axis_size(axis)
    return lax.ppermute(x, axis, [(i, (i + step) % size) for i in range(size)])


def shift(x, axis, step):
    size = lax.axis_size(axis)
    return lax.ppermute(x, axis, [(i, i + step) for i in range(size - step)])


def column(row, rows):
    return jnp.broadcast_to(row, (rows, row.shape[1])).T


def call(body, grid, in_specs, out_specs, out_shape, scratch=(), flops=0, moved=0, aliases=None):
    return pl.pallas_call(
        body,
        out_shape=out_shape,
        grid_spec=pltpu.PrefetchScalarGridSpec(
            num_scalar_prefetch=1,
            grid=grid,
            in_specs=in_specs,
            out_specs=out_specs,
            scratch_shapes=list(scratch),
        ),
        input_output_aliases=aliases or {},
        cost_estimate=pl.CostEstimate(flops=flops, bytes_accessed=moved, transcendentals=0),
    )


def places(chips):
    base = 3 * chips
    return dict(to_start=base, to_end=base + 1, first=base + 2, row=base + 3, second=base + 4)


def states_body(chips, cores, meta, *refs):
    decays = refs[:chips]
    docs, k_own, v_own, k_far, v_far = refs[chips : chips + 5]
    state_x, state_b, state_z, state_0, logs, coef = refs[chips + 5 : chips + 11]
    weight = refs[chips + 11]
    step = pl.program_id(0)
    core, chip = meta[0], meta[1]
    pieces = chips * cores
    per_block, rows = logs.shape[2], logs.shape[3]
    at = places(chips)

    @pl.when(step == 0)
    def tables():
        lane = lax.broadcasted_iota(jnp.int32, (per_block, rows), 1)
        for slot in range(chips):
            block = lax.rem(chip - slot + chips, chips)
            factors = []
            for piece in range(pieces):
                total = decays[slot][:, piece * rows : (piece + 1) * rows]
                reach = 1
                while reach < rows:
                    total = total + jnp.where(lane >= reach, pltpu.roll(total, reach, 1), 0.0)
                    reach *= 2
                logs[piece, block] = total
                end = jnp.broadcast_to(total[:, rows - 1 :], (per_block, rows))
                weight[piece, block] = jnp.exp(end - total) * docs[1, piece : piece + 1, :]
                passed = jnp.broadcast_to(docs[2, piece : piece + 1, rows - 1 :], (per_block, rows))
                factors.append(jnp.exp(end) * passed)
            through = []
            for c in range(chips):
                product = factors[c * cores]
                for u in range(1, cores):
                    product = product * factors[c * cores + u]
                through.append(product)
            one, zero = jnp.ones_like(through[0]), jnp.zeros_like(through[0])

            def between(low, high):
                product = one
                for c in range(low, high):
                    product = product * through[c]
                return product

            def pick(index, options):
                result = options[-1]
                for c in range(len(options) - 2, -1, -1):
                    result = jnp.where(index == c, options[c], result)
                return result

            to_start = pick(chip, [between(0, c) for c in range(chips)])
            coef[at["to_start"], block] = to_start
            coef[at["to_end"], block] = pick(chip, [between(0, c + 1) for c in range(chips)])
            coef[at["first"], block] = pick(chip, [factors[c * cores] for c in range(chips)])
            coef[at["second"], block] = pick(chip, [factors[c * cores + 1] for c in range(chips)])
            coef[at["row"], block] = between(0, chips)
            for back in range(chips):
                source = lax.rem(chip - back + chips, chips)
                coef[back, block] = pick(source, [between(c + 1, chips) for c in range(chips)])
                earlier = pick(
                    chip,
                    [
                        between(c - back + 1, c) if 0 <= c - back < c else zero
                        for c in range(chips)
                    ],
                )
                coef[chips + back, block] = earlier
                coef[2 * chips + back, block] = jnp.where(
                    (source < chip) & (back > 0), earlier, to_start
                )

    own = chip * cores + core
    far = chip * cores + (1 - core)
    is_first = core == 0
    for c in range(per_block):
        cols = slice(c * rows, (c + 1) * rows)
        sums = []
        for k_ref, v_ref, piece in ((k_own, v_own, own), (k_far, v_far, far)):
            keys = k_ref[:, cols].T.astype(F32) * weight[piece, step, c : c + 1, :]
            sums.append(jnp.dot(keys.astype(BF16), v_ref[:, cols], preferred_element_type=F32))
        first = jnp.where(is_first, sums[0], sums[1])
        last = jnp.where(is_first, sums[1], sums[0])
        state = last + coef[at["second"], step, c : c + 1, :] * first
        state_0[c] = first

        @pl.when(step < chips // 2)
        def by_x():
            state_x[c] = state.astype(BF16)

        @pl.when(step >= chips // 2)
        def by_z():
            state_b[c] = state.astype(BF16)
            state_z[c] = (coef[0, step, c : c + 1, :] * state).astype(BF16)


def block_body(cores, meta, logs_own, logs_far, docs, q, k, v, out):
    step = pl.program_id(0)
    core = meta[0]
    per_block, rows = logs_own.shape[2], logs_own.shape[3]
    mine = lax.rem(step, cores) == core
    doc = docs[0, pl.ds(meta[2], 1), :]
    docs_here = jnp.broadcast_to(doc, (rows, rows))
    t = lax.broadcasted_iota(jnp.int32, (rows, rows), 0)
    s = lax.broadcasted_iota(jnp.int32, (rows, rows), 1)
    linked = (docs_here.T == docs_here) & (t >= s)
    logs = jnp.where(mine, logs_own[0, 0], logs_far[0, 0])
    for c in range(per_block):
        cols = slice(c * rows, (c + 1) * rows)
        row = logs[c : c + 1, :]
        damping = jnp.exp(jnp.where(linked, column(row, rows) - row, -1e30))
        scores = lax.dot_general(
            q[:, cols], k[:, cols], (((1,), (1,)), ((), ())), preferred_element_type=F32
        )
        out[:, cols] = jnp.dot(
            (scores * damping).astype(BF16), v[:, cols], preferred_element_type=F32
        )


def first_join_body(chips, others, meta, *refs):
    coef, state_x, state_b, past_b = refs[:4]
    from_x = refs[4 : 4 + others]
    total = refs[4 + others]
    messages = refs[5 + others :]
    group = state_x.shape[0]
    step = pl.program_id(0)
    chip = meta[1]
    at = places(chips)
    per_block = coef.shape[2]
    for g in range(group):
        if group == per_block:
            block, c = step, g
        else:
            block, c = step // (per_block // group), None

        def factor(place, half):
            chosen = block + half * (chips // 2)
            if c is not None:
                return coef[place, chosen, c : c + 1, :]
            return coef[place, chosen, pl.ds(lax.rem(step, per_block // group) * group + g, 1), :]

        row_total = factor(0, 0) * state_x[g].astype(F32)
        for back in range(1, chips):
            row_total = row_total + factor(back, 0) * from_x[back - 1][g].astype(F32)
        total[g] = row_total.astype(BF16)
        past = past_b[g]
        ahead = (state_b[g].astype(F32) + factor(at["to_end"], 1) * past.astype(F32)).astype(BF16)
        for back in range(1, chips):
            messages[back - 1][g] = jnp.where(chip + back < chips, ahead, past)


def second_join_body(chips, others, meta, *refs):
    coef, first, past_a, past_b = refs[:4]
    from_a = refs[4 : 4 + others]
    from_b = refs[4 + others : 4 + 2 * others]
    keep, send = refs[4 + 2 * others :]
    group = keep.shape[0]
    step = pl.program_id(0)
    core = meta[0]
    at = places(chips)
    per_block = coef.shape[2]
    spread = per_block // group
    half_steps = (chips // 2) * spread
    block = step // spread
    offset = lax.rem(step, spread) * group
    for half, past_ref, others_refs, base in (
        (0, past_a, from_a, chips),
        (1, past_b, from_b, 2 * chips),
    ):

        @pl.when((step >= half_steps) == bool(half))
        def join():
            for g in range(group):

                def factor(place):
                    return coef[place, block, pl.ds(offset + g, 1), :]

                entering = factor(at["to_start"]) * past_ref[g].astype(F32)
                for back in range(1, chips):
                    entering = entering + factor(base + back) * others_refs[back - 1][g].astype(F32)
                later = (first[g] + factor(at["first"]) * entering).astype(BF16)
                entering = entering.astype(BF16)
                keep[g] = jnp.where(core == 0, entering, later)
                send[g] = jnp.where(core == 0, later, entering)


def finish_body(meta, logs, docs, gain, q, within, entering, *rest):
    out = rest[-1]
    per_block, rows = logs.shape[2], logs.shape[3]
    carry_rows = jnp.exp(logs[0, 0]) * docs[2, pl.ds(meta[2], 1), :]
    for c in range(per_block):
        cols = slice(c * rows, (c + 1) * rows)
        carried = column(carry_rows[c : c + 1, :], rows)
        result = within[:, cols] + carried * jnp.dot(
            q[:, cols], entering[c], preferred_element_type=F32
        )
        mean_square = jnp.mean(result * result, axis=1, keepdims=True)
        out[:, cols] = (result * lax.rsqrt(mean_square + 1e-06) * gain[0, c : c + 1, :]).astype(BF16)


def doc_tables(doc_lengths, row_start, pieces, rows):
    count = doc_lengths.shape[0]
    order = jnp.arange(count, dtype=jnp.int32)
    starts = jnp.sum(jnp.where(order[None, :] < order[:, None], doc_lengths[None, :], 0), axis=1)
    position = row_start + (
        jnp.arange(pieces, dtype=jnp.int32)[:, None] * rows
        + jnp.arange(rows, dtype=jnp.int32)[None, :]
    )
    firsts = row_start + jnp.arange(pieces, dtype=jnp.int32) * rows

    def index(at):
        return jnp.sum((starts <= at[..., None]).astype(jnp.int32), axis=-1)

    doc = index(position)
    same_end = doc == index(firsts + rows - 1)[:, None]
    same_before = doc == index(firsts - 1)[:, None]
    return jnp.stack([doc.astype(F32), same_end.astype(F32), same_before.astype(F32)])


def earlier_rows(value, row_factor, reach):
    total, factor, step = value, row_factor, 1
    while step < reach:
        before = shift(total, "seq", step).astype(F32)
        total = (total.astype(F32) + factor[:, None, :] * before).astype(BF16)
        factor = factor * shift(factor, "seq", step)
        step *= 2
    return shift(total, "seq", 1)


def per_device(query, key, value, log_decay, gain, doc_lengths):
    rows, width = query.shape
    per_block, row_tokens = log_decay.shape
    head_width = gain.shape[1]
    chips, cores, depth = lax.axis_size("head"), lax.axis_size("sub"), lax.axis_size("seq")
    assert cores == 2 and chips % 2 == 0 and rows == head_width
    pieces = chips * cores
    others = chips - 1
    heads = chips * per_block
    half = heads // 2
    block = per_block * head_width
    reach = max(1, -(-depth // 4))
    core, chip = lax.axis_index("sub"), lax.axis_index("head")
    meta = jnp.stack([core, chip, chip * cores + core]).astype(jnp.int32)

    decays = [log_decay] + [rotate(log_decay, "head", k) for k in range(1, chips)]
    key_far, value_far = rotate(key, "sub", 1), rotate(value, "sub", 1)
    docs = doc_tables(doc_lengths, lax.axis_index("seq") * row_tokens, pieces, rows)

    def sds(shape, kind):
        return jax.ShapeDtypeStruct(shape, kind)

    square = (head_width, head_width)
    cell = per_block * head_width * head_width
    n_coef = 3 * chips + 5
    mine = pl.BlockSpec((rows, block), lambda i, m: (0, i * cores + m[0]))
    mid = chips // 2
    low = pl.BlockSpec((per_block,) + square, lambda i, m: (jnp.minimum(i, mid - 1), 0, 0))
    high = pl.BlockSpec((per_block,) + square, lambda i, m: (jnp.maximum(i - mid, 0), 0, 0))
    every = pl.BlockSpec((per_block,) + square, lambda i, m: (i, 0, 0))
    log_shape = (pieces, chips, per_block, rows)
    coef_shape = (n_coef, chips, per_block, rows)
    state_x, state_b, state_z, first, logs, coef = call(
        functools.partial(states_body, chips, cores),
        (chips,),
        [whole(per_block, row_tokens)] * chips + [whole(3, pieces, rows)] + [mine] * 4,
        [low, high, high, every, whole(*log_shape), whole(*coef_shape)],
        [
            sds((half,) + square, BF16),
            sds((half,) + square, BF16),
            sds((half,) + square, BF16),
            sds((heads,) + square, F32),
            sds(log_shape, F32),
            sds(coef_shape, F32),
        ],
        [pltpu.VMEM(log_shape, F32)],
        flops=4 * rows * heads * head_width * head_width,
        moved=8 * rows * heads * head_width,
    )(meta, *decays, docs, key, value, key_far, value_far)

    logs_far = rotate(logs, "sub", 1)
    from_x = [rotate(state_x, "head", k) for k in range(1, chips)]
    row_factor = coef[places(chips)["row"]].reshape(heads, rows) if reach > 1 else None
    past_b = earlier_rows(state_z, row_factor[half:] if reach > 1 else None, reach)

    log_block = (1, 1, per_block, rows)
    here = pl.BlockSpec((rows, block), lambda j, m: (0, j))
    within = call(
        functools.partial(block_body, cores),
        (pieces,),
        [pl.BlockSpec(log_block, lambda j, m: (m[2], j // cores, 0, 0))] * 2
        + [whole(3, pieces, rows)]
        + [here] * 3,
        here,
        sds((rows, width), F32),
        flops=4 * rows * rows * width,
        moved=10 * rows * width,
    )(meta, logs, logs_far, docs, query, key, value)

    group = min(4, per_block)
    part = pl.BlockSpec((group,) + square, lambda i, m: (i, 0, 0))
    total, *messages = call(
        functools.partial(first_join_body, chips, others),
        (half // group,),
        [whole(*coef_shape)] + [part] * (3 + others),
        [part] * (1 + others),
        [sds((half,) + square, BF16)] * (1 + others),
        moved=12 * half * head_width * head_width,
    )(meta, coef, state_x, state_b, past_b, *from_x)

    past_a = earlier_rows(total, row_factor[:half] if reach > 1 else None, reach)
    from_b = [rotate(messages[k - 1], "head", k) for k in range(1, chips)]

    last = half // group - 1
    low_part = pl.BlockSpec((group,) + square, lambda i, m: (jnp.minimum(i, last), 0, 0))
    high_part = pl.BlockSpec((group,) + square, lambda i, m: (jnp.maximum(i - last - 1, 0), 0, 0))
    keep, send = call(
        functools.partial(second_join_body, chips, others),
        (heads // group,),
        [whole(*coef_shape), part, low_part, high_part] + [low_part] * others + [high_part] * others,
        [part, part],
        [sds((heads,) + square, BF16)] * 2,
        moved=12 * heads * head_width * head_width,
    )(meta, coef, first, past_a, past_b, *from_x, *from_b)
    received = rotate(send, "sub", 1)

    gain_rows = gains(gain, chips, cores)

    def finish(far, logs_used, entering, earlier):
        def place(i, m):
            return i * cores + (1 - m[0] if far else m[0])

        cols = pl.BlockSpec((rows, block), lambda i, m: (0, place(i, m)))
        return call(
            finish_body,
            (chips,),
            [
                pl.BlockSpec(log_block, lambda i, m: (m[2], i, 0, 0)),
                whole(3, pieces, rows),
                pl.BlockSpec((1, per_block, head_width), lambda i, m: (place(i, m), 0, 0)),
                cols,
                cols,
                every,
            ]
            + [ANY] * len(earlier),
            cols,
            sds((rows, width), BF16),
            flops=2 * rows * head_width * width // 2,
            moved=5 * rows * width,
            aliases={7: 0} if earlier else None,
        )(meta, logs_used, docs, gain_rows, query, within, entering, *earlier)

    out = finish(False, logs, keep, ())
    return finish(True, logs_far, received, (out,))


def gains(gain, chips, cores):
    core, chip = lax.axis_index("sub"), lax.axis_index("head")
    across = [gain] + [rotate(gain, "head", k) for k in range(1, chips)]
    own = jnp.stack([across[k] for k in range(chips)])
    order = (chip - jnp.arange(chips)) % chips
    own = jnp.zeros_like(own).at[order].set(own)
    far = rotate(own, "sub", 1)
    pair = jnp.stack([jnp.where(core == 0, own, far), jnp.where(core == 0, far, own)], axis=1)
    return pair.reshape((chips * cores,) + gain.shape)


def solution(mesh):
    rows = P(("groups", "seq", "head", "sub"), None)
    return jax.shard_map(
        per_device,
        mesh=mesh,
        in_specs=(rows, rows, rows, P(("head", "sub"), ("groups", "seq")), P(("head", "sub"), None), P("groups")),
        out_specs=rows,
        check_vma=False,
    )
```

```python
import functools

import jax
import jax.numpy as jnp
from jax import lax
from jax.experimental import pallas as pl
from jax.experimental.pallas import tpu as pltpu
from jax.sharding import PartitionSpec as P

BF16 = jnp.bfloat16
F32 = jnp.float32
ANY = pl.BlockSpec(memory_space=pl.ANY)
HBM = pl.BlockSpec(memory_space=pltpu.HBM)
VMEM = pl.BlockSpec(memory_space=pltpu.VMEM)
SMEM = pl.BlockSpec(memory_space=pltpu.SMEM)


def rotate(x, axis, step):
    size = lax.axis_size(axis)
    return lax.ppermute(x, axis, [(i, (i + step) % size) for i in range(size)])


def shift(x, axis, step):
    size = lax.axis_size(axis)
    return lax.ppermute(x, axis, [(i, i + step) for i in range(size - step)])


def column(row, rows):
    return jnp.broadcast_to(row, (rows, row.shape[1])).T


def call(body, out_shape, in_specs, out_specs, scratch=(), flops=0, moved=0, aliases=None, vmem=8 << 20):
    return pl.pallas_call(
        body,
        out_shape=out_shape,
        in_specs=in_specs,
        out_specs=out_specs,
        scratch_shapes=list(scratch),
        input_output_aliases=aliases or {},
        cost_estimate=pl.CostEstimate(flops=flops, bytes_accessed=moved, transcendentals=0),
        compiler_params=pltpu.CompilerParams(vmem_limit_bytes=vmem),
    )


def each(low, high, body):
    if high - low == 1:
        body(low)
    elif high > low:
        lax.fori_loop(low, high, lambda i, _: (body(i), 0)[1], 0)


def cols(place, c, width):
    start = (place * width[0] + c) * width[1]
    return pl.ds(start if isinstance(start, int) else pl.multiple_of(start, width[1]), width[1])


def places(chips):
    base = 3 * chips
    return dict(to_start=base, to_end=base + 1, first=base + 2, row=base + 3, second=base + 4)


def states_body(chips, cores, *refs):
    decays, gains = refs[:chips], refs[chips : 2 * chips]
    docs, k_own, v_own, k_far, v_far = refs[2 * chips : 2 * chips + 5]
    state_x, state_b, state_z, state_0, logs, coef = refs[2 * chips + 5 : 2 * chips + 11]
    weight = refs[2 * chips + 11]
    core, chip = lax.axis_index("sub"), lax.axis_index("head")
    pieces = chips * cores
    per_block, rows = logs.shape[2], logs.shape[3]
    at = places(chips)
    lane = lax.broadcasted_iota(jnp.int32, (per_block, rows), 1)
    for slot in range(chips):
        block = lax.rem(chip - slot + chips, chips)
        logs[pieces, block] = gains[slot][...]
        factors = []
        for piece in range(pieces):
            total = decays[slot][:, piece * rows : (piece + 1) * rows]
            reach = 1
            while reach < rows:
                total = total + jnp.where(lane >= reach, pltpu.roll(total, reach, 1), 0.0)
                reach *= 2
            logs[piece, block] = total
            end = jnp.broadcast_to(total[:, rows - 1 :], (per_block, rows))
            weight[piece, block] = jnp.exp(end - total) * docs[1, piece : piece + 1, :]
            passed = jnp.broadcast_to(docs[2, piece : piece + 1, rows - 1 :], (per_block, rows))
            factors.append(jnp.exp(end) * passed)
        through = []
        for c in range(chips):
            product = factors[c * cores]
            for u in range(1, cores):
                product = product * factors[c * cores + u]
            through.append(product)
        one, zero = jnp.ones_like(through[0]), jnp.zeros_like(through[0])

        def between(low, high):
            product = one
            for c in range(low, high):
                product = product * through[c]
            return product

        def pick(index, options):
            result = options[-1]
            for c in range(len(options) - 2, -1, -1):
                result = jnp.where(index == c, options[c], result)
            return result

        to_start = pick(chip, [between(0, c) for c in range(chips)])
        coef[at["to_start"], block] = to_start
        coef[at["to_end"], block] = pick(chip, [between(0, c + 1) for c in range(chips)])
        coef[at["first"], block] = pick(chip, [factors[c * cores] for c in range(chips)])
        coef[at["second"], block] = pick(chip, [factors[c * cores + 1] for c in range(chips)])
        coef[at["row"], block] = between(0, chips)
        for back in range(chips):
            source = lax.rem(chip - back + chips, chips)
            coef[back, block] = pick(source, [between(c + 1, chips) for c in range(chips)])
            earlier = pick(
                chip,
                [between(c - back + 1, c) if 0 <= c - back < c else zero for c in range(chips)],
            )
            coef[chips + back, block] = earlier
            coef[2 * chips + back, block] = jnp.where(
                (source < chip) & (back > 0), earlier, to_start
            )

    own = chip * cores + core
    far = chip * cores + (1 - core)
    is_first = core == 0
    mid = chips // 2

    def states_of(i, keep):
        for c in range(per_block):
            here = cols(i * cores + core, c, (per_block, rows))
            sums = []
            for k_ref, v_ref, piece in ((k_own, v_own, own), (k_far, v_far, far)):
                keys = k_ref[:, here].T.astype(F32) * weight[piece, i, c : c + 1, :]
                sums.append(jnp.dot(keys.astype(BF16), v_ref[:, here], preferred_element_type=F32))
            first = jnp.where(is_first, sums[0], sums[1])
            last = jnp.where(is_first, sums[1], sums[0])
            state_0[i, c] = first
            keep(i, c, last + coef[at["second"], i, c : c + 1, :] * first)

    def keep_x(i, c, state):
        state_x[i, c] = state.astype(BF16)

    def keep_z(i, c, state):
        state_b[i - mid, c] = state.astype(BF16)
        state_z[i - mid, c] = (coef[0, i, c : c + 1, :] * state).astype(BF16)

    each(mid, chips, lambda i: states_of(i, keep_z))
    each(0, mid, lambda i: states_of(i, keep_x))


def block_body(chips, cores, logs_own, logs_far, docs, q, k, v, out):
    core = lax.axis_index("sub")
    piece = lax.axis_index("head") * cores + core
    per_block, rows = logs_own.shape[2], logs_own.shape[3]
    doc = docs[0, pl.ds(piece, 1), :]
    docs_here = jnp.broadcast_to(doc, (rows, rows))
    t = lax.broadcasted_iota(jnp.int32, (rows, rows), 0)
    s = lax.broadcasted_iota(jnp.int32, (rows, rows), 1)
    linked = (docs_here.T == docs_here) & (t >= s)

    def heads_of(j):
        mine = lax.rem(j, cores) == core
        i = j // cores
        logs = jnp.where(mine, logs_own[piece, i], logs_far[piece, i])
        for c in range(per_block):
            here = cols(j, c, (per_block, rows))
            row = logs[c : c + 1, :]
            damping = jnp.exp(jnp.where(linked, column(row, rows) - row, -1e30))
            scores = lax.dot_general(
                q[:, here], k[:, here], (((1,), (1,)), ((), ())), preferred_element_type=F32
            )
            out[:, here] = jnp.dot(
                (scores * damping).astype(BF16), v[:, here], preferred_element_type=F32
            )

    each(0, chips * cores, heads_of)


def first_join_body(chips, others, *refs):
    coef, state_x, state_b, past_b = refs[:4]
    from_x = refs[4 : 4 + others]
    total = refs[4 + others]
    messages = refs[5 + others :]
    chip = lax.axis_index("head")
    at = places(chips)
    mid = chips // 2

    def join(i):
        for c in range(state_x.shape[1]):

            def factor(place, half):
                return coef[place, i + half * mid, c : c + 1, :]

            row_total = factor(0, 0) * state_x[i, c].astype(F32)
            for back in range(1, chips):
                row_total = row_total + factor(back, 0) * from_x[back - 1][i, c].astype(F32)
            total[i, c] = row_total.astype(BF16)
            past = past_b[i, c]
            ahead = state_b[i, c].astype(F32) + factor(at["to_end"], 1) * past.astype(F32)
            for back in range(1, chips):
                messages[back - 1][i, c] = jnp.where(
                    chip + back < chips, ahead.astype(BF16), past
                )

    each(0, mid, join)


def second_join_body(chips, others, *refs):
    coef, first, past_a, past_b = refs[:4]
    from_a = refs[4 : 4 + others]
    from_b = refs[4 + others : 4 + 2 * others]
    keep, send = refs[4 + 2 * others :]
    is_first = lax.axis_index("sub") == 0
    at = places(chips)
    mid = chips // 2

    def join(past, others_refs, base, offset, i):
        for c in range(past.shape[1]):

            def factor(place):
                return coef[place, i + offset, c : c + 1, :]

            entering = factor(at["to_start"]) * past[i, c].astype(F32)
            for back in range(1, chips):
                entering = entering + factor(base + back) * others_refs[back - 1][i, c].astype(F32)
            later = first[i + offset, c] + factor(at["first"]) * entering
            keep[i + offset, c] = jnp.where(is_first, entering, later).astype(BF16)
            send[i + offset, c] = jnp.where(is_first, later, entering).astype(BF16)

    each(0, mid, functools.partial(join, past_a, from_a, chips, 0))
    each(0, mid, functools.partial(join, past_b, from_b, 2 * chips, mid))


def finish_body(chips, cores, far, logs, docs, q, within, entering, *rest):
    out, buffer, sem = rest[-3:]
    core = lax.axis_index("sub")
    piece = lax.axis_index("head") * cores + core
    core = 1 - core if far else core
    per_block, rows = logs.shape[2], logs.shape[3]
    carries = docs[2, pl.ds(piece, 1), :]

    def copy(i):
        place = cols(i * cores + core, 0, (1, per_block * rows))
        return pltpu.make_async_copy(buffer.at[i], out.at[:, place], sem.at[i])

    def heads_of(i):
        carry_rows = jnp.exp(logs[piece, i]) * carries
        for c in range(per_block):
            here = cols(i * cores + core, c, (per_block, rows))
            result = within[:, here] + column(carry_rows[c : c + 1, :], rows) * jnp.dot(
                q[:, here], entering[i, c], preferred_element_type=F32
            )
            mean_square = jnp.mean(result * result, axis=1, keepdims=True)
            scaled = result * lax.rsqrt(mean_square + 1e-06) * logs[chips * cores, i, c : c + 1, :]
            buffer[i, :, c * rows : (c + 1) * rows] = scaled.astype(BF16)
        copy(i).start()

    each(0, chips, heads_of)
    for i in range(chips):
        copy(i).wait()


def prepare_body(lengths, q_far, k_far, v_far, q, k, v, docs, sems):
    copies = [
        pltpu.make_async_copy(source, target, sems.at[n])
        for n, (source, target) in enumerate(((k_far, k), (v_far, v), (q_far, q)))
    ]
    for copy in copies:
        copy.start()
    pieces, rows = docs.shape[1:]
    piece = lax.broadcasted_iota(jnp.int32, (pieces, rows), 0)
    lane = lax.broadcasted_iota(jnp.int32, (pieces, rows), 1)
    first = (lax.axis_index("seq") * pieces + piece) * rows
    here, before = jnp.zeros((pieces, rows), F32), jnp.zeros((pieces, rows), F32)
    start = 0
    for n in range(lengths.shape[0]):
        here += jnp.where(start <= first + lane, 1.0, 0.0)
        before += jnp.where(start < first, 1.0, 0.0)
        start = start + lengths[n]
    end = jnp.broadcast_to(here[:, rows - 1 :], (pieces, rows))
    docs[0] = here
    docs[1] = jnp.where(here == end, 1.0, 0.0)
    docs[2] = jnp.where(here == before, 1.0, 0.0)
    for copy in copies:
        copy.wait()


def earlier_rows(value, row_factor, reach):
    total, factor, step = value, row_factor, 1
    while step < reach:
        before = shift(total, "seq", step).astype(F32)
        total = (total.astype(F32) + factor[:, :, None, :] * before).astype(BF16)
        factor = factor * shift(factor, "seq", step)
        step *= 2
    return shift(total, "seq", 1)


def per_device(query, key, value, log_decay, gain, doc_lengths):
    rows, width = query.shape
    per_block, _ = log_decay.shape
    head_width = gain.shape[1]
    chips, cores, depth = lax.axis_size("head"), lax.axis_size("sub"), lax.axis_size("seq")
    assert cores == 2 and chips % 2 == 0 and rows == head_width
    pieces = chips * cores
    others = chips - 1
    mid = chips // 2
    reach = max(1, -(-depth // 4))

    def sds(shape, kind):
        return jax.ShapeDtypeStruct(shape, kind)

    key_far = rotate(key, "sub", 1)
    value_far = rotate(value, "sub", 1)
    decays = [log_decay] + [rotate(log_decay, "head", k) for k in range(1, chips)]
    gains = [gain] + [rotate(gain, "head", k) for k in range(1, chips)]
    query, key, value, docs = call(
        prepare_body,
        [sds((rows, width), BF16)] * 3 + [sds((3, pieces, rows), F32)],
        [SMEM] + [HBM] * 3,
        [VMEM] * 4,
        [pltpu.SemaphoreType.DMA((3,))],
        moved=12 * rows * width,
        vmem=67043328 - 28 * rows * width,
    )(doc_lengths, query, key, value)

    square = (per_block, head_width, head_width)
    area = per_block * head_width * head_width
    log_shape = (pieces + 1, chips, per_block, rows)
    coef_shape = (3 * chips + 5, chips, per_block, rows)
    state_x, state_b, state_z, first, logs, coef = call(
        functools.partial(states_body, chips, cores),
        [sds((mid,) + square, BF16)] * 3
        + [sds((chips,) + square, F32), sds(log_shape, F32), sds(coef_shape, F32)],
        [VMEM] * (2 * chips + 5),
        [VMEM] * 6,
        [pltpu.VMEM((pieces,) + log_shape[1:], F32)],
        flops=4 * rows * chips * area,
        moved=16 * chips * area,
    )(*decays, *gains, docs, key, value, key_far, value_far)

    past_b = earlier_rows(state_z, coef[places(chips)["row"], mid:] if reach > 1 else None, reach)
    from_x = [rotate(state_x, "head", k) for k in range(1, chips)]
    logs_far = rotate(logs, "sub", 1)

    within = call(
        functools.partial(block_body, chips, cores),
        sds((rows, width), F32),
        [VMEM] * 6,
        VMEM,
        flops=4 * rows * rows * width,
        moved=10 * rows * width,
    )(logs, logs_far, docs, query, key, value)

    total, *messages = call(
        functools.partial(first_join_body, chips, others),
        [sds((mid,) + square, BF16)] * (1 + others),
        [VMEM] * (4 + others),
        [VMEM] * (1 + others),
        moved=12 * mid * area,
    )(coef, state_x, state_b, past_b, *from_x)

    past_a = earlier_rows(total, coef[places(chips)["row"], :mid] if reach > 1 else None, reach)
    from_b = [rotate(messages[k - 1], "head", k) for k in range(1, chips)]

    keep, send = call(
        functools.partial(second_join_body, chips, others),
        [sds((chips,) + square, BF16)] * 2,
        [VMEM] * (4 + 2 * others),
        [VMEM] * 2,
        moved=12 * chips * area,
    )(coef, first, past_a, past_b, *from_x, *from_b)
    received = rotate(send, "sub", 1)

    def finish(far, logs_used, entering, earlier):
        return call(
            functools.partial(finish_body, chips, cores, far),
            sds((rows, width), BF16),
            [VMEM] * 5 + [ANY] * len(earlier),
            ANY,
            [pltpu.VMEM((chips, rows, per_block * rows), BF16), pltpu.SemaphoreType.DMA((chips,))],
            flops=rows * head_width * width,
            moved=5 * rows * width,
            aliases={5: 0} if earlier else None,
        )(logs_used, docs, query, within, entering, *earlier)

    out = finish(False, logs, keep, ())
    return finish(True, logs_far, received, (out,))


def solution(mesh):
    rows = P(("groups", "seq", "head", "sub"), None)

    return jax.shard_map(
        per_device,
        mesh=mesh,
        in_specs=(
            rows,
            rows,
            rows,
            P(("head", "sub"), ("groups", "seq")),
            P(("head", "sub"), None),
            P("groups"),
        ),
        out_specs=rows,
        check_vma=False,
    )
```

```python
import functools

import jax
import jax.numpy as jnp
from jax import lax
from jax.experimental import pallas as pl
from jax.experimental.pallas import tpu as pltpu
from jax.sharding import PartitionSpec as P

BF16 = jnp.bfloat16
F32 = jnp.float32
ANY = pl.BlockSpec(memory_space=pl.ANY)
HBM = pl.BlockSpec(memory_space=pltpu.HBM)
VMEM = pl.BlockSpec(memory_space=pltpu.VMEM)
SMEM = pl.BlockSpec(memory_space=pltpu.SMEM)


def rotate(x, axis, step):
    size = lax.axis_size(axis)
    return lax.ppermute(x, axis, [(i, (i + step) % size) for i in range(size)])


def shift(x, axis, step):
    size = lax.axis_size(axis)
    return lax.ppermute(x, axis, [(i, i + step) for i in range(size - step)])


def column(row, rows):
    return jnp.broadcast_to(row, (rows, row.shape[1])).T


def call(body, out_shape, in_specs, out_specs, scratch=(), flops=0, moved=0, aliases=None, vmem=8 << 20):
    return pl.pallas_call(
        body,
        out_shape=out_shape,
        in_specs=in_specs,
        out_specs=out_specs,
        scratch_shapes=list(scratch),
        input_output_aliases=aliases or {},
        cost_estimate=pl.CostEstimate(flops=flops, bytes_accessed=moved, transcendentals=0),
        compiler_params=pltpu.CompilerParams(vmem_limit_bytes=vmem),
    )


def each(low, high, body):
    if high - low == 1:
        body(low)
    elif high > low:
        lax.fori_loop(low, high, lambda i, _: (body(i), 0)[1], 0)


def cols(place, c, width):
    start = (place * width[0] + c) * width[1]
    return pl.ds(start if isinstance(start, int) else pl.multiple_of(start, width[1]), width[1])


def places(chips):
    base = 3 * chips
    return dict(to_start=base, to_end=base + 1, first=base + 2, row=base + 3, second=base + 4)


def states_of(chips, k_own, v_own, k_far, v_far, weight, coef, i, keep):
    cores = 2
    core, chip = lax.axis_index("sub"), lax.axis_index("head")
    own, far = chip * cores + core, chip * cores + (1 - core)
    per_block, rows = weight.shape[2:]
    at = places(chips)
    for c in range(per_block):
        here = slice(c * rows, (c + 1) * rows)
        sums = []
        for k_ref, v_ref, piece in ((k_own, v_own, own), (k_far, v_far, far)):
            keys = k_ref[i, :, here].T.astype(F32) * weight[piece, i, c : c + 1, :]
            sums.append(jnp.dot(keys.astype(BF16), v_ref[i, :, here], preferred_element_type=F32))
        first = jnp.where(core == 0, sums[0], sums[1])
        last = jnp.where(core == 0, sums[1], sums[0])
        keep(c, first, last + coef[at["second"], i, c : c + 1, :] * first)


def states_a_body(chips, cores, *refs):
    decays, gains = refs[:chips], refs[chips : 2 * chips]
    docs, *kv = refs[2 * chips : 2 * chips + 5]
    state_x, state_0, logs, coef, weight = refs[2 * chips + 5 :]
    chip = lax.axis_index("head")
    pieces = chips * cores
    per_block, rows = logs.shape[2], logs.shape[3]
    at = places(chips)
    lane = lax.broadcasted_iota(jnp.int32, (per_block, rows), 1)
    for slot in range(chips):
        block = lax.rem(chip - slot + chips, chips)
        logs[pieces, block] = gains[slot][...]
        factors = []
        for piece in range(pieces):
            total = decays[slot][:, piece * rows : (piece + 1) * rows]
            reach = 1
            while reach < rows:
                total = total + jnp.where(lane >= reach, pltpu.roll(total, reach, 1), 0.0)
                reach *= 2
            logs[piece, block] = total
            end = jnp.broadcast_to(total[:, rows - 1 :], (per_block, rows))
            weight[piece, block] = jnp.exp(end - total) * docs[1, piece : piece + 1, :]
            passed = jnp.broadcast_to(docs[2, piece : piece + 1, rows - 1 :], (per_block, rows))
            factors.append(jnp.exp(end) * passed)
        through = []
        for c in range(chips):
            product = factors[c * cores]
            for u in range(1, cores):
                product = product * factors[c * cores + u]
            through.append(product)
        one, zero = jnp.ones_like(through[0]), jnp.zeros_like(through[0])

        def between(low, high):
            product = one
            for c in range(low, high):
                product = product * through[c]
            return product

        def pick(index, options):
            result = options[-1]
            for c in range(len(options) - 2, -1, -1):
                result = jnp.where(index == c, options[c], result)
            return result

        to_start = pick(chip, [between(0, c) for c in range(chips)])
        coef[at["to_start"], block] = to_start
        coef[at["to_end"], block] = pick(chip, [between(0, c + 1) for c in range(chips)])
        coef[at["first"], block] = pick(chip, [factors[c * cores] for c in range(chips)])
        coef[at["second"], block] = pick(chip, [factors[c * cores + 1] for c in range(chips)])
        coef[at["row"], block] = between(0, chips)
        for back in range(chips):
            source = lax.rem(chip - back + chips, chips)
            coef[back, block] = pick(source, [between(c + 1, chips) for c in range(chips)])
            earlier = pick(
                chip,
                [between(c - back + 1, c) if 0 <= c - back < c else zero for c in range(chips)],
            )
            coef[chips + back, block] = earlier
            coef[2 * chips + back, block] = jnp.where(
                (source < chip) & (back > 0), earlier, to_start
            )


    def block(i):
        def keep(c, first, state):
            state_0[i, c] = first
            state_x[i, c] = state.astype(BF16)

        states_of(chips, *kv, weight, coef, i, keep)

    each(0, chips // 2, block)


def states_b_body(chips, weight, coef, *refs):
    kv = refs[:4]
    state_b, state_z, state_0 = refs[4:]
    mid = chips // 2

    def block(i):
        def keep(c, first, state):
            state_0[i - mid, c] = first
            state_b[i - mid, c] = state.astype(BF16)
            state_z[i - mid, c] = (coef[0, i, c : c + 1, :] * state).astype(BF16)

        states_of(chips, *kv, weight, coef, i, keep)

    each(mid, chips, block)


def within_body(chips, cores, far, logs, docs, q, k, v, out, carry):
    core = lax.axis_index("sub")
    piece = lax.axis_index("head") * cores + core
    core = 1 - core if far else core
    per_block, rows = logs.shape[2], logs.shape[3]
    docs_here = jnp.broadcast_to(docs[0, pl.ds(piece, 1), :], (rows, rows))
    t = lax.broadcasted_iota(jnp.int32, (rows, rows), 0)
    s = lax.broadcasted_iota(jnp.int32, (rows, rows), 1)
    linked = (docs_here.T == docs_here) & (t >= s)
    carries = column(docs[2, pl.ds(piece, 1), :], rows)

    def heads_of(i):
        for c in range(per_block):
            here = slice(c * rows, (c + 1) * rows)
            row = logs[piece, i, c : c + 1, :]
            down = column(row, rows)
            damping = jnp.exp(jnp.where(linked, down - row, -1e30))
            scores = lax.dot_general(
                q[:, cols(i * cores + core, c, (per_block, rows))],
                k[i, :, here],
                (((1,), (1,)), ((), ())),
                preferred_element_type=F32,
            )
            out[i, :, here] = jnp.dot(
                (scores * damping).astype(BF16), v[i, :, here], preferred_element_type=F32
            )
            carry[i, :, here] = jnp.exp(down) * carries

    each(0, chips, heads_of)


def row_total_body(chips, coef, state_x, *refs):
    from_x, total = refs[:-1], refs[-1]

    def join(i):
        for c in range(state_x.shape[1]):
            sum_ = coef[0, i, c : c + 1, :] * state_x[i, c].astype(F32)
            for back in range(1, chips):
                sum_ = sum_ + coef[back, i, c : c + 1, :] * from_x[back - 1][i, c].astype(F32)
            total[i, c] = sum_.astype(BF16)

    each(0, chips // 2, join)


def messages_body(chips, coef, state_b, past_b, *messages):
    chip = lax.axis_index("head")
    mid = chips // 2

    def join(i):
        for c in range(state_b.shape[1]):
            past = past_b[i, c]
            factor = coef[places(chips)["to_end"], i + mid, c : c + 1, :]
            ahead = (state_b[i, c].astype(F32) + factor * past.astype(F32)).astype(BF16)
            for back in range(1, chips):
                messages[back - 1][i, c] = jnp.where(chip + back < chips, ahead, past)

    each(0, mid, join)


def entering_body(chips, half, coef, first, past, *refs):
    others = refs[:-2]
    keep, send = refs[-2:]
    is_first = lax.axis_index("sub") == 0
    at = places(chips)
    mid = chips // 2
    base = (1 + half) * chips

    def join(i):
        for c in range(past.shape[1]):

            def factor(place):
                return coef[place, i + half * mid, c : c + 1, :]

            entering = factor(at["to_start"]) * past[i, c].astype(F32)
            for back in range(1, chips):
                entering = entering + factor(base + back) * others[back - 1][i, c].astype(F32)
            later = first[i, c] + factor(at["first"]) * entering
            keep[i, c] = jnp.where(is_first, entering, later).astype(BF16)
            send[i, c] = jnp.where(is_first, later, entering).astype(BF16)

    each(0, mid, join)


def finish_body(chips, cores, far, halves, logs, q, within, carry, *rest):
    out, buffer, sem = rest[-3:]
    entering = rest[: len(halves)]
    core = lax.axis_index("sub")
    core = 1 - core if far else core
    per_block, rows = logs.shape[2], logs.shape[3]
    mid = chips // 2

    def copy(i):
        place = cols(i * cores + core, 0, (1, per_block * rows))
        return pltpu.make_async_copy(buffer.at[i], out.at[:, place], sem.at[i])

    def heads_of(state, half, n):
        i = n + half * mid
        for c in range(per_block):
            here = slice(c * rows, (c + 1) * rows)
            result = within[i, :, here] + carry[i, :, here] * jnp.dot(
                q[:, cols(i * cores + core, c, (per_block, rows))],
                state[n, c],
                preferred_element_type=F32,
            )
            mean_square = jnp.mean(result * result, axis=1, keepdims=True)
            scaled = result * lax.rsqrt(mean_square + 1e-06) * logs[chips * cores, i, c : c + 1, :]
            buffer[i, :, here] = scaled.astype(BF16)
        copy(i).start()

    for half, state in zip(halves, entering):
        each(0, mid, functools.partial(heads_of, state, half))
    for half in halves:
        for n in range(mid):
            copy(n + half * mid).wait()


def block_copies(chips, cores, core, pairs, sems):
    width = pairs[0][1].shape[2]
    return [
        pltpu.make_async_copy(
            source.at[:, cols(i * cores + core, 0, (1, width))], target.at[i], sems.at[n, i]
        )
        for n, (source, target) in enumerate(pairs)
        for i in range(chips)
    ]


def slice_body(chips, cores, k_all, v_all, k, v, sems):
    copies = block_copies(
        chips, cores, 1 - lax.axis_index("sub"), ((k_all, k), (v_all, v)), sems
    )
    for copy in copies:
        copy.start()
    for copy in copies:
        copy.wait()


def prepare_body(chips, cores, lengths_all, q_all, k_all, v_all, q, k, v, docs, *scratch):
    lengths, sems, q_sem, length_sem = scratch
    copies = block_copies(chips, cores, lax.axis_index("sub"), ((k_all, k), (v_all, v)), sems)
    copies.append(pltpu.make_async_copy(q_all, q, q_sem))
    lengths_copy = pltpu.make_async_copy(lengths_all, lengths, length_sem)
    lengths_copy.start()
    for copy in copies:
        copy.start()
    lengths_copy.wait()
    pieces, rows = docs.shape[1:]
    piece = lax.broadcasted_iota(jnp.int32, (pieces, rows), 0)
    lane = lax.broadcasted_iota(jnp.int32, (pieces, rows), 1)
    first = (lax.axis_index("seq") * pieces + piece) * rows
    here, before = jnp.zeros((pieces, rows), F32), jnp.zeros((pieces, rows), F32)
    start = 0
    for n in range(lengths.shape[0]):
        here += jnp.where(start <= first + lane, 1.0, 0.0)
        before += jnp.where(start < first, 1.0, 0.0)
        start = start + lengths[n]
    end = jnp.broadcast_to(here[:, rows - 1 :], (pieces, rows))
    docs[0] = here
    docs[1] = jnp.where(here == end, 1.0, 0.0)
    docs[2] = jnp.where(here == before, 1.0, 0.0)
    for copy in copies:
        copy.wait()


def earlier_rows(value, row_factor, blocks, reach):
    total, step = value, 1
    factor = row_factor[blocks] if reach > 1 else None
    while step < reach:
        before = shift(total, "seq", step).astype(F32)
        total = (total.astype(F32) + factor[:, :, None, :] * before).astype(BF16)
        factor = factor * shift(factor, "seq", step)
        step *= 2
    return shift(total, "seq", 1)


def per_device(query, key, value, log_decay, gain, doc_lengths):
    rows, width = query.shape
    per_block, _ = log_decay.shape
    head_width = gain.shape[1]
    chips, cores, depth = lax.axis_size("head"), lax.axis_size("sub"), lax.axis_size("seq")
    assert cores == 2 and chips % 2 == 0 and rows == head_width
    pieces = chips * cores
    others = chips - 1
    mid = chips // 2
    reach = max(1, -(-depth // 4))

    def sds(shape, kind):
        return jax.ShapeDtypeStruct(shape, kind)

    square = (per_block, head_width, head_width)
    area = per_block * head_width * head_width
    block = (chips, rows, per_block * head_width)
    half = sds((mid,) + square, BF16)
    half_wide = sds((mid,) + square, F32)
    log_shape = (pieces + 1, chips, per_block, rows)
    coef_shape = (3 * chips + 5, chips, per_block, rows)

    key_send, value_send = call(
        functools.partial(slice_body, chips, cores),
        [sds(block, BF16)] * 2,
        [HBM] * 2,
        [VMEM] * 2,
        [pltpu.SemaphoreType.DMA((2, chips))],
        moved=8 * rows * width,
        vmem=67043328 - SLICE_ROOM * rows * width,
    )(key, value)
    key_far = rotate(key_send, "sub", 1)
    value_far = rotate(value_send, "sub", 1)
    decays = [log_decay] + [rotate(log_decay, "head", k) for k in range(1, chips)]
    gains = [gain] + [rotate(gain, "head", k) for k in range(1, chips)]
    query, key, value, docs = call(
        functools.partial(prepare_body, chips, cores),
        [sds((rows, width), BF16)] + [sds(block, BF16)] * 2 + [sds((3, pieces, rows), F32)],
        [HBM] * 4,
        [VMEM] * 4,
        [
            pltpu.SMEM(doc_lengths.shape, jnp.int32),
            pltpu.SemaphoreType.DMA((2, chips)),
            pltpu.SemaphoreType.DMA(()),
            pltpu.SemaphoreType.DMA(()),
        ],
        moved=12 * rows * width,
        vmem=67043328 - PREPARE_ROOM * rows * width,
    )(doc_lengths, query, key, value)

    kv = (key, value, key_far, value_far)
    state_x, first_a, logs, coef, weight = call(
        functools.partial(states_a_body, chips, cores),
        [half, half_wide]
        + [sds(log_shape, F32), sds(coef_shape, F32), sds((pieces,) + log_shape[1:], F32)],
        [VMEM] * (2 * chips + 5),
        [VMEM] * 5,
        flops=2 * rows * chips * area,
        moved=8 * chips * area,
    )(*decays, *gains, docs, *kv)
    from_x = [rotate(state_x, "head", k) for k in range(1, chips)]
    state_b, state_z, first_b = call(
        functools.partial(states_b_body, chips),
        [half, half, half_wide],
        [VMEM] * 6,
        [VMEM] * 3,
        flops=2 * rows * chips * area,
        moved=8 * chips * area,
    )(weight, coef, *kv)
    row_factor = coef[places(chips)["row"]] if reach > 1 else None
    past_b = earlier_rows(state_z, row_factor, slice(mid, chips), reach)
    logs_far = rotate(logs, "sub", 1)

    def within(far, *args):
        return call(
            functools.partial(within_body, chips, cores, far),
            [sds(block, F32)] * 2,
            [VMEM] * 5,
            [VMEM] * 2,
            flops=2 * rows * rows * width,
            moved=7 * rows * width,
        )(*args)

    within_own, carry_own = within(False, logs, docs, query, key, value)

    total = call(
        functools.partial(row_total_body, chips),
        half,
        [VMEM] * (2 + others),
        VMEM,
        moved=6 * mid * area,
    )(coef, state_x, *from_x)
    past_a = earlier_rows(total, row_factor, slice(0, mid), reach)

    messages = call(
        functools.partial(messages_body, chips),
        [half] * others,
        [VMEM] * 3,
        [VMEM] * others,
        moved=6 * mid * area,
    )(coef, state_b, past_b)
    from_b = [rotate(messages[k - 1], "head", k) for k in range(1, chips)]

    within_far, carry_far = within(True, logs_far, docs, query, key_send, value_send)

    def entering(which, first, past, arrived):
        return call(
            functools.partial(entering_body, chips, which),
            [half] * 2,
            [VMEM] * (3 + others),
            [VMEM] * 2,
            moved=8 * mid * area,
        )(coef, first, past, *arrived)

    def finish(far, halves, logs_used, local, carry, states, earlier):
        return call(
            functools.partial(finish_body, chips, cores, far, halves),
            sds((rows, width), BF16),
            [VMEM] * (4 + len(states)) + [ANY] * len(earlier),
            ANY,
            [pltpu.VMEM(block, BF16), pltpu.SemaphoreType.DMA((chips,))],
            flops=rows * head_width * width,
            moved=5 * rows * width,
            aliases={4 + len(states): 0} if earlier else None,
        )(logs_used, query, local, carry, *states, *earlier)

    keep_a, send_a = entering(0, first_a, past_a, from_x)
    far_a = rotate(send_a, "sub", 1)
    own = (logs, within_own, carry_own)
    out = finish(False, (0,), *own, (keep_a,), ())
    keep_b, send_b = entering(1, first_b, past_b, from_b)
    far_b = rotate(send_b, "sub", 1)
    out = finish(False, (1,), *own, (keep_b,), (out,))
    return finish(True, (0, 1), logs_far, within_far, carry_far, (far_a, far_b), (out,))


SLICE_ROOM = 22
PREPARE_ROOM = 26


def solution(mesh):
    rows = P(("groups", "seq", "head", "sub"), None)

    return jax.shard_map(
        per_device,
        mesh=mesh,
        in_specs=(
            rows,
            rows,
            rows,
            P(("head", "sub"), ("groups", "seq")),
            P(("head", "sub"), None),
            P("groups"),
        ),
        out_specs=rows,
        check_vma=False,
    )
```

```python
import functools

import jax
import jax.numpy as jnp
from jax import lax
from jax.experimental import pallas as pl
from jax.experimental.pallas import tpu as pltpu
from jax.sharding import PartitionSpec as P

BF16 = jnp.bfloat16
F32 = jnp.float32
ANY = pl.BlockSpec(memory_space=pl.ANY)
HBM = pl.BlockSpec(memory_space=pltpu.HBM)
VMEM = pl.BlockSpec(memory_space=pltpu.VMEM)
SMEM = pl.BlockSpec(memory_space=pltpu.SMEM)


def rotate(x, axis, step):
    size = lax.axis_size(axis)
    return lax.ppermute(x, axis, [(i, (i + step) % size) for i in range(size)])


def shift(x, axis, step):
    size = lax.axis_size(axis)
    return lax.ppermute(x, axis, [(i, i + step) for i in range(size - step)])


def column(row, rows):
    return jnp.broadcast_to(row, (rows, row.shape[1])).T


def call(body, out_shape, in_specs, out_specs, scratch=(), flops=0, moved=0, aliases=None, vmem=8 << 20):
    return pl.pallas_call(
        body,
        out_shape=out_shape,
        in_specs=in_specs,
        out_specs=out_specs,
        scratch_shapes=list(scratch),
        input_output_aliases=aliases or {},
        cost_estimate=pl.CostEstimate(flops=flops, bytes_accessed=moved, transcendentals=0),
        compiler_params=pltpu.CompilerParams(vmem_limit_bytes=vmem),
    )


def each(low, high, body):
    if high - low == 1:
        body(low)
    elif high > low:
        lax.fori_loop(low, high, lambda i, _: (body(i), 0)[1], 0)


def cols(place, c, width):
    start = (place * width[0] + c) * width[1]
    return pl.ds(start if isinstance(start, int) else pl.multiple_of(start, width[1]), width[1])


def places(chips):
    base = 3 * chips
    return dict(to_start=base, to_end=base + 1, first=base + 2, row=base + 3, second=base + 4)


def states_of(chips, k_own, v_own, k_far, v_far, weight, coef, i, keep):
    cores = 2
    core, chip = lax.axis_index("sub"), lax.axis_index("head")
    own, far = chip * cores + core, chip * cores + (1 - core)
    per_block, rows = weight.shape[2:]
    at = places(chips)
    for c in range(per_block):
        here = slice(c * rows, (c + 1) * rows)
        sums = []
        for k_ref, v_ref, piece in ((k_own, v_own, own), (k_far, v_far, far)):
            keys = k_ref[i, :, here].T.astype(F32) * weight[piece, i, c : c + 1, :]
            sums.append(jnp.dot(keys.astype(BF16), v_ref[i, :, here], preferred_element_type=F32))
        first = jnp.where(core == 0, sums[0], sums[1])
        last = jnp.where(core == 0, sums[1], sums[0])
        keep(c, first, last + coef[at["second"], i, c : c + 1, :] * first)


def states_a_body(chips, cores, *refs):
    decays = refs[:chips]
    docs, *kv = refs[chips : chips + 5]
    state_x, state_0, logs, coef, weight = refs[chips + 5 :]
    chip = lax.axis_index("head")
    pieces = chips * cores
    per_block, rows = logs.shape[2], logs.shape[3]
    at = places(chips)
    lane = lax.broadcasted_iota(jnp.int32, (per_block, rows), 1)
    for slot in range(chips):
        block = lax.rem(chip - slot + chips, chips)
        factors = []
        for piece in range(pieces):
            total = decays[slot][:, piece * rows : (piece + 1) * rows]
            reach = 1
            while reach < rows:
                total = total + jnp.where(lane >= reach, pltpu.roll(total, reach, 1), 0.0)
                reach *= 2
            logs[piece, block] = total
            end = jnp.broadcast_to(total[:, rows - 1 :], (per_block, rows))
            weight[piece, block] = jnp.exp(end - total) * docs[1, piece : piece + 1, :]
            passed = jnp.broadcast_to(docs[2, piece : piece + 1, rows - 1 :], (per_block, rows))
            factors.append(jnp.exp(end) * passed)
        through = []
        for c in range(chips):
            product = factors[c * cores]
            for u in range(1, cores):
                product = product * factors[c * cores + u]
            through.append(product)
        one, zero = jnp.ones_like(through[0]), jnp.zeros_like(through[0])

        def between(low, high):
            product = one
            for c in range(low, high):
                product = product * through[c]
            return product

        def pick(index, options):
            result = options[-1]
            for c in range(len(options) - 2, -1, -1):
                result = jnp.where(index == c, options[c], result)
            return result

        to_start = pick(chip, [between(0, c) for c in range(chips)])
        coef[at["to_start"], block] = to_start
        coef[at["to_end"], block] = pick(chip, [between(0, c + 1) for c in range(chips)])
        coef[at["first"], block] = pick(chip, [factors[c * cores] for c in range(chips)])
        coef[at["second"], block] = pick(chip, [factors[c * cores + 1] for c in range(chips)])
        coef[at["row"], block] = between(0, chips)
        for back in range(chips):
            source = lax.rem(chip - back + chips, chips)
            coef[back, block] = pick(source, [between(c + 1, chips) for c in range(chips)])
            earlier = pick(
                chip,
                [between(c - back + 1, c) if 0 <= c - back < c else zero for c in range(chips)],
            )
            coef[chips + back, block] = earlier
            coef[2 * chips + back, block] = jnp.where(
                (source < chip) & (back > 0), earlier, to_start
            )


    def block(i):
        def keep(c, first, state):
            state_0[i, c] = first
            state_x[i, c] = state.astype(BF16)

        states_of(chips, *kv, weight, coef, i, keep)

    each(0, chips // 2, block)


def states_b_body(chips, weight, coef, *refs):
    kv = refs[:4]
    state_b, state_z, state_0 = refs[4:]
    mid = chips // 2

    def block(i):
        def keep(c, first, state):
            state_0[i - mid, c] = first
            state_b[i - mid, c] = state.astype(BF16)
            state_z[i - mid, c] = (coef[0, i, c : c + 1, :] * state).astype(BF16)

        states_of(chips, *kv, weight, coef, i, keep)

    each(mid, chips, block)


def within_body(cores, far, blocks, logs, docs, q, k, v, out, carry):
    core = lax.axis_index("sub")
    piece = lax.axis_index("head") * cores + core
    core = 1 - core if far else core
    per_block, rows = logs.shape[2], logs.shape[3]
    docs_here = jnp.broadcast_to(docs[0, pl.ds(piece, 1), :], (rows, rows))
    t = lax.broadcasted_iota(jnp.int32, (rows, rows), 0)
    s = lax.broadcasted_iota(jnp.int32, (rows, rows), 1)
    linked = (docs_here.T == docs_here) & (t >= s)
    carries = column(docs[2, pl.ds(piece, 1), :], rows)

    def heads_of(i):
        for c in range(per_block):
            here = slice(c * rows, (c + 1) * rows)
            row = logs[piece, i, c : c + 1, :]
            down = column(row, rows)
            damping = jnp.exp(jnp.where(linked, down - row, -1e30))
            scores = lax.dot_general(
                q[:, cols(i * cores + core, c, (per_block, rows))],
                k[i, :, here],
                (((1,), (1,)), ((), ())),
                preferred_element_type=F32,
            )
            out[i - blocks[0], :, here] = jnp.dot(
                (scores * damping).astype(BF16), v[i, :, here], preferred_element_type=F32
            )
            carry[i - blocks[0], :, here] = jnp.exp(down) * carries

    each(*blocks, heads_of)


def row_total_body(chips, coef, state_x, *refs):
    from_x, total = refs[:-1], refs[-1]

    def join(i):
        for c in range(state_x.shape[1]):
            sum_ = coef[0, i, c : c + 1, :] * state_x[i, c].astype(F32)
            for back in range(1, chips):
                sum_ = sum_ + coef[back, i, c : c + 1, :] * from_x[back - 1][i, c].astype(F32)
            total[i, c] = sum_.astype(BF16)

    each(0, chips // 2, join)


def messages_body(chips, coef, state_b, past_b, *messages):
    chip = lax.axis_index("head")
    mid = chips // 2

    def join(i):
        for c in range(state_b.shape[1]):
            past = past_b[i, c]
            factor = coef[places(chips)["to_end"], i + mid, c : c + 1, :]
            ahead = (state_b[i, c].astype(F32) + factor * past.astype(F32)).astype(BF16)
            for back in range(1, chips):
                messages[back - 1][i, c] = jnp.where(chip + back < chips, ahead, past)

    each(0, mid, join)


def entering_body(chips, half, coef, first, past, *refs):
    others = refs[:-2]
    keep, send = refs[-2:]
    is_first = lax.axis_index("sub") == 0
    at = places(chips)
    mid = chips // 2
    base = (1 + half) * chips

    def join(i):
        for c in range(past.shape[1]):

            def factor(place):
                return coef[place, i + half * mid, c : c + 1, :]

            entering = factor(at["to_start"]) * past[i, c].astype(F32)
            for back in range(1, chips):
                entering = entering + factor(base + back) * others[back - 1][i, c].astype(F32)
            later = first[i, c] + factor(at["first"]) * entering
            keep[i, c] = jnp.where(is_first, entering, later).astype(BF16)
            send[i, c] = jnp.where(is_first, later, entering).astype(BF16)

    each(0, mid, join)


def finish_heads(chips, cores, far, half, gains, q, within, carry, state, n, put):
    core, chip = lax.axis_index("sub"), lax.axis_index("head")
    core = 1 - core if far else core
    i = n + half * (chips // 2)
    per_block, rows = gains[0].shape[0], q.shape[0]
    slot = lax.rem(chip - i + chips, chips)
    gain = gains[0][...]
    for k in range(1, chips):
        gain = jnp.where(slot == k, gains[k][...], gain)
    for c in range(per_block):
        here = slice(c * rows, (c + 1) * rows)
        result = within[n, :, here] + carry[n, :, here] * jnp.dot(
            q[:, cols(i * cores + core, c, (per_block, rows))],
            state[n, c],
            preferred_element_type=F32,
        )
        mean_square = jnp.mean(result * result, axis=1, keepdims=True)
        put(here, (result * lax.rsqrt(mean_square + 1e-06) * gain[c : c + 1, :]).astype(BF16))


def finish_own_body(chips, cores, half, *refs):
    gains, (q, within, carry, state, out) = refs[:chips], refs[chips:]

    def block(n):
        def put(here, value):
            out[n, :, here] = value

        finish_heads(chips, cores, False, half, gains, q, within, carry, state, n, put)

    each(0, chips // 2, block)


def finish_far_body(chips, cores, *refs):
    gains = refs[:chips]
    q, within_a, carry_a, within_b, carry_b, state_a, state_b, own_a, own_b = refs[chips : chips + 9]
    out, buffer, sem, own_sem = refs[chips + 9 :]
    core = lax.axis_index("sub")
    mid = chips // 2
    width = buffer.shape[2]

    def copy(source, i, place, sem):
        target = out.at[:, cols(i * cores + place, 0, (1, width))]
        return pltpu.make_async_copy(source, target, sem.at[i])

    copies = []
    for half, own in enumerate((own_a, own_b)):
        for n in range(mid):
            i = n + half * mid
            copies.append(copy(own.at[n], i, core, own_sem))
            copies[-1].start()
    for half, local, carry, state in ((0, within_a, carry_a, state_a), (1, within_b, carry_b, state_b)):
        for n in range(mid):
            i = n + half * mid

            def put(here, value):
                buffer[i, :, here] = value

            finish_heads(chips, cores, True, half, gains, q, local, carry, state, n, put)
            copies.append(copy(buffer.at[i], i, 1 - core, sem))
            copies[-1].start()
    for one in copies:
        one.wait()


def block_copies(chips, cores, core, pairs, sems):
    width = pairs[0][1].shape[2]
    return [
        pltpu.make_async_copy(
            source.at[:, cols(i * cores + core, 0, (1, width))], target.at[i], sems.at[n, i]
        )
        for n, (source, target) in enumerate(pairs)
        for i in range(chips)
    ]


def slice_body(chips, cores, k_all, v_all, k, v, sems):
    copies = block_copies(
        chips, cores, 1 - lax.axis_index("sub"), ((k_all, k), (v_all, v)), sems
    )
    for copy in copies:
        copy.start()
    for copy in copies:
        copy.wait()


def prepare_body(chips, cores, lengths_all, k_all, v_all, k, v, docs, *scratch):
    lengths, sems, length_sem = scratch
    copies = block_copies(chips, cores, lax.axis_index("sub"), ((k_all, k), (v_all, v)), sems)
    lengths_copy = pltpu.make_async_copy(lengths_all, lengths, length_sem)
    lengths_copy.start()
    for copy in copies:
        copy.start()
    lengths_copy.wait()
    pieces, rows = docs.shape[1:]
    piece = lax.broadcasted_iota(jnp.int32, (pieces, rows), 0)
    lane = lax.broadcasted_iota(jnp.int32, (pieces, rows), 1)
    first = (lax.axis_index("seq") * pieces + piece) * rows
    here, before = jnp.zeros((pieces, rows), F32), jnp.zeros((pieces, rows), F32)
    start = 0
    for n in range(lengths.shape[0]):
        here += jnp.where(start <= first + lane, 1.0, 0.0)
        before += jnp.where(start < first, 1.0, 0.0)
        start = start + lengths[n]
    end = jnp.broadcast_to(here[:, rows - 1 :], (pieces, rows))
    docs[0] = here
    docs[1] = jnp.where(here == end, 1.0, 0.0)
    docs[2] = jnp.where(here == before, 1.0, 0.0)
    for copy in copies:
        copy.wait()


def earlier_rows(value, row_factor, blocks, reach):
    total, step = value, 1
    factor = row_factor[blocks] if reach > 1 else None
    while step < reach:
        before = shift(total, "seq", step).astype(F32)
        total = (total.astype(F32) + factor[:, :, None, :] * before).astype(BF16)
        factor = factor * shift(factor, "seq", step)
        step *= 2
    return shift(total, "seq", 1)


def per_device(query, key, value, log_decay, gain, doc_lengths):
    rows, width = query.shape
    per_block, _ = log_decay.shape
    head_width = gain.shape[1]
    chips, cores, depth = lax.axis_size("head"), lax.axis_size("sub"), lax.axis_size("seq")
    assert cores == 2 and chips % 2 == 0 and rows == head_width
    pieces = chips * cores
    others = chips - 1
    mid = chips // 2
    reach = max(1, -(-depth // 4))

    def sds(shape, kind):
        return jax.ShapeDtypeStruct(shape, kind)

    square = (per_block, head_width, head_width)
    area = per_block * head_width * head_width
    block = (chips, rows, per_block * head_width)
    half = sds((mid,) + square, BF16)
    half_wide = sds((mid,) + square, F32)
    log_shape = (pieces, chips, per_block, rows)
    coef_shape = (3 * chips + 5, chips, per_block, rows)

    key_send, value_send = call(
        functools.partial(slice_body, chips, cores),
        [sds(block, BF16)] * 2,
        [HBM] * 2,
        [VMEM] * 2,
        [pltpu.SemaphoreType.DMA((2, chips))],
        moved=8 * rows * width,
        vmem=67043328 - SLICE_ROOM * rows * width,
    )(key, value)
    key_far = rotate(key_send, "sub", 1)
    value_far = rotate(value_send, "sub", 1)
    decays = [log_decay] + [rotate(log_decay, "head", k) for k in range(1, chips)]
    key, value, docs = call(
        functools.partial(prepare_body, chips, cores),
        [sds(block, BF16)] * 2 + [sds((3, pieces, rows), F32)],
        [HBM] * 3,
        [VMEM] * 3,
        [
            pltpu.SMEM(doc_lengths.shape, jnp.int32),
            pltpu.SemaphoreType.DMA((2, chips)),
            pltpu.SemaphoreType.DMA(()),
        ],
        moved=12 * rows * width,
        vmem=67043328 - PREPARE_ROOM * rows * width,
    )(doc_lengths, key, value)

    kv = (key, value, key_far, value_far)
    state_x, first_a, logs, coef, weight = call(
        functools.partial(states_a_body, chips, cores),
        [half, half_wide]
        + [sds(log_shape, F32), sds(coef_shape, F32), sds(log_shape, F32)],
        [VMEM] * (chips + 5),
        [VMEM] * 5,
        flops=2 * rows * chips * area,
        moved=8 * chips * area,
    )(*decays, docs, *kv)
    from_x = [rotate(state_x, "head", k) for k in range(1, chips)]
    state_b, state_z, first_b = call(
        functools.partial(states_b_body, chips),
        [half, half, half_wide],
        [VMEM] * 6,
        [VMEM] * 3,
        flops=2 * rows * chips * area,
        moved=8 * chips * area,
    )(weight, coef, *kv)
    row_factor = coef[places(chips)["row"]] if reach > 1 else None
    past_b = earlier_rows(state_z, row_factor, slice(mid, chips), reach)
    logs_far = rotate(logs, "sub", 1)

    def within(far, blocks, *args):
        return call(
            functools.partial(within_body, cores, far, blocks),
            [sds((mid,) + block[1:], F32)] * 2,
            [VMEM] * 5,
            [VMEM] * 2,
            flops=rows * rows * width,
            moved=4 * rows * width,
        )(*args)

    low, high = (0, mid), (mid, chips)
    own = (logs, docs, query, key, value)
    own_a = within(False, low, *own)

    total = call(
        functools.partial(row_total_body, chips),
        half,
        [VMEM] * (2 + others),
        VMEM,
        moved=6 * mid * area,
    )(coef, state_x, *from_x)
    past_a = earlier_rows(total, row_factor, slice(0, mid), reach)

    messages = call(
        functools.partial(messages_body, chips),
        [half] * others,
        [VMEM] * 3,
        [VMEM] * others,
        moved=6 * mid * area,
    )(coef, state_b, past_b)
    from_b = [rotate(messages[k - 1], "head", k) for k in range(1, chips)]

    gains = [gain] + [rotate(gain, "head", k) for k in range(1, chips)]
    own_b = within(False, high, *own)
    far = (logs_far, docs, query, key_send, value_send)
    far_low = within(True, low, *far)
    gains_far = [rotate(part, "sub", 1) for part in gains]
    far_high = within(True, high, *far)

    def entering(which, first, past, arrived):
        return call(
            functools.partial(entering_body, chips, which),
            [half] * 2,
            [VMEM] * (3 + others),
            [VMEM] * 2,
            moved=8 * mid * area,
        )(coef, first, past, *arrived)

    def finish_own(which, local, state):
        return call(
            functools.partial(finish_own_body, chips, cores, which),
            sds((mid,) + block[1:], BF16),
            [VMEM] * (chips + 4),
            VMEM,
            flops=rows * head_width * width // 2,
            moved=3 * rows * width,
        )(*gains, query, *local, state)

    keep_a, send_a = entering(0, first_a, past_a, from_x)
    far_a = rotate(send_a, "sub", 1)
    out_a = finish_own(0, own_a, keep_a)
    keep_b, send_b = entering(1, first_b, past_b, from_b)
    far_b = rotate(send_b, "sub", 1)
    out_b = finish_own(1, own_b, keep_b)
    return call(
        functools.partial(finish_far_body, chips, cores),
        sds((rows, width), BF16),
        [VMEM] * (chips + 9),
        ANY,
        [pltpu.VMEM(block, BF16)] + [pltpu.SemaphoreType.DMA((chips,))] * 2,
        flops=rows * head_width * width,
        moved=7 * rows * width,
    )(*gains_far, query, *far_low, *far_high, far_a, far_b, out_a, out_b)


SLICE_ROOM = 22
PREPARE_ROOM = 24


def solution(mesh):
    rows = P(("groups", "seq", "head", "sub"), None)

    return jax.shard_map(
        per_device,
        mesh=mesh,
        in_specs=(
            rows,
            rows,
            rows,
            P(("head", "sub"), ("groups", "seq")),
            P(("head", "sub"), None),
            P("groups"),
        ),
        out_specs=rows,
        check_vma=False,
    )
```

```python
import functools

import jax
import jax.numpy as jnp
from jax import lax
from jax.experimental import pallas as pl
from jax.experimental.pallas import tpu as pltpu
from jax.sharding import PartitionSpec as P

BF16 = jnp.bfloat16
F32 = jnp.float32
ANY = pl.BlockSpec(memory_space=pl.ANY)
HBM = pl.BlockSpec(memory_space=pltpu.HBM)
VMEM = pl.BlockSpec(memory_space=pltpu.VMEM)
SMEM = pl.BlockSpec(memory_space=pltpu.SMEM)


def rotate(x, axis, step):
    size = lax.axis_size(axis)
    return lax.ppermute(x, axis, [(i, (i + step) % size) for i in range(size)])


def shift(x, axis, step):
    size = lax.axis_size(axis)
    return lax.ppermute(x, axis, [(i, i + step) for i in range(size - step)])


def column(row, rows):
    return jnp.broadcast_to(row, (rows, row.shape[1])).T


def call(body, out_shape, in_specs, out_specs, scratch=(), flops=0, moved=0, aliases=None, vmem=8 << 20):
    return pl.pallas_call(
        body,
        out_shape=out_shape,
        in_specs=in_specs,
        out_specs=out_specs,
        scratch_shapes=list(scratch),
        input_output_aliases=aliases or {},
        cost_estimate=pl.CostEstimate(flops=flops, bytes_accessed=moved, transcendentals=0),
        compiler_params=pltpu.CompilerParams(vmem_limit_bytes=vmem),
    )


def each(low, high, body):
    if high - low == 1:
        body(low)
    elif high > low:
        lax.fori_loop(low, high, lambda i, _: (body(i), 0)[1], 0)


def cols(place, c, width):
    start = (place * width[0] + c) * width[1]
    return pl.ds(start if isinstance(start, int) else pl.multiple_of(start, width[1]), width[1])


def places(chips):
    base = 3 * chips
    return dict(to_start=base, to_end=base + 1, first=base + 2, row=base + 3, second=base + 4)


def states_of(chips, k_own, v_own, k_far, v_far, weight, coef, i, keep):
    cores = 2
    core, chip = lax.axis_index("sub"), lax.axis_index("head")
    own, far = chip * cores + core, chip * cores + (1 - core)
    per_block, rows = weight.shape[2:]
    at = places(chips)
    for c in range(per_block):
        here = slice(c * rows, (c + 1) * rows)
        sums = []
        for k_ref, v_ref, piece in ((k_own, v_own, own), (k_far, v_far, far)):
            keys = k_ref[i, :, here].T.astype(F32) * weight[piece, i, c : c + 1, :]
            sums.append(jnp.dot(keys.astype(BF16), v_ref[i, :, here], preferred_element_type=F32))
        first = jnp.where(core == 0, sums[0], sums[1])
        last = jnp.where(core == 0, sums[1], sums[0])
        keep(c, first, last + coef[at["second"], i, c : c + 1, :] * first)


def states_a_body(chips, cores, *refs):
    decays = refs[:chips]
    docs, *kv = refs[chips : chips + 5]
    state_x, state_0, logs, coef, weight = refs[chips + 5 :]
    chip = lax.axis_index("head")
    pieces = chips * cores
    per_block, rows = logs.shape[2], logs.shape[3]
    at = places(chips)
    lane = lax.broadcasted_iota(jnp.int32, (per_block, rows), 1)
    for slot in range(chips):
        block = lax.rem(chip - slot + chips, chips)
        factors = []
        for piece in range(pieces):
            total = decays[slot][:, piece * rows : (piece + 1) * rows]
            reach = 1
            while reach < rows:
                total = total + jnp.where(lane >= reach, pltpu.roll(total, reach, 1), 0.0)
                reach *= 2
            logs[piece, block] = total
            end = jnp.broadcast_to(total[:, rows - 1 :], (per_block, rows))
            weight[piece, block] = jnp.exp(end - total) * docs[1, piece : piece + 1, :]
            passed = jnp.broadcast_to(docs[2, piece : piece + 1, rows - 1 :], (per_block, rows))
            factors.append(jnp.exp(end) * passed)
        through = []
        for c in range(chips):
            product = factors[c * cores]
            for u in range(1, cores):
                product = product * factors[c * cores + u]
            through.append(product)
        one, zero = jnp.ones_like(through[0]), jnp.zeros_like(through[0])

        def between(low, high):
            product = one
            for c in range(low, high):
                product = product * through[c]
            return product

        def pick(index, options):
            result = options[-1]
            for c in range(len(options) - 2, -1, -1):
                result = jnp.where(index == c, options[c], result)
            return result

        to_start = pick(chip, [between(0, c) for c in range(chips)])
        coef[at["to_start"], block] = to_start
        coef[at["to_end"], block] = pick(chip, [between(0, c + 1) for c in range(chips)])
        coef[at["first"], block] = pick(chip, [factors[c * cores] for c in range(chips)])
        coef[at["second"], block] = pick(chip, [factors[c * cores + 1] for c in range(chips)])
        coef[at["row"], block] = between(0, chips)
        for back in range(chips):
            source = lax.rem(chip - back + chips, chips)
            coef[back, block] = pick(source, [between(c + 1, chips) for c in range(chips)])
            earlier = pick(
                chip,
                [between(c - back + 1, c) if 0 <= c - back < c else zero for c in range(chips)],
            )
            coef[chips + back, block] = earlier
            coef[2 * chips + back, block] = jnp.where(
                (source < chip) & (back > 0), earlier, to_start
            )


    def block(i):
        def keep(c, first, state):
            state_0[i, c] = first
            state_x[i, c] = state.astype(BF16)

        states_of(chips, *kv, weight, coef, i, keep)

    each(0, chips // 2, block)


def states_b_body(chips, weight, coef, *refs):
    kv = refs[:4]
    state_b, state_z, state_0 = refs[4:]
    mid = chips // 2

    def block(i):
        def keep(c, first, state):
            state_0[i - mid, c] = first
            state_b[i - mid, c] = state.astype(BF16)
            state_z[i - mid, c] = (coef[0, i, c : c + 1, :] * state).astype(BF16)

        states_of(chips, *kv, weight, coef, i, keep)

    each(mid, chips, block)


def within_body(cores, far, blocks, logs, docs, q, k, v, out, carry):
    core = lax.axis_index("sub")
    piece = lax.axis_index("head") * cores + core
    core = 1 - core if far else core
    per_block, rows = logs.shape[2], logs.shape[3]
    docs_here = jnp.broadcast_to(docs[0, pl.ds(piece, 1), :], (rows, rows))
    t = lax.broadcasted_iota(jnp.int32, (rows, rows), 0)
    s = lax.broadcasted_iota(jnp.int32, (rows, rows), 1)
    linked = (docs_here.T == docs_here) & (t >= s)
    carries = column(docs[2, pl.ds(piece, 1), :], rows)

    def heads_of(i):
        for c in range(per_block):
            here = slice(c * rows, (c + 1) * rows)
            row = logs[piece, i, c : c + 1, :]
            down = column(row, rows)
            damping = jnp.exp(jnp.where(linked, down - row, -1e30))
            scores = lax.dot_general(
                q[:, cols(i * cores + core, c, (per_block, rows))],
                k[i, :, here],
                (((1,), (1,)), ((), ())),
                preferred_element_type=F32,
            )
            out[i - blocks[0], :, here] = jnp.dot(
                (scores * damping).astype(BF16), v[i, :, here], preferred_element_type=F32
            )
            carry[i - blocks[0], :, here] = jnp.exp(down) * carries

    each(*blocks, heads_of)


def row_total_body(chips, coef, state_x, *refs):
    from_x, total = refs[:-1], refs[-1]

    def join(i):
        for c in range(state_x.shape[1]):
            sum_ = coef[0, i, c : c + 1, :] * state_x[i, c].astype(F32)
            for back in range(1, chips):
                sum_ = sum_ + coef[back, i, c : c + 1, :] * from_x[back - 1][i, c].astype(F32)
            total[i, c] = sum_.astype(BF16)

    each(0, chips // 2, join)


def messages_body(chips, coef, state_b, past_b, *messages):
    chip = lax.axis_index("head")
    mid = chips // 2

    def join(i):
        for c in range(state_b.shape[1]):
            past = past_b[i, c]
            factor = coef[places(chips)["to_end"], i + mid, c : c + 1, :]
            ahead = (state_b[i, c].astype(F32) + factor * past.astype(F32)).astype(BF16)
            for back in range(1, chips):
                messages[back - 1][i, c] = jnp.where(chip + back < chips, ahead, past)

    each(0, mid, join)


def entering_body(chips, half, coef, first, past, *refs):
    others = refs[:-2]
    keep, send = refs[-2:]
    is_first = lax.axis_index("sub") == 0
    at = places(chips)
    mid = chips // 2
    base = (1 + half) * chips

    def join(i):
        for c in range(past.shape[1]):

            def factor(place):
                return coef[place, i + half * mid, c : c + 1, :]

            entering = factor(at["to_start"]) * past[i, c].astype(F32)
            for back in range(1, chips):
                entering = entering + factor(base + back) * others[back - 1][i, c].astype(F32)
            later = first[i, c] + factor(at["first"]) * entering
            keep[i, c] = jnp.where(is_first, entering, later).astype(BF16)
            send[i, c] = jnp.where(is_first, later, entering).astype(BF16)

    each(0, mid, join)


def finish_heads(chips, cores, far, half, gains, q, within, carry, state, n, put):
    core, chip = lax.axis_index("sub"), lax.axis_index("head")
    core = 1 - core if far else core
    i = n + half * (chips // 2)
    per_block, rows = gains[0].shape[0], q.shape[0]
    slot = lax.rem(chip - i + chips, chips)
    gain = gains[0][...]
    for k in range(1, chips):
        gain = jnp.where(slot == k, gains[k][...], gain)
    for c in range(per_block):
        here = slice(c * rows, (c + 1) * rows)
        result = within[n, :, here] + carry[n, :, here] * jnp.dot(
            q[:, cols(i * cores + core, c, (per_block, rows))],
            state[n, c],
            preferred_element_type=F32,
        )
        mean_square = jnp.mean(result * result, axis=1, keepdims=True)
        put(here, (result * lax.rsqrt(mean_square + 1e-06) * gain[c : c + 1, :]).astype(BF16))


def finish_body(chips, cores, far, half, *refs):
    gains, (q, within, carry, state, out) = refs[:chips], refs[chips:]

    def block(n):
        def put(here, value):
            out[n, :, here] = value

        finish_heads(chips, cores, far, half, gains, q, within, carry, state, n, put)

    each(0, chips // 2, block)


def last_body(chips, cores, *refs):
    gains = refs[:chips]
    q, within, carry, state, *done = refs[chips : chips + 7]
    out, buffer, sem, done_sem = refs[chips + 7 :]
    core = lax.axis_index("sub")
    mid = chips // 2
    width = buffer.shape[2]

    def copy(source, i, place, sem):
        target = out.at[:, cols(i * cores + place, 0, (1, width))]
        return pltpu.make_async_copy(source, target, sem)

    copies = []
    for k, (half, place) in enumerate(((0, core), (1, core), (0, 1 - core))):
        for n in range(mid):
            copies.append(copy(done[k].at[n], n + half * mid, place, done_sem.at[k, n]))
            copies[-1].start()
    for n in range(mid):

        def put(here, value):
            buffer[n, :, here] = value

        finish_heads(chips, cores, True, 1, gains, q, within, carry, state, n, put)
        copies.append(copy(buffer.at[n], n + mid, 1 - core, sem.at[n]))
        copies[-1].start()
    for one in copies:
        one.wait()


def block_copies(chips, cores, core, pairs, sems):
    width = pairs[0][1].shape[2]
    return [
        pltpu.make_async_copy(
            source.at[:, cols(i * cores + core, 0, (1, width))], target.at[i], sems.at[n, i]
        )
        for n, (source, target) in enumerate(pairs)
        for i in range(chips)
    ]


def slice_body(chips, cores, k_all, v_all, k, v, sems):
    copies = block_copies(
        chips, cores, 1 - lax.axis_index("sub"), ((k_all, k), (v_all, v)), sems
    )
    for copy in copies:
        copy.start()
    for copy in copies:
        copy.wait()


def prepare_body(chips, cores, lengths_all, k_all, v_all, k, v, docs, *scratch):
    lengths, sems, length_sem = scratch
    copies = block_copies(chips, cores, lax.axis_index("sub"), ((k_all, k), (v_all, v)), sems)
    lengths_copy = pltpu.make_async_copy(lengths_all, lengths, length_sem)
    lengths_copy.start()
    for copy in copies:
        copy.start()
    lengths_copy.wait()
    pieces, rows = docs.shape[1:]
    piece = lax.broadcasted_iota(jnp.int32, (pieces, rows), 0)
    lane = lax.broadcasted_iota(jnp.int32, (pieces, rows), 1)
    first = (lax.axis_index("seq") * pieces + piece) * rows
    here, before = jnp.zeros((pieces, rows), F32), jnp.zeros((pieces, rows), F32)
    start = 0
    for n in range(lengths.shape[0]):
        here += jnp.where(start <= first + lane, 1.0, 0.0)
        before += jnp.where(start < first, 1.0, 0.0)
        start = start + lengths[n]
    end = jnp.broadcast_to(here[:, rows - 1 :], (pieces, rows))
    docs[0] = here
    docs[1] = jnp.where(here == end, 1.0, 0.0)
    docs[2] = jnp.where(here == before, 1.0, 0.0)
    for copy in copies:
        copy.wait()


def earlier_rows(value, row_factor, blocks, reach):
    total, step = value, 1
    factor = row_factor[blocks] if reach > 1 else None
    while step < reach:
        before = shift(total, "seq", step).astype(F32)
        total = (total.astype(F32) + factor[:, :, None, :] * before).astype(BF16)
        factor = factor * shift(factor, "seq", step)
        step *= 2
    return shift(total, "seq", 1)


def per_device(query, key, value, log_decay, gain, doc_lengths):
    rows, width = query.shape
    per_block, _ = log_decay.shape
    head_width = gain.shape[1]
    chips, cores, depth = lax.axis_size("head"), lax.axis_size("sub"), lax.axis_size("seq")
    assert cores == 2 and chips % 2 == 0 and rows == head_width
    pieces = chips * cores
    others = chips - 1
    mid = chips // 2
    reach = max(1, -(-depth // 4))

    def sds(shape, kind):
        return jax.ShapeDtypeStruct(shape, kind)

    square = (per_block, head_width, head_width)
    area = per_block * head_width * head_width
    block = (chips, rows, per_block * head_width)
    half = sds((mid,) + square, BF16)
    half_wide = sds((mid,) + square, F32)
    log_shape = (pieces, chips, per_block, rows)
    coef_shape = (3 * chips + 5, chips, per_block, rows)

    key_send, value_send = call(
        functools.partial(slice_body, chips, cores),
        [sds(block, BF16)] * 2,
        [HBM] * 2,
        [VMEM] * 2,
        [pltpu.SemaphoreType.DMA((2, chips))],
        moved=8 * rows * width,
        vmem=67043328 - SLICE_ROOM * rows * width,
    )(key, value)
    key_far = rotate(key_send, "sub", 1)
    value_far = rotate(value_send, "sub", 1)
    decays = [log_decay] + [rotate(log_decay, "head", k) for k in range(1, chips)]
    gains = [gain] + [rotate(gain, "head", k) for k in range(1, chips)]
    key, value, docs = call(
        functools.partial(prepare_body, chips, cores),
        [sds(block, BF16)] * 2 + [sds((3, pieces, rows), F32)],
        [HBM] * 3,
        [VMEM] * 3,
        [
            pltpu.SMEM(doc_lengths.shape, jnp.int32),
            pltpu.SemaphoreType.DMA((2, chips)),
            pltpu.SemaphoreType.DMA(()),
        ],
        moved=12 * rows * width,
        vmem=67043328 - PREPARE_ROOM * rows * width,
    )(doc_lengths, key, value)

    kv = (key, value, key_far, value_far)
    state_x, first_a, logs, coef, weight = call(
        functools.partial(states_a_body, chips, cores),
        [half, half_wide]
        + [sds(log_shape, F32), sds(coef_shape, F32), sds(log_shape, F32)],
        [VMEM] * (chips + 5),
        [VMEM] * 5,
        flops=2 * rows * chips * area,
        moved=8 * chips * area,
    )(*decays, docs, *kv)
    from_x = [rotate(state_x, "head", k) for k in range(1, chips)]
    state_b, state_z, first_b = call(
        functools.partial(states_b_body, chips),
        [half, half, half_wide],
        [VMEM] * 6,
        [VMEM] * 3,
        flops=2 * rows * chips * area,
        moved=8 * chips * area,
    )(weight, coef, *kv)
    row_factor = coef[places(chips)["row"]] if reach > 1 else None
    past_b = earlier_rows(state_z, row_factor, slice(mid, chips), reach)
    logs_far = rotate(logs, "sub", 1)

    def within(far, blocks, *args):
        return call(
            functools.partial(within_body, cores, far, blocks),
            [sds((mid,) + block[1:], F32)] * 2,
            [VMEM] * 5,
            [VMEM] * 2,
            flops=rows * rows * width,
            moved=4 * rows * width,
        )(*args)

    low, high = (0, mid), (mid, chips)
    own = (logs, docs, query, key, value)
    own_a = within(False, low, *own)

    total = call(
        functools.partial(row_total_body, chips),
        half,
        [VMEM] * (2 + others),
        VMEM,
        moved=6 * mid * area,
    )(coef, state_x, *from_x)
    past_a = earlier_rows(total, row_factor, slice(0, mid), reach)

    messages = call(
        functools.partial(messages_body, chips),
        [half] * others,
        [VMEM] * 3,
        [VMEM] * others,
        moved=6 * mid * area,
    )(coef, state_b, past_b)
    from_b = [rotate(messages[k - 1], "head", k) for k in range(1, chips)]

    own_b = within(False, high, *own)
    far = (logs_far, docs, query, key_send, value_send)
    far_low = within(True, low, *far)
    gains_far = [rotate(part, "sub", 1) for part in gains]
    far_high = within(True, high, *far)

    def entering(which, first, past, arrived):
        return call(
            functools.partial(entering_body, chips, which),
            [half] * 2,
            [VMEM] * (3 + others),
            [VMEM] * 2,
            moved=8 * mid * area,
        )(coef, first, past, *arrived)

    def finish(far, which, gain_parts, local, state):
        return call(
            functools.partial(finish_body, chips, cores, far, which),
            sds((mid,) + block[1:], BF16),
            [VMEM] * (chips + 4),
            VMEM,
            flops=rows * head_width * width // 2,
            moved=3 * rows * width,
        )(*gain_parts, query, *local, state)

    keep_a, send_a = entering(0, first_a, past_a, from_x)
    far_a = rotate(send_a, "sub", 1)
    out_a = finish(False, 0, gains, own_a, keep_a)
    keep_b, send_b = entering(1, first_b, past_b, from_b)
    far_b = rotate(send_b, "sub", 1)
    out_b = finish(False, 1, gains, own_b, keep_b)
    out_far = finish(True, 0, gains_far, far_low, far_a)
    return call(
        functools.partial(last_body, chips, cores),
        sds((rows, width), BF16),
        [VMEM] * (chips + 7),
        ANY,
        [
            pltpu.VMEM((mid,) + block[1:], BF16),
            pltpu.SemaphoreType.DMA((mid,)),
            pltpu.SemaphoreType.DMA((3, mid)),
        ],
        flops=rows * head_width * width,
        moved=7 * rows * width,
    )(*gains_far, query, *far_high, far_b, out_a, out_b, out_far)


SLICE_ROOM = 22
PREPARE_ROOM = 24


def solution(mesh):
    rows = P(("groups", "seq", "head", "sub"), None)

    return jax.shard_map(
        per_device,
        mesh=mesh,
        in_specs=(
            rows,
            rows,
            rows,
            P(("head", "sub"), ("groups", "seq")),
            P(("head", "sub"), None),
            P("groups"),
        ),
        out_specs=rows,
        check_vma=False,
    )
```

```python
import functools

import jax
import jax.numpy as jnp
from jax import lax
from jax.experimental import pallas as pl
from jax.experimental.pallas import tpu as pltpu
from jax.sharding import PartitionSpec as P

BF16 = jnp.bfloat16
F32 = jnp.float32
ANY = pl.BlockSpec(memory_space=pl.ANY)
HBM = pl.BlockSpec(memory_space=pltpu.HBM)
VMEM = pl.BlockSpec(memory_space=pltpu.VMEM)
SMEM = pl.BlockSpec(memory_space=pltpu.SMEM)


def rotate(x, axis, step):
    size = lax.axis_size(axis)
    return lax.ppermute(x, axis, [(i, (i + step) % size) for i in range(size)])


def shift(x, axis, step):
    size = lax.axis_size(axis)
    return lax.ppermute(x, axis, [(i, i + step) for i in range(size - step)])


def column(row, rows):
    return jnp.broadcast_to(row, (rows, row.shape[1])).T


def call(body, out_shape, in_specs, out_specs, scratch=(), flops=0, moved=0, aliases=None, vmem=8 << 20):
    return pl.pallas_call(
        body,
        out_shape=out_shape,
        in_specs=in_specs,
        out_specs=out_specs,
        scratch_shapes=list(scratch),
        input_output_aliases=aliases or {},
        cost_estimate=pl.CostEstimate(flops=flops, bytes_accessed=moved, transcendentals=0),
        compiler_params=pltpu.CompilerParams(vmem_limit_bytes=vmem),
    )


def each(low, high, body):
    if high - low == 1:
        body(low)
    elif high > low:
        lax.fori_loop(low, high, lambda i, _: (body(i), 0)[1], 0)


def cols(place, c, width):
    start = (place * width[0] + c) * width[1]
    return pl.ds(start if isinstance(start, int) else pl.multiple_of(start, width[1]), width[1])


def places(chips):
    base = 3 * chips
    return dict(to_start=base, to_end=base + 1, first=base + 2, row=base + 3)


def running(decays, slot, piece, rows):
    here = slice(piece * rows, (piece + 1) * rows)
    if not isinstance(piece, int):
        here = pl.ds(pl.multiple_of(piece * rows, rows), rows)
    total = decays[0][:, here]
    for k in range(1, len(decays)):
        total = jnp.where(slot == k, decays[k][:, here], total)
    lane = lax.broadcasted_iota(jnp.int32, total.shape, 1)
    reach = 1
    while reach < rows:
        total = total + jnp.where(lane >= reach, pltpu.roll(total, reach, 1), 0.0)
        reach *= 2
    return total


def passes(total, docs, piece):
    rows = total.shape[1]
    passed = docs[2, pl.ds(piece, 1), :][:, rows - 1 :]
    return jnp.exp(jnp.broadcast_to(total[:, rows - 1 :], total.shape)) * passed


def pick(index, options):
    result = options[-1]
    for c in range(len(options) - 2, -1, -1):
        result = jnp.where(index == c, options[c], result)
    return result


def states_of(chips, decays, docs, kv, i, keep):
    cores = 2
    core, chip = lax.axis_index("sub"), lax.axis_index("head")
    k_own, v_own, k_far, v_far = kv
    rows = docs.shape[2]
    slot = lax.rem(chip - i + chips, chips)
    totals, weights = [], []
    for place in (core, 1 - core):
        piece = chip * cores + place
        total = running(decays, slot, piece, rows)
        end = jnp.broadcast_to(total[:, rows - 1 :], total.shape)
        totals.append(total)
        weights.append(jnp.exp(end - total) * docs[1, pl.ds(piece, 1), :])
    second = passes(jnp.where(core == 0, totals[1], totals[0]), docs, chip * cores + 1)
    for c in range(second.shape[0]):
        here = slice(c * rows, (c + 1) * rows)
        sums = []
        for k_ref, v_ref, weight in ((k_own, v_own, weights[0]), (k_far, v_far, weights[1])):
            keys = k_ref[i, :, here].T.astype(F32) * weight[c : c + 1, :]
            sums.append(jnp.dot(keys.astype(BF16), v_ref[i, :, here], preferred_element_type=F32))
        first = jnp.where(core == 0, sums[0], sums[1])
        last = jnp.where(core == 0, sums[1], sums[0])
        keep(c, first, last + second[c : c + 1, :] * first)


def states_a_body(chips, *refs):
    decays, (docs, *kv), (state_x, state_0) = refs[:chips], refs[chips:-2], refs[-2:]
    for i in range(chips // 2):

        def keep(c, first, state):
            state_0[i, c] = first
            state_x[i, c] = state.astype(BF16)

        states_of(chips, decays, docs, kv, i, keep)


def states_b_body(chips, *refs):
    decays, (docs, *kv), (state_b, state_z, state_0) = refs[:chips], refs[chips:-3], refs[-3:]
    cores = 2
    mid = chips // 2
    rows = docs.shape[2]
    chip = lax.axis_index("head")
    for i in range(mid, chips):
        slot = lax.rem(chip - i + chips, chips)
        after = None
        for piece in range(cores, chips * cores):
            factor = passes(running(decays, slot, piece, rows), docs, piece)
            factor = jnp.where(piece >= (chip + 1) * cores, factor, 1.0)
            after = factor if after is None else after * factor

        def keep(c, first, state):
            state_0[i - mid, c] = first
            state_b[i - mid, c] = state.astype(BF16)
            state_z[i - mid, c] = (after[c : c + 1, :] * state).astype(BF16)

        states_of(chips, decays, docs, kv, i, keep)


def tables_body(chips, cores, *refs):
    decays, docs, logs, coef = refs[:chips], refs[chips], refs[chips + 1], refs[chips + 2]
    chip = lax.axis_index("head")
    pieces = chips * cores
    rows = docs.shape[2]
    at = places(chips)
    for block in range(chips):
        slot = lax.rem(chip - block + chips, chips)
        gain = decays[0][:, pieces * rows :]
        for k in range(1, chips):
            gain = jnp.where(slot == k, decays[k][:, pieces * rows :], gain)
        logs[pieces, block] = gain
        factors = []
        for piece in range(pieces):
            total = running(decays, slot, piece, rows)
            logs[piece, block] = total
            factors.append(passes(total, docs, piece))
        through = []
        for c in range(chips):
            product = factors[c * cores]
            for u in range(1, cores):
                product = product * factors[c * cores + u]
            through.append(product)
        one, zero = jnp.ones_like(through[0]), jnp.zeros_like(through[0])

        def between(low, high):
            product = one
            for c in range(low, high):
                product = product * through[c]
            return product

        to_start = pick(chip, [between(0, c) for c in range(chips)])
        coef[at["to_start"], block] = to_start
        coef[at["to_end"], block] = pick(chip, [between(0, c + 1) for c in range(chips)])
        coef[at["first"], block] = pick(chip, [factors[c * cores] for c in range(chips)])
        coef[at["row"], block] = between(0, chips)
        for back in range(chips):
            source = lax.rem(chip - back + chips, chips)
            coef[back, block] = pick(source, [between(c + 1, chips) for c in range(chips)])
            earlier = pick(
                chip,
                [between(c - back + 1, c) if 0 <= c - back < c else zero for c in range(chips)],
            )
            coef[chips + back, block] = earlier
            coef[2 * chips + back, block] = jnp.where(
                (source < chip) & (back > 0), earlier, to_start
            )


def within_body(cores, far, blocks, logs, docs, q, k, v, out, carry):
    core = lax.axis_index("sub")
    piece = lax.axis_index("head") * cores + core
    core = 1 - core if far else core
    per_block, rows = logs.shape[2], logs.shape[3]
    docs_here = jnp.broadcast_to(docs[0, pl.ds(piece, 1), :], (rows, rows))
    t = lax.broadcasted_iota(jnp.int32, (rows, rows), 0)
    s = lax.broadcasted_iota(jnp.int32, (rows, rows), 1)
    linked = (docs_here.T == docs_here) & (t >= s)
    carries = column(docs[2, pl.ds(piece, 1), :], rows)

    def heads_of(i):
        for c in range(per_block):
            here = slice(c * rows, (c + 1) * rows)
            row = logs[piece, i, c : c + 1, :]
            down = column(row, rows)
            damping = jnp.exp(jnp.where(linked, down - row, -1e30))
            scores = lax.dot_general(
                q[:, cols(i * cores + core, c, (per_block, rows))],
                k[i, :, here],
                (((1,), (1,)), ((), ())),
                preferred_element_type=F32,
            )
            out[i - blocks[0], :, here] = jnp.dot(
                (scores * damping).astype(BF16), v[i, :, here], preferred_element_type=F32
            )
            carry[i - blocks[0], :, here] = jnp.exp(down) * carries

    each(*blocks, heads_of)


def row_total_body(chips, coef, state_x, *refs):
    from_x, total = refs[:-1], refs[-1]

    def join(i):
        for c in range(state_x.shape[1]):
            sum_ = coef[0, i, c : c + 1, :] * state_x[i, c].astype(F32)
            for back in range(1, chips):
                sum_ = sum_ + coef[back, i, c : c + 1, :] * from_x[back - 1][i, c].astype(F32)
            total[i, c] = sum_.astype(BF16)

    each(0, chips // 2, join)


def messages_body(chips, coef, state_b, past_b, *messages):
    chip = lax.axis_index("head")
    mid = chips // 2

    def join(i):
        for c in range(state_b.shape[1]):
            past = past_b[i, c]
            factor = coef[places(chips)["to_end"], i + mid, c : c + 1, :]
            ahead = (state_b[i, c].astype(F32) + factor * past.astype(F32)).astype(BF16)
            for back in range(1, chips):
                messages[back - 1][i, c] = jnp.where(chip + back < chips, ahead, past)

    each(0, mid, join)


def entering_body(chips, half, coef, first, past, *refs):
    others = refs[:-2]
    keep, send = refs[-2:]
    is_first = lax.axis_index("sub") == 0
    at = places(chips)
    mid = chips // 2
    base = (1 + half) * chips

    def join(i):
        for c in range(past.shape[1]):

            def factor(place):
                return coef[place, i + half * mid, c : c + 1, :]

            entering = factor(at["to_start"]) * past[i, c].astype(F32)
            for back in range(1, chips):
                entering = entering + factor(base + back) * others[back - 1][i, c].astype(F32)
            later = first[i, c] + factor(at["first"]) * entering
            keep[i, c] = jnp.where(is_first, entering, later).astype(BF16)
            send[i, c] = jnp.where(is_first, later, entering).astype(BF16)

    each(0, mid, join)


def finish_heads(chips, cores, far, half, logs, q, within, carry, state, n, put):
    core = lax.axis_index("sub")
    core = 1 - core if far else core
    i = n + half * (chips // 2)
    per_block, rows = logs.shape[2:]
    gain = logs[chips * cores, i]
    for c in range(per_block):
        here = slice(c * rows, (c + 1) * rows)
        result = within[n, :, here] + carry[n, :, here] * jnp.dot(
            q[:, cols(i * cores + core, c, (per_block, rows))],
            state[n, c],
            preferred_element_type=F32,
        )
        mean_square = jnp.mean(result * result, axis=1, keepdims=True)
        put(here, (result * lax.rsqrt(mean_square + 1e-06) * gain[c : c + 1, :]).astype(BF16))


def finish_body(chips, cores, far, half, logs, q, within, carry, state, out):

    def block(n):
        def put(here, value):
            out[n, :, here] = value

        finish_heads(chips, cores, far, half, logs, q, within, carry, state, n, put)

    each(0, chips // 2, block)


def last_body(chips, cores, logs, *refs):
    q, within, carry, state, *done = refs[:7]
    out, buffer, sem, done_sem = refs[7:]
    core = lax.axis_index("sub")
    mid = chips // 2
    width = buffer.shape[2]

    def copy(source, i, place, sem):
        target = out.at[:, cols(i * cores + place, 0, (1, width))]
        return pltpu.make_async_copy(source, target, sem)

    copies = []
    for k, (half, place) in enumerate(((0, core), (1, core), (0, 1 - core))):
        for n in range(mid):
            copies.append(copy(done[k].at[n], n + half * mid, place, done_sem.at[k, n]))
            copies[-1].start()
    for n in range(mid):

        def put(here, value):
            buffer[n, :, here] = value

        finish_heads(chips, cores, True, 1, logs, q, within, carry, state, n, put)
        copies.append(copy(buffer.at[n], n + mid, 1 - core, sem.at[n]))
        copies[-1].start()
    for one in copies:
        one.wait()


def block_copies(chips, cores, core, pairs, sems):
    width = pairs[0][1].shape[2]
    return [
        pltpu.make_async_copy(
            source.at[:, cols(i * cores + core, 0, (1, width))], target.at[i], sems.at[n, i]
        )
        for n, (source, target) in enumerate(pairs)
        for i in range(chips)
    ]


def slice_body(chips, cores, k_all, v_all, k, v, sems):
    copies = block_copies(
        chips, cores, 1 - lax.axis_index("sub"), ((k_all, k), (v_all, v)), sems
    )
    for copy in copies:
        copy.start()
    for copy in copies:
        copy.wait()


def pack_body(log_decay, gain, packed):
    packed[:, : log_decay.shape[1]] = log_decay[...]
    packed[:, log_decay.shape[1] :] = gain[...]


def prepare_body(chips, cores, lengths_all, k_all, v_all, k, v, docs, *scratch):
    lengths, sems, length_sem = scratch
    copies = block_copies(chips, cores, lax.axis_index("sub"), ((k_all, k), (v_all, v)), sems)
    lengths_copy = pltpu.make_async_copy(lengths_all, lengths, length_sem)
    lengths_copy.start()
    for copy in copies:
        copy.start()
    lengths_copy.wait()
    pieces, rows = docs.shape[1:]
    piece = lax.broadcasted_iota(jnp.int32, (pieces, rows), 0)
    lane = lax.broadcasted_iota(jnp.int32, (pieces, rows), 1)
    first = (lax.axis_index("seq") * pieces + piece) * rows
    here, before = jnp.zeros((pieces, rows), F32), jnp.zeros((pieces, rows), F32)
    start = 0
    for n in range(lengths.shape[0]):
        here += jnp.where(start <= first + lane, 1.0, 0.0)
        before += jnp.where(start < first, 1.0, 0.0)
        start = start + lengths[n]
    end = jnp.broadcast_to(here[:, rows - 1 :], (pieces, rows))
    docs[0] = here
    docs[1] = jnp.where(here == end, 1.0, 0.0)
    docs[2] = jnp.where(here == before, 1.0, 0.0)
    for copy in copies:
        copy.wait()


def earlier_rows(value, row_factor, blocks, reach):
    total, step = value, 1
    factor = row_factor[blocks] if reach > 1 else None
    while step < reach:
        before = shift(total, "seq", step).astype(F32)
        total = (total.astype(F32) + factor[:, :, None, :] * before).astype(BF16)
        factor = factor * shift(factor, "seq", step)
        step *= 2
    return shift(total, "seq", 1)


def per_device(query, key, value, log_decay, gain, doc_lengths):
    rows, width = query.shape
    per_block, row_tokens = log_decay.shape
    head_width = gain.shape[1]
    chips, cores, depth = lax.axis_size("head"), lax.axis_size("sub"), lax.axis_size("seq")
    assert cores == 2 and chips % 2 == 0 and rows == head_width
    pieces = chips * cores
    others = chips - 1
    mid = chips // 2
    reach = max(1, -(-depth // 4))

    def sds(shape, kind):
        return jax.ShapeDtypeStruct(shape, kind)

    square = (per_block, head_width, head_width)
    area = per_block * head_width * head_width
    block = (chips, rows, per_block * head_width)
    half = sds((mid,) + square, BF16)
    half_wide = sds((mid,) + square, F32)
    log_shape = (pieces + 1, chips, per_block, rows)
    coef_shape = (3 * chips + 4, chips, per_block, rows)

    key_send, value_send = call(
        functools.partial(slice_body, chips, cores),
        [sds(block, BF16)] * 2,
        [HBM] * 2,
        [VMEM] * 2,
        [pltpu.SemaphoreType.DMA((2, chips))],
        moved=8 * rows * width,
        vmem=67043328 - SLICE_ROOM * rows * width,
    )(key, value)
    key_far = rotate(key_send, "sub", 1)
    value_far = rotate(value_send, "sub", 1)
    packed = call(
        pack_body,
        sds((per_block, row_tokens + head_width), F32),
        [VMEM] * 2,
        VMEM,
    )(log_decay, gain)
    decays = [packed] + [rotate(packed, "head", k) for k in range(1, chips)]
    key, value, docs = call(
        functools.partial(prepare_body, chips, cores),
        [sds(block, BF16)] * 2 + [sds((3, pieces, rows), F32)],
        [HBM] * 3,
        [VMEM] * 3,
        [
            pltpu.SMEM(doc_lengths.shape, jnp.int32),
            pltpu.SemaphoreType.DMA((2, chips)),
            pltpu.SemaphoreType.DMA(()),
        ],
        moved=12 * rows * width,
        vmem=67043328 - PREPARE_ROOM * rows * width,
    )(doc_lengths, key, value)

    kv = (key, value, key_far, value_far)
    state_x, first_a = call(
        functools.partial(states_a_body, chips),
        [half, half_wide],
        [VMEM] * (chips + 5),
        [VMEM] * 2,
        flops=2 * rows * chips * area,
        moved=8 * chips * area,
    )(*decays, docs, *kv)
    from_x = [rotate(state_x, "head", k) for k in range(1, chips)]
    state_b, state_z, first_b = call(
        functools.partial(states_b_body, chips),
        [half, half, half_wide],
        [VMEM] * (chips + 5),
        [VMEM] * 3,
        flops=2 * rows * chips * area,
        moved=8 * chips * area,
    )(*decays, docs, *kv)
    logs, coef = call(
        functools.partial(tables_body, chips, cores),
        [sds(log_shape, F32), sds(coef_shape, F32)],
        [VMEM] * (chips + 1),
        [VMEM] * 2,
        moved=8 * area,
    )(*decays, docs)
    row_factor = coef[places(chips)["row"]] if reach > 1 else None
    past_b = earlier_rows(state_z, row_factor, slice(mid, chips), reach)
    logs_far = rotate(logs, "sub", 1)

    def within(far, blocks, *args):
        return call(
            functools.partial(within_body, cores, far, blocks),
            [sds((mid,) + block[1:], F32)] * 2,
            [VMEM] * 5,
            [VMEM] * 2,
            flops=rows * rows * width,
            moved=4 * rows * width,
        )(*args)

    low, high = (0, mid), (mid, chips)
    own = (logs, docs, query, key, value)
    own_a = within(False, low, *own)

    total = call(
        functools.partial(row_total_body, chips),
        half,
        [VMEM] * (2 + others),
        VMEM,
        moved=6 * mid * area,
    )(coef, state_x, *from_x)
    past_a = earlier_rows(total, row_factor, slice(0, mid), reach)

    messages = call(
        functools.partial(messages_body, chips),
        [half] * others,
        [VMEM] * 3,
        [VMEM] * others,
        moved=6 * mid * area,
    )(coef, state_b, past_b)
    from_b = [rotate(messages[k - 1], "head", k) for k in range(1, chips)]

    own_b = within(False, high, *own)
    far = (logs_far, docs, query, key_send, value_send)
    far_low = within(True, low, *far)
    far_high = within(True, high, *far)

    def entering(which, first, past, arrived):
        return call(
            functools.partial(entering_body, chips, which),
            [half] * 2,
            [VMEM] * (3 + others),
            [VMEM] * 2,
            moved=8 * mid * area,
        )(coef, first, past, *arrived)

    def finish(far, which, logs_used, local, state):
        return call(
            functools.partial(finish_body, chips, cores, far, which),
            sds((mid,) + block[1:], BF16),
            [VMEM] * 5,
            VMEM,
            flops=rows * head_width * width // 2,
            moved=3 * rows * width,
        )(logs_used, query, *local, state)

    keep_a, send_a = entering(0, first_a, past_a, from_x)
    far_a = rotate(send_a, "sub", 1)
    out_a = finish(False, 0, logs, own_a, keep_a)
    keep_b, send_b = entering(1, first_b, past_b, from_b)
    far_b = rotate(send_b, "sub", 1)
    out_b = finish(False, 1, logs, own_b, keep_b)
    out_far = finish(True, 0, logs_far, far_low, far_a)
    return call(
        functools.partial(last_body, chips, cores),
        sds((rows, width), BF16),
        [VMEM] * 8,
        ANY,
        [
            pltpu.VMEM((mid,) + block[1:], BF16),
            pltpu.SemaphoreType.DMA((mid,)),
            pltpu.SemaphoreType.DMA((3, mid)),
        ],
        flops=rows * head_width * width,
        moved=7 * rows * width,
    )(logs_far, query, *far_high, far_b, out_a, out_b, out_far)


SLICE_ROOM = 22
PREPARE_ROOM = 24


def solution(mesh):
    rows = P(("groups", "seq", "head", "sub"), None)

    return jax.shard_map(
        per_device,
        mesh=mesh,
        in_specs=(
            rows,
            rows,
            rows,
            P(("head", "sub"), ("groups", "seq")),
            P(("head", "sub"), None),
            P("groups"),
        ),
        out_specs=rows,
        check_vma=False,
    )
```

```python
import functools

import jax
import jax.numpy as jnp
from jax import lax
from jax.experimental import pallas as pl
from jax.experimental.pallas import tpu as pltpu
from jax.sharding import PartitionSpec as P

BF16 = jnp.bfloat16
F32 = jnp.float32
ANY = pl.BlockSpec(memory_space=pl.ANY)
HBM = pl.BlockSpec(memory_space=pltpu.HBM)
VMEM = pl.BlockSpec(memory_space=pltpu.VMEM)
SMEM = pl.BlockSpec(memory_space=pltpu.SMEM)


def rotate(x, axis, step):
    size = lax.axis_size(axis)
    return lax.ppermute(x, axis, [(i, (i + step) % size) for i in range(size)])


def shift(x, axis, step):
    size = lax.axis_size(axis)
    return lax.ppermute(x, axis, [(i, i + step) for i in range(size - step)])


def column(row, rows):
    return jnp.broadcast_to(row, (rows, row.shape[1])).T


def call(body, out_shape, in_specs, out_specs, scratch=(), flops=0, moved=0, aliases=None, vmem=8 << 20):
    return pl.pallas_call(
        body,
        out_shape=out_shape,
        in_specs=in_specs,
        out_specs=out_specs,
        scratch_shapes=list(scratch),
        input_output_aliases=aliases or {},
        cost_estimate=pl.CostEstimate(flops=flops, bytes_accessed=moved, transcendentals=0),
        compiler_params=pltpu.CompilerParams(vmem_limit_bytes=vmem),
    )


def each(low, high, body):
    if high - low == 1:
        body(low)
    elif high > low:
        lax.fori_loop(low, high, lambda i, _: (body(i), 0)[1], 0)


def cols(place, c, width):
    start = (place * width[0] + c) * width[1]
    return pl.ds(start if isinstance(start, int) else pl.multiple_of(start, width[1]), width[1])


def places(chips):
    base = 3 * chips
    return dict(to_start=base, to_end=base + 1, first=base + 2, row=base + 3, second=base + 4)


def pick(index, options):
    result = options[-1]
    for c in range(len(options) - 2, -1, -1):
        result = jnp.where(index == c, options[c], result)
    return result


def states_of(chips, weight, coef, own, far, n, i, keep):
    cores = 2
    core, chip = lax.axis_index("sub"), lax.axis_index("head")
    per_block, rows = weight.shape[2:]
    for c in range(per_block):
        here = slice(c * rows, (c + 1) * rows)
        sums = []
        for ref, block, place in ((own, i, core), (far, n, 1 - core)):
            keys = ref[0, block, :, here].T.astype(F32)
            keys = keys * weight[chip * cores + place, i, c : c + 1, :]
            values = ref[1, block, :, here]
            sums.append(jnp.dot(keys.astype(BF16), values, preferred_element_type=F32))
        first = jnp.where(core == 0, sums[0], sums[1])
        last = jnp.where(core == 0, sums[1], sums[0])
        keep(c, first, last + coef[places(chips)["second"], i, c : c + 1, :] * first)


def tables(chips, cores, decays, docs, logs, coef, weight, stack):
    chip = lax.axis_index("head")
    pieces = chips * cores
    per_block, rows = logs.shape[2:]
    at = places(chips)
    for slot in range(chips):
        for piece in range(pieces):
            place = (slot * pieces + piece) * per_block
            stack[0, place : place + per_block] = decays[slot][:, piece * rows : (piece + 1) * rows]
    earlier = lax.broadcasted_iota(jnp.int32, (rows, rows), 0)
    later = lax.broadcasted_iota(jnp.int32, (rows, rows), 1)
    stack[1] = jnp.dot(
        stack[0],
        jnp.where(earlier <= later, 1.0, 0.0),
        precision=lax.Precision.HIGHEST,
        preferred_element_type=F32,
    )
    for slot in range(chips):
        block = lax.rem(chip - slot + chips, chips)
        logs[pieces, block] = decays[slot][:, pieces * rows :]
        factors = []
        for piece in range(pieces):
            place = (slot * pieces + piece) * per_block
            total = stack[1, place : place + per_block]
            logs[piece, block] = total
            end = jnp.broadcast_to(total[:, rows - 1 :], (per_block, rows))
            weight[piece, block] = jnp.exp(end - total) * docs[1, piece : piece + 1, :]
            passed = jnp.broadcast_to(docs[2, piece : piece + 1, rows - 1 :], (per_block, rows))
            factors.append(jnp.exp(end) * passed)
        through = []
        for c in range(chips):
            product = factors[c * cores]
            for u in range(1, cores):
                product = product * factors[c * cores + u]
            through.append(product)
        one, zero = jnp.ones_like(through[0]), jnp.zeros_like(through[0])

        def between(low, high):
            product = one
            for c in range(low, high):
                product = product * through[c]
            return product

        to_start = pick(chip, [between(0, c) for c in range(chips)])
        coef[at["to_start"], block] = to_start
        coef[at["to_end"], block] = pick(chip, [between(0, c + 1) for c in range(chips)])
        coef[at["first"], block] = pick(chip, [factors[c * cores] for c in range(chips)])
        coef[at["second"], block] = pick(chip, [factors[c * cores + 1] for c in range(chips)])
        coef[at["row"], block] = between(0, chips)
        for back in range(chips):
            source = lax.rem(chip - back + chips, chips)
            coef[back, block] = pick(source, [between(c + 1, chips) for c in range(chips)])
            before = pick(
                chip,
                [between(c - back + 1, c) if 0 <= c - back < c else zero for c in range(chips)],
            )
            coef[chips + back, block] = before
            coef[2 * chips + back, block] = jnp.where(
                (source < chip) & (back > 0), before, to_start
            )


def states_a_body(chips, cores, *refs):
    decays, (docs, own, far) = refs[:chips], refs[chips : chips + 3]
    state_x, state_0, logs, coef, weight, stack = refs[chips + 3 :]
    tables(chips, cores, decays, docs, logs, coef, weight, stack)
    for i in range(chips // 2):

        def keep(c, first, state):
            state_0[i, c] = first
            state_x[i, c] = state.astype(BF16)

        states_of(chips, weight, coef, own, far, i, i, keep)


def states_b_body(chips, weight, coef, own, far, state_b, state_z, state_0):
    mid = chips // 2
    for n in range(mid):
        i = n + mid

        def keep(c, first, state):
            state_0[n, c] = first
            state_b[n, c] = state.astype(BF16)
            state_z[n, c] = (coef[0, i, c : c + 1, :] * state).astype(BF16)

        states_of(chips, weight, coef, own, far, n, i, keep)


def within_body(cores, far, blocks, logs, docs, q, kv, out, carry):
    core = lax.axis_index("sub")
    piece = lax.axis_index("head") * cores + core
    core = 1 - core if far else core
    per_block, rows = logs.shape[2], logs.shape[3]
    docs_here = jnp.broadcast_to(docs[0, pl.ds(piece, 1), :], (rows, rows))
    t = lax.broadcasted_iota(jnp.int32, (rows, rows), 0)
    s = lax.broadcasted_iota(jnp.int32, (rows, rows), 1)
    linked = (docs_here.T == docs_here) & (t >= s)
    carries = column(docs[2, pl.ds(piece, 1), :], rows)
    shift_ = blocks[0] if far else 0

    def heads_of(i):
        for c in range(per_block):
            here = slice(c * rows, (c + 1) * rows)
            row = logs[piece, i, c : c + 1, :]
            down = column(row, rows)
            damping = jnp.exp(jnp.where(linked, down - row, -1e30))
            scores = lax.dot_general(
                q[:, cols(i * cores + core, c, (per_block, rows))],
                kv[0, i - shift_, :, here],
                (((1,), (1,)), ((), ())),
                preferred_element_type=F32,
            )
            out[i - blocks[0], :, here] = jnp.dot(
                (scores * damping).astype(BF16), kv[1, i - shift_, :, here], preferred_element_type=F32
            )
            carry[i - blocks[0], :, here] = jnp.exp(down) * carries

    each(*blocks, heads_of)


def row_total_body(chips, coef, state_x, *refs):
    from_x, total = refs[:-1], refs[-1]

    def join(i):
        for c in range(state_x.shape[1]):
            sum_ = coef[0, i, c : c + 1, :] * state_x[i, c].astype(F32)
            for back in range(1, chips):
                sum_ = sum_ + coef[back, i, c : c + 1, :] * from_x[back - 1][i, c].astype(F32)
            total[i, c] = sum_.astype(BF16)

    each(0, chips // 2, join)


def messages_body(chips, coef, state_b, past_b, *messages):
    chip = lax.axis_index("head")
    mid = chips // 2

    def join(i):
        for c in range(state_b.shape[1]):
            past = past_b[i, c]
            factor = coef[places(chips)["to_end"], i + mid, c : c + 1, :]
            ahead = (state_b[i, c].astype(F32) + factor * past.astype(F32)).astype(BF16)
            for back in range(1, chips):
                messages[back - 1][i, c] = jnp.where(chip + back < chips, ahead, past)

    each(0, mid, join)


def entering_body(chips, half, coef, first, past, *refs):
    others = refs[:-2]
    keep, send = refs[-2:]
    is_first = lax.axis_index("sub") == 0
    at = places(chips)
    mid = chips // 2
    base = (1 + half) * chips

    def join(i):
        for c in range(past.shape[1]):

            def factor(place):
                return coef[place, i + half * mid, c : c + 1, :]

            entering = factor(at["to_start"]) * past[i, c].astype(F32)
            for back in range(1, chips):
                entering = entering + factor(base + back) * others[back - 1][i, c].astype(F32)
            later = first[i, c] + factor(at["first"]) * entering
            keep[i, c] = jnp.where(is_first, entering, later).astype(BF16)
            send[i, c] = jnp.where(is_first, later, entering).astype(BF16)

    each(0, mid, join)


def finish_heads(chips, cores, far, half, logs, q, within, carry, state, n, put):
    core = lax.axis_index("sub")
    core = 1 - core if far else core
    i = n + half * (chips // 2)
    per_block, rows = logs.shape[2:]
    gain = logs[chips * cores, i]
    for c in range(per_block):
        here = slice(c * rows, (c + 1) * rows)
        result = within[n, :, here] + carry[n, :, here] * jnp.dot(
            q[:, cols(i * cores + core, c, (per_block, rows))],
            state[n, c],
            preferred_element_type=F32,
        )
        mean_square = jnp.mean(result * result, axis=1, keepdims=True)
        put(here, (result * lax.rsqrt(mean_square + 1e-06) * gain[c : c + 1, :]).astype(BF16))


def finish_body(chips, cores, far, half, logs, q, within, carry, state, out):

    def block(n):
        def put(here, value):
            out[n, :, here] = value

        finish_heads(chips, cores, far, half, logs, q, within, carry, state, n, put)

    each(0, chips // 2, block)


def last_body(chips, cores, logs, *refs):
    q, within, carry, state, *done = refs[:7]
    out, buffer, sem, done_sem = refs[7:]
    core = lax.axis_index("sub")
    mid = chips // 2
    width = buffer.shape[2]

    def copy(source, i, place, sem):
        target = out.at[:, cols(i * cores + place, 0, (1, width))]
        return pltpu.make_async_copy(source, target, sem)

    copies = []
    for k, (half, place) in enumerate(((0, core), (1, core), (0, 1 - core))):
        for n in range(mid):
            copies.append(copy(done[k].at[n], n + half * mid, place, done_sem.at[k, n]))
            copies[-1].start()
    for n in range(mid):

        def put(here, value):
            buffer[n, :, here] = value

        finish_heads(chips, cores, True, 1, logs, q, within, carry, state, n, put)
        copies.append(copy(buffer.at[n], n + mid, 1 - core, sem.at[n]))
        copies[-1].start()
    for one in copies:
        one.wait()


def block_copies(cores, core, blocks, sources, target, sems):
    width = target.shape[3]
    return [
        pltpu.make_async_copy(
            source.at[:, cols(i * cores + core, 0, (1, width))],
            target.at[n, i - blocks[0]],
            sems.at[n, i - blocks[0]],
        )
        for n, source in enumerate(sources)
        for i in range(*blocks)
    ]


def slice_body(chips, cores, k_all, v_all, send, sems):
    core = 1 - lax.axis_index("sub")
    copies = block_copies(cores, core, (0, chips // 2), (k_all, v_all), send, sems)
    for copy in copies:
        copy.start()
    for copy in copies:
        copy.wait()


def pack_body(log_decay, gain, packed):
    packed[:, : log_decay.shape[1]] = log_decay[...]
    packed[:, log_decay.shape[1] :] = gain[...]


def prepare_body(chips, cores, lengths_all, k_all, v_all, send, own, docs, *scratch):
    lengths, send_sems, own_sems, length_sem = scratch
    core = lax.axis_index("sub")
    both = (k_all, v_all)
    copies = block_copies(cores, 1 - core, (chips // 2, chips), both, send, send_sems)
    copies += block_copies(cores, core, (0, chips), both, own, own_sems)
    lengths_copy = pltpu.make_async_copy(lengths_all, lengths, length_sem)
    lengths_copy.start()
    for copy in copies:
        copy.start()
    lengths_copy.wait()
    pieces, rows = docs.shape[1:]
    piece = lax.broadcasted_iota(jnp.int32, (pieces, rows), 0)
    lane = lax.broadcasted_iota(jnp.int32, (pieces, rows), 1)
    first = (lax.axis_index("seq") * pieces + piece) * rows
    here, before = jnp.zeros((pieces, rows), F32), jnp.zeros((pieces, rows), F32)
    start = 0
    for n in range(lengths.shape[0]):
        here += jnp.where(start <= first + lane, 1.0, 0.0)
        before += jnp.where(start < first, 1.0, 0.0)
        start = start + lengths[n]
    end = jnp.broadcast_to(here[:, rows - 1 :], (pieces, rows))
    docs[0] = here
    docs[1] = jnp.where(here == end, 1.0, 0.0)
    docs[2] = jnp.where(here == before, 1.0, 0.0)
    for copy in copies:
        copy.wait()


def earlier_rows(value, row_factor, blocks, reach):
    total, step = value, 1
    factor = row_factor[blocks] if reach > 1 else None
    while step < reach:
        before = shift(total, "seq", step).astype(F32)
        total = (total.astype(F32) + factor[:, :, None, :] * before).astype(BF16)
        factor = factor * shift(factor, "seq", step)
        step *= 2
    return shift(total, "seq", 1)


def per_device(query, key, value, log_decay, gain, doc_lengths):
    rows, width = query.shape
    per_block, row_tokens = log_decay.shape
    head_width = gain.shape[1]
    chips, cores, depth = lax.axis_size("head"), lax.axis_size("sub"), lax.axis_size("seq")
    assert cores == 2 and chips % 2 == 0 and rows == head_width
    pieces = chips * cores
    others = chips - 1
    mid = chips // 2
    reach = max(1, -(-depth // 4))

    def sds(shape, kind):
        return jax.ShapeDtypeStruct(shape, kind)

    square = (per_block, head_width, head_width)
    area = per_block * head_width * head_width
    block = (chips, rows, per_block * head_width)
    half = sds((mid,) + square, BF16)
    half_wide = sds((mid,) + square, F32)
    log_shape = (pieces + 1, chips, per_block, rows)
    coef_shape = (3 * chips + 5, chips, per_block, rows)

    half_kv = sds((2, mid) + block[1:], BF16)
    send_low = call(
        functools.partial(slice_body, chips, cores),
        half_kv,
        [HBM] * 2,
        VMEM,
        [pltpu.SemaphoreType.DMA((2, mid))],
        moved=4 * rows * width,
        vmem=67043328 - SLICE_ROOM * rows * width,
    )(key, value)
    far_low = rotate(send_low, "sub", 1)
    packed = call(
        pack_body,
        sds((per_block, row_tokens + head_width), F32),
        [VMEM] * 2,
        VMEM,
    )(log_decay, gain)
    decays = [packed] + [rotate(packed, "head", k) for k in range(1, chips)]
    send_high, own, docs = call(
        functools.partial(prepare_body, chips, cores),
        [half_kv, sds((2,) + block, BF16), sds((3, pieces, rows), F32)],
        [HBM] * 3,
        [VMEM] * 3,
        [
            pltpu.SMEM(doc_lengths.shape, jnp.int32),
            pltpu.SemaphoreType.DMA((2, mid)),
            pltpu.SemaphoreType.DMA((2, chips)),
            pltpu.SemaphoreType.DMA(()),
        ],
        moved=12 * rows * width,
        vmem=67043328 - PREPARE_ROOM * rows * width,
    )(doc_lengths, key, value)
    far_high = rotate(send_high, "sub", 1)

    state_x, first_a, logs, coef, weight = call(
        functools.partial(states_a_body, chips, cores),
        [half, half_wide]
        + [sds(log_shape, F32), sds(coef_shape, F32), sds((pieces,) + log_shape[1:], F32)],
        [VMEM] * (chips + 3),
        [VMEM] * 5,
        [pltpu.VMEM((2, chips * pieces * per_block, rows), F32)],
        flops=2 * rows * chips * area,
        moved=8 * chips * area,
    )(*decays, docs, own, far_low)
    from_x = [rotate(state_x, "head", k) for k in range(1, chips)]
    state_b, state_z, first_b = call(
        functools.partial(states_b_body, chips),
        [half, half, half_wide],
        [VMEM] * 4,
        [VMEM] * 3,
        flops=2 * rows * chips * area,
        moved=8 * chips * area,
    )(weight, coef, own, far_high)
    row_factor = coef[places(chips)["row"]] if reach > 1 else None
    past_b = earlier_rows(state_z, row_factor, slice(mid, chips), reach)
    logs_far = rotate(logs, "sub", 1)

    def within(far, blocks, *args):
        return call(
            functools.partial(within_body, cores, far, blocks),
            [sds((mid,) + block[1:], F32)] * 2,
            [VMEM] * 4,
            [VMEM] * 2,
            flops=rows * rows * width,
            moved=4 * rows * width,
        )(*args)

    low, high = (0, mid), (mid, chips)
    own_a = within(False, low, logs, docs, query, own)

    total = call(
        functools.partial(row_total_body, chips),
        half,
        [VMEM] * (2 + others),
        VMEM,
        moved=6 * mid * area,
    )(coef, state_x, *from_x)
    past_a = earlier_rows(total, row_factor, slice(0, mid), reach)

    messages = call(
        functools.partial(messages_body, chips),
        [half] * others,
        [VMEM] * 3,
        [VMEM] * others,
        moved=6 * mid * area,
    )(coef, state_b, past_b)
    from_b = [rotate(messages[k - 1], "head", k) for k in range(1, chips)]

    own_b = within(False, high, logs, docs, query, own)
    other_a = within(True, low, logs_far, docs, query, send_low)
    other_b = within(True, high, logs_far, docs, query, send_high)

    def entering(which, first, past, arrived):
        return call(
            functools.partial(entering_body, chips, which),
            [half] * 2,
            [VMEM] * (3 + others),
            [VMEM] * 2,
            moved=8 * mid * area,
        )(coef, first, past, *arrived)

    def finish(far, which, logs_used, local, state):
        return call(
            functools.partial(finish_body, chips, cores, far, which),
            sds((mid,) + block[1:], BF16),
            [VMEM] * 5,
            VMEM,
            flops=rows * head_width * width // 2,
            moved=3 * rows * width,
        )(logs_used, query, *local, state)

    keep_a, send_a = entering(0, first_a, past_a, from_x)
    far_a = rotate(send_a, "sub", 1)
    out_a = finish(False, 0, logs, own_a, keep_a)
    keep_b, send_b = entering(1, first_b, past_b, from_b)
    far_b = rotate(send_b, "sub", 1)
    out_b = finish(False, 1, logs, own_b, keep_b)
    out_far = finish(True, 0, logs_far, other_a, far_a)
    return call(
        functools.partial(last_body, chips, cores),
        sds((rows, width), BF16),
        [VMEM] * 8,
        ANY,
        [
            pltpu.VMEM((mid,) + block[1:], BF16),
            pltpu.SemaphoreType.DMA((mid,)),
            pltpu.SemaphoreType.DMA((3, mid)),
        ],
        flops=rows * head_width * width,
        moved=7 * rows * width,
    )(logs_far, query, *other_b, far_b, out_a, out_b, out_far)


SLICE_ROOM = 20
PREPARE_ROOM = 24


def solution(mesh):
    rows = P(("groups", "seq", "head", "sub"), None)

    return jax.shard_map(
        per_device,
        mesh=mesh,
        in_specs=(
            rows,
            rows,
            rows,
            P(("head", "sub"), ("groups", "seq")),
            P(("head", "sub"), None),
            P("groups"),
        ),
        out_specs=rows,
        check_vma=False,
    )
```

```python
import functools

import jax
import jax.numpy as jnp
from jax import lax
from jax.experimental import pallas as pl
from jax.experimental.pallas import tpu as pltpu
from jax.sharding import PartitionSpec as P

BF16 = jnp.bfloat16
F32 = jnp.float32
ANY = pl.BlockSpec(memory_space=pl.ANY)
HBM = pl.BlockSpec(memory_space=pltpu.HBM)
VMEM = pl.BlockSpec(memory_space=pltpu.VMEM)
SMEM = pl.BlockSpec(memory_space=pltpu.SMEM)


def rotate(x, axis, step):
    size = lax.axis_size(axis)
    return lax.ppermute(x, axis, [(i, (i + step) % size) for i in range(size)])


def shift(x, axis, step):
    size = lax.axis_size(axis)
    return lax.ppermute(x, axis, [(i, i + step) for i in range(size - step)])


def column(row, rows):
    return jnp.broadcast_to(row, (rows, row.shape[1])).T


def call(body, out_shape, in_specs, out_specs, scratch=(), flops=0, moved=0, aliases=None, vmem=8 << 20):
    return pl.pallas_call(
        body,
        out_shape=out_shape,
        in_specs=in_specs,
        out_specs=out_specs,
        scratch_shapes=list(scratch),
        input_output_aliases=aliases or {},
        cost_estimate=pl.CostEstimate(flops=flops, bytes_accessed=moved, transcendentals=0),
        compiler_params=pltpu.CompilerParams(vmem_limit_bytes=vmem),
    )


def each(low, high, body):
    if high - low == 1:
        body(low)
    elif high > low:
        lax.fori_loop(low, high, lambda i, _: (body(i), 0)[1], 0)


def cols(place, c, width):
    start = (place * width[0] + c) * width[1]
    return pl.ds(start if isinstance(start, int) else pl.multiple_of(start, width[1]), width[1])


def places(chips):
    base = 3 * chips
    return dict(to_start=base, to_end=base + 1, first=base + 2, row=base + 3, second=base + 4)


def pick(index, options):
    result = options[-1]
    for c in range(len(options) - 2, -1, -1):
        result = jnp.where(index == c, options[c], result)
    return result


def states_of(chips, weight, coef, own, far, n, i, keep):
    cores = 2
    core, chip = lax.axis_index("sub"), lax.axis_index("head")
    per_block, rows = weight.shape[2:]
    for c in range(per_block):
        here = slice(c * rows, (c + 1) * rows)
        sums = []
        for ref, block, place in ((own, i, core), (far, n, 1 - core)):
            keys = ref[0, block, :, here].T.astype(F32)
            keys = keys * weight[chip * cores + place, i, c : c + 1, :]
            values = ref[1, block, :, here]
            sums.append(jnp.dot(keys.astype(BF16), values, preferred_element_type=F32))
        first = jnp.where(core == 0, sums[0], sums[1])
        last = jnp.where(core == 0, sums[1], sums[0])
        keep(c, first, last + coef[places(chips)["second"], i, c : c + 1, :] * first)


def tables(chips, cores, decays, docs, logs, coef, weight, stack):
    chip = lax.axis_index("head")
    pieces = chips * cores
    per_block, rows = logs.shape[2:]
    at = places(chips)
    for slot in range(chips):
        for piece in range(pieces):
            place = (slot * pieces + piece) * per_block
            stack[0, place : place + per_block] = decays[slot][:, piece * rows : (piece + 1) * rows]
    earlier = lax.broadcasted_iota(jnp.int32, (rows, rows), 0)
    later = lax.broadcasted_iota(jnp.int32, (rows, rows), 1)
    stack[1] = jnp.dot(
        stack[0],
        jnp.where(earlier <= later, 1.0, 0.0),
        precision=lax.Precision.HIGHEST,
        preferred_element_type=F32,
    )
    for slot in range(chips):
        block = lax.rem(chip - slot + chips, chips)
        logs[pieces, block] = decays[slot][:, pieces * rows :]
        factors = []
        for piece in range(pieces):
            place = (slot * pieces + piece) * per_block
            total = stack[1, place : place + per_block]
            logs[piece, block] = total
            end = jnp.broadcast_to(total[:, rows - 1 :], (per_block, rows))
            weight[piece, block] = jnp.exp(end - total) * docs[1, piece : piece + 1, :]
            passed = jnp.broadcast_to(docs[2, piece : piece + 1, rows - 1 :], (per_block, rows))
            factors.append(jnp.exp(end) * passed)
        through = []
        for c in range(chips):
            product = factors[c * cores]
            for u in range(1, cores):
                product = product * factors[c * cores + u]
            through.append(product)
        one, zero = jnp.ones_like(through[0]), jnp.zeros_like(through[0])

        def between(low, high):
            product = one
            for c in range(low, high):
                product = product * through[c]
            return product

        to_start = pick(chip, [between(0, c) for c in range(chips)])
        coef[at["to_start"], block] = to_start
        coef[at["to_end"], block] = pick(chip, [between(0, c + 1) for c in range(chips)])
        coef[at["first"], block] = pick(chip, [factors[c * cores] for c in range(chips)])
        coef[at["second"], block] = pick(chip, [factors[c * cores + 1] for c in range(chips)])
        coef[at["row"], block] = between(0, chips)
        for back in range(chips):
            source = lax.rem(chip - back + chips, chips)
            coef[back, block] = pick(source, [between(c + 1, chips) for c in range(chips)])
            before = pick(
                chip,
                [between(c - back + 1, c) if 0 <= c - back < c else zero for c in range(chips)],
            )
            coef[chips + back, block] = before
            coef[2 * chips + back, block] = jnp.where(
                (source < chip) & (back > 0), before, to_start
            )


def states_a_body(chips, cores, *refs):
    decays, (docs, own, far) = refs[:chips], refs[chips : chips + 3]
    state_x, state_0, logs, coef, weight, stack = refs[chips + 3 :]
    tables(chips, cores, decays, docs, logs, coef, weight, stack)
    for i in range(chips // 2):

        def keep(c, first, state):
            state_0[i, c] = first
            state_x[i, c] = state.astype(BF16)

        states_of(chips, weight, coef, own, far, i, i, keep)


def states_b_body(chips, weight, coef, own, far, state_b, state_z, state_0):
    mid = chips // 2
    for n in range(mid):
        i = n + mid

        def keep(c, first, state):
            state_0[n, c] = first
            state_b[n, c] = state.astype(BF16)
            state_z[n, c] = (coef[0, i, c : c + 1, :] * state).astype(BF16)

        states_of(chips, weight, coef, own, far, n, i, keep)


def within_body(cores, far, blocks, logs, docs, q, kv, out, carry):
    core = lax.axis_index("sub")
    piece = lax.axis_index("head") * cores + core
    core = 1 - core if far else core
    per_block, rows = logs.shape[2], logs.shape[3]
    docs_here = jnp.broadcast_to(docs[0, pl.ds(piece, 1), :], (rows, rows))
    t = lax.broadcasted_iota(jnp.int32, (rows, rows), 0)
    s = lax.broadcasted_iota(jnp.int32, (rows, rows), 1)
    linked = (docs_here.T == docs_here) & (t >= s)
    carries = column(docs[2, pl.ds(piece, 1), :], rows)
    shift_ = blocks[0] if far else 0

    def heads_of(i):
        for c in range(per_block):
            here = slice(c * rows, (c + 1) * rows)
            row = logs[piece, i, c : c + 1, :]
            down = column(row, rows)
            damping = jnp.exp(jnp.where(linked, down - row, -1e30))
            scores = lax.dot_general(
                q[:, cols(i * cores + core, c, (per_block, rows))],
                kv[0, i - shift_, :, here],
                (((1,), (1,)), ((), ())),
                preferred_element_type=F32,
            )
            out[i - blocks[0], :, here] = jnp.dot(
                (scores * damping).astype(BF16), kv[1, i - shift_, :, here], preferred_element_type=F32
            )
            carry[i - blocks[0], :, here] = jnp.exp(down) * carries

    each(*blocks, heads_of)


def row_total_body(chips, coef, state_x, *refs):
    from_x, total = refs[:-1], refs[-1]

    def join(i):
        for c in range(state_x.shape[1]):
            sum_ = coef[0, i, c : c + 1, :] * state_x[i, c].astype(F32)
            for back in range(1, chips):
                sum_ = sum_ + coef[back, i, c : c + 1, :] * from_x[back - 1][i, c].astype(F32)
            total[i, c] = sum_.astype(BF16)

    each(0, chips // 2, join)


def messages_body(chips, coef, state_b, past_b, *messages):
    chip = lax.axis_index("head")
    mid = chips // 2

    def join(i):
        for c in range(state_b.shape[1]):
            past = past_b[i, c]
            factor = coef[places(chips)["to_end"], i + mid, c : c + 1, :]
            ahead = (state_b[i, c].astype(F32) + factor * past.astype(F32)).astype(BF16)
            for back in range(1, chips):
                messages[back - 1][i, c] = jnp.where(chip + back < chips, ahead, past)

    each(0, mid, join)


def entering_body(chips, half, coef, first, past, *refs):
    others = refs[:-2]
    keep, send = refs[-2:]
    is_first = lax.axis_index("sub") == 0
    at = places(chips)
    mid = chips // 2
    base = (1 + half) * chips

    def join(i):
        for c in range(past.shape[1]):

            def factor(place):
                return coef[place, i + half * mid, c : c + 1, :]

            entering = factor(at["to_start"]) * past[i, c].astype(F32)
            for back in range(1, chips):
                entering = entering + factor(base + back) * others[back - 1][i, c].astype(F32)
            later = first[i, c] + factor(at["first"]) * entering
            keep[i, c] = jnp.where(is_first, entering, later).astype(BF16)
            send[i, c] = jnp.where(is_first, later, entering).astype(BF16)

    each(0, mid, join)


def finish_heads(chips, cores, far, half, logs, q, within, carry, state, n, put):
    core = lax.axis_index("sub")
    core = 1 - core if far else core
    i = n + half * (chips // 2)
    per_block, rows = logs.shape[2:]
    gain = logs[chips * cores, i]
    for c in range(per_block):
        here = slice(c * rows, (c + 1) * rows)
        result = within[n, :, here] + carry[n, :, here] * jnp.dot(
            q[:, cols(i * cores + core, c, (per_block, rows))],
            state[n, c],
            preferred_element_type=F32,
        )
        mean_square = jnp.mean(result * result, axis=1, keepdims=True)
        put(here, (result * lax.rsqrt(mean_square + 1e-06) * gain[c : c + 1, :]).astype(BF16))


def finish_body(chips, cores, half, logs, q, within, carry, state, out):

    def block(n):
        def put(here, value):
            out[n, :, here] = value

        finish_heads(chips, cores, False, half, logs, q, within, carry, state, n, put)

    each(0, chips // 2, block)


def last_body(chips, cores, half, done, logs, q, within, carry, state, *refs):
    finished = refs[:done]
    out, buffer, sem, done_sem = refs[-4:]
    core = lax.axis_index("sub")
    mid = chips // 2
    width = buffer.shape[2]

    def copy(source, i, place, sem):
        target = out.at[:, cols(i * cores + place, 0, (1, width))]
        return pltpu.make_async_copy(source, target, sem)

    copies = []
    for k in range(done):
        for n in range(mid):
            copies.append(copy(finished[k].at[n], n + k * mid, core, done_sem.at[k, n]))
            copies[-1].start()
    for n in range(mid):

        def put(here, value):
            buffer[n, :, here] = value

        finish_heads(chips, cores, True, half, logs, q, within, carry, state, n, put)
        copies.append(copy(buffer.at[n], n + half * mid, 1 - core, sem.at[n]))
        copies[-1].start()
    for one in copies:
        one.wait()


def block_copies(cores, core, blocks, sources, target, sems):
    width = target.shape[3]
    return [
        pltpu.make_async_copy(
            source.at[:, cols(i * cores + core, 0, (1, width))],
            target.at[n, i - blocks[0]],
            sems.at[n, i - blocks[0]],
        )
        for n, source in enumerate(sources)
        for i in range(*blocks)
    ]


def slice_body(chips, cores, k_all, v_all, send, sems):
    core = 1 - lax.axis_index("sub")
    copies = block_copies(cores, core, (0, chips // 2), (k_all, v_all), send, sems)
    for copy in copies:
        copy.start()
    for copy in copies:
        copy.wait()


def pack_body(log_decay, gain, packed):
    packed[:, : log_decay.shape[1]] = log_decay[...]
    packed[:, log_decay.shape[1] :] = gain[...]


def prepare_body(chips, cores, lengths_all, k_all, v_all, send, own, docs, *scratch):
    lengths, send_sems, own_sems, length_sem = scratch
    core = lax.axis_index("sub")
    both = (k_all, v_all)
    copies = block_copies(cores, 1 - core, (chips // 2, chips), both, send, send_sems)
    copies += block_copies(cores, core, (0, chips), both, own, own_sems)
    lengths_copy = pltpu.make_async_copy(lengths_all, lengths, length_sem)
    lengths_copy.start()
    for copy in copies:
        copy.start()
    lengths_copy.wait()
    pieces, rows = docs.shape[1:]
    piece = lax.broadcasted_iota(jnp.int32, (pieces, rows), 0)
    lane = lax.broadcasted_iota(jnp.int32, (pieces, rows), 1)
    first = (lax.axis_index("seq") * pieces + piece) * rows
    here, before = jnp.zeros((pieces, rows), F32), jnp.zeros((pieces, rows), F32)
    start = 0
    for n in range(lengths.shape[0]):
        here += jnp.where(start <= first + lane, 1.0, 0.0)
        before += jnp.where(start < first, 1.0, 0.0)
        start = start + lengths[n]
    end = jnp.broadcast_to(here[:, rows - 1 :], (pieces, rows))
    docs[0] = here
    docs[1] = jnp.where(here == end, 1.0, 0.0)
    docs[2] = jnp.where(here == before, 1.0, 0.0)
    for copy in copies:
        copy.wait()


def earlier_rows(value, row_factor, blocks, reach):
    total, step = value, 1
    factor = row_factor[blocks] if reach > 1 else None
    while step < reach:
        before = shift(total, "seq", step).astype(F32)
        total = (total.astype(F32) + factor[:, :, None, :] * before).astype(BF16)
        factor = factor * shift(factor, "seq", step)
        step *= 2
    return shift(total, "seq", 1)


def per_device(query, key, value, log_decay, gain, doc_lengths):
    rows, width = query.shape
    per_block, row_tokens = log_decay.shape
    head_width = gain.shape[1]
    chips, cores, depth = lax.axis_size("head"), lax.axis_size("sub"), lax.axis_size("seq")
    assert cores == 2 and chips % 2 == 0 and rows == head_width
    pieces = chips * cores
    others = chips - 1
    mid = chips // 2
    reach = max(1, -(-depth // 4))

    def sds(shape, kind):
        return jax.ShapeDtypeStruct(shape, kind)

    square = (per_block, head_width, head_width)
    area = per_block * head_width * head_width
    block = (chips, rows, per_block * head_width)
    half = sds((mid,) + square, BF16)
    half_wide = sds((mid,) + square, F32)
    log_shape = (pieces + 1, chips, per_block, rows)
    coef_shape = (3 * chips + 5, chips, per_block, rows)

    half_kv = sds((2, mid) + block[1:], BF16)
    send_low = call(
        functools.partial(slice_body, chips, cores),
        half_kv,
        [HBM] * 2,
        VMEM,
        [pltpu.SemaphoreType.DMA((2, mid))],
        moved=4 * rows * width,
        vmem=67043328 - SLICE_ROOM * rows * width,
    )(key, value)
    far_low = rotate(send_low, "sub", 1)
    packed = call(
        pack_body,
        sds((per_block, row_tokens + head_width), F32),
        [VMEM] * 2,
        VMEM,
    )(log_decay, gain)
    decays = [packed] + [rotate(packed, "head", k) for k in range(1, chips)]
    send_high, own, docs = call(
        functools.partial(prepare_body, chips, cores),
        [half_kv, sds((2,) + block, BF16), sds((3, pieces, rows), F32)],
        [HBM] * 3,
        [VMEM] * 3,
        [
            pltpu.SMEM(doc_lengths.shape, jnp.int32),
            pltpu.SemaphoreType.DMA((2, mid)),
            pltpu.SemaphoreType.DMA((2, chips)),
            pltpu.SemaphoreType.DMA(()),
        ],
        moved=12 * rows * width,
        vmem=67043328 - PREPARE_ROOM * rows * width,
    )(doc_lengths, key, value)
    far_high = rotate(send_high, "sub", 1)

    state_x, first_a, logs, coef, weight = call(
        functools.partial(states_a_body, chips, cores),
        [half, half_wide]
        + [sds(log_shape, F32), sds(coef_shape, F32), sds((pieces,) + log_shape[1:], F32)],
        [VMEM] * (chips + 3),
        [VMEM] * 5,
        [pltpu.VMEM((2, chips * pieces * per_block, rows), F32)],
        flops=2 * rows * chips * area,
        moved=8 * chips * area,
    )(*decays, docs, own, far_low)
    from_x = [rotate(state_x, "head", k) for k in range(1, chips)]
    state_b, state_z, first_b = call(
        functools.partial(states_b_body, chips),
        [half, half, half_wide],
        [VMEM] * 4,
        [VMEM] * 3,
        flops=2 * rows * chips * area,
        moved=8 * chips * area,
    )(weight, coef, own, far_high)
    row_factor = coef[places(chips)["row"]] if reach > 1 else None
    past_b = earlier_rows(state_z, row_factor, slice(mid, chips), reach)
    logs_far = rotate(logs, "sub", 1)

    def within(far, blocks, *args):
        return call(
            functools.partial(within_body, cores, far, blocks),
            [sds((mid,) + block[1:], F32)] * 2,
            [VMEM] * 4,
            [VMEM] * 2,
            flops=rows * rows * width,
            moved=4 * rows * width,
        )(*args)

    low, high = (0, mid), (mid, chips)
    own_a = within(False, low, logs, docs, query, own)

    total = call(
        functools.partial(row_total_body, chips),
        half,
        [VMEM] * (2 + others),
        VMEM,
        moved=6 * mid * area,
    )(coef, state_x, *from_x)
    past_a = earlier_rows(total, row_factor, slice(0, mid), reach)

    messages = call(
        functools.partial(messages_body, chips),
        [half] * others,
        [VMEM] * 3,
        [VMEM] * others,
        moved=6 * mid * area,
    )(coef, state_b, past_b)
    from_b = [rotate(messages[k - 1], "head", k) for k in range(1, chips)]

    own_b = within(False, high, logs, docs, query, own)
    other_a = within(True, low, logs_far, docs, query, send_low)
    other_b = within(True, high, logs_far, docs, query, send_high)

    def entering(which, first, past, arrived):
        return call(
            functools.partial(entering_body, chips, which),
            [half] * 2,
            [VMEM] * (3 + others),
            [VMEM] * 2,
            moved=8 * mid * area,
        )(coef, first, past, *arrived)

    def finish(which, local, state):
        return call(
            functools.partial(finish_body, chips, cores, which),
            sds((mid,) + block[1:], BF16),
            [VMEM] * 5,
            VMEM,
            flops=rows * head_width * width // 2,
            moved=3 * rows * width,
        )(logs, query, *local, state)

    def last(which, local, state, finished, earlier):
        done = len(finished)
        return call(
            functools.partial(last_body, chips, cores, which, done),
            sds((rows, width), BF16),
            [VMEM] * (5 + done) + [ANY] * len(earlier),
            ANY,
            [
                pltpu.VMEM((mid,) + block[1:], BF16),
                pltpu.SemaphoreType.DMA((mid,)),
                pltpu.SemaphoreType.DMA((max(done, 1), mid)),
            ],
            flops=rows * head_width * width // 2,
            moved=4 * rows * width,
            aliases={5 + done: 0} if earlier else None,
        )(logs_far, query, *local, state, *finished, *earlier)

    keep_a, send_a = entering(0, first_a, past_a, from_x)
    far_a = rotate(send_a, "sub", 1)
    out_a = finish(0, own_a, keep_a)
    keep_b, send_b = entering(1, first_b, past_b, from_b)
    far_b = rotate(send_b, "sub", 1)
    out_b = finish(1, own_b, keep_b)
    out = last(0, other_a, far_a, (out_a, out_b), ())
    return last(1, other_b, far_b, (), (out,))


SLICE_ROOM = 21
PREPARE_ROOM = 24


def solution(mesh):
    rows = P(("groups", "seq", "head", "sub"), None)

    return jax.shard_map(
        per_device,
        mesh=mesh,
        in_specs=(
            rows,
            rows,
            rows,
            P(("head", "sub"), ("groups", "seq")),
            P(("head", "sub"), None),
            P("groups"),
        ),
        out_specs=rows,
        check_vma=False,
    )
```

```python
import functools

import jax
import jax.numpy as jnp
from jax import lax
from jax.experimental import pallas as pl
from jax.experimental.pallas import tpu as pltpu
from jax.sharding import PartitionSpec as P

BF16 = jnp.bfloat16
F32 = jnp.float32
ANY = pl.BlockSpec(memory_space=pl.ANY)
HBM = pl.BlockSpec(memory_space=pltpu.HBM)
VMEM = pl.BlockSpec(memory_space=pltpu.VMEM)
SMEM = pl.BlockSpec(memory_space=pltpu.SMEM)


def rotate(x, axis, step):
    size = lax.axis_size(axis)
    return lax.ppermute(x, axis, [(i, (i + step) % size) for i in range(size)])


def shift(x, axis, step):
    size = lax.axis_size(axis)
    return lax.ppermute(x, axis, [(i, i + step) for i in range(size - step)])


def fold(x):
    depth = lax.axis_size("seq")
    results = []
    for up in range(2):
        down = 1 - up
        pairs = []
        for z in range(depth):
            pairs.append((2 * z + up, 2 * (z + 1) + up if z < depth - 1 else 2 * z + down))
            pairs.append((2 * z + down, 2 * (z - 1) + down if z > 0 else 2 * z + up))
        results.append(lax.ppermute(x, ("seq", "sub"), pairs))
    return results


def of_core(refs, *index):
    if len(refs) == 1:
        return refs[0][index]
    return jnp.where(lax.axis_index("sub") == 0, refs[0][index], refs[1][index])


def column(row, rows):
    return jnp.broadcast_to(row, (rows, row.shape[1])).T


def call(body, out_shape, in_specs, out_specs, scratch=(), flops=0, moved=0, aliases=None, vmem=8 << 20):
    return pl.pallas_call(
        body,
        out_shape=out_shape,
        in_specs=in_specs,
        out_specs=out_specs,
        scratch_shapes=list(scratch),
        input_output_aliases=aliases or {},
        cost_estimate=pl.CostEstimate(flops=flops, bytes_accessed=moved, transcendentals=0),
        compiler_params=pltpu.CompilerParams(vmem_limit_bytes=vmem),
    )


def each(low, high, body):
    if high - low == 1:
        body(low)
    elif high > low:
        lax.fori_loop(low, high, lambda i, _: (body(i), 0)[1], 0)


def cols(place, c, width):
    start = (place * width[0] + c) * width[1]
    return pl.ds(start if isinstance(start, int) else pl.multiple_of(start, width[1]), width[1])


def places(chips):
    base = 3 * chips
    return dict(to_start=base, to_end=base + 1, first=base + 2, row=base + 3, second=base + 4)


def pick(index, options):
    result = options[-1]
    for c in range(len(options) - 2, -1, -1):
        result = jnp.where(index == c, options[c], result)
    return result


def states_of(chips, weight, coef, own, far, n, i, keep):
    cores = 2
    core, chip = lax.axis_index("sub"), lax.axis_index("head")
    per_block, rows = weight.shape[2:]
    for c in range(per_block):
        here = slice(c * rows, (c + 1) * rows)
        sums = []
        for ref, block, place in ((own, i, core), (far, n, 1 - core)):
            keys = ref[0, block, :, here].T.astype(F32)
            keys = keys * weight[chip * cores + place, i, c : c + 1, :]
            values = ref[1, block, :, here]
            sums.append(jnp.dot(keys.astype(BF16), values, preferred_element_type=F32))
        first = jnp.where(core == 0, sums[0], sums[1])
        last = jnp.where(core == 0, sums[1], sums[0])
        keep(c, first, last + coef[places(chips)["second"], i, c : c + 1, :] * first)


def tables(chips, cores, decays, docs, logs, coef, weight, stack):
    chip = lax.axis_index("head")
    pieces = chips * cores
    per_block, rows = logs.shape[2:]
    at = places(chips)
    for slot in range(chips):
        for piece in range(pieces):
            place = (slot * pieces + piece) * per_block
            stack[0, place : place + per_block] = decays[slot][:, piece * rows : (piece + 1) * rows]
    earlier = lax.broadcasted_iota(jnp.int32, (rows, rows), 0)
    later = lax.broadcasted_iota(jnp.int32, (rows, rows), 1)
    stack[1] = jnp.dot(
        stack[0],
        jnp.where(earlier <= later, 1.0, 0.0),
        precision=lax.Precision.HIGHEST,
        preferred_element_type=F32,
    )
    for slot in range(chips):
        block = lax.rem(chip - slot + chips, chips)
        logs[pieces, block] = decays[slot][:, pieces * rows :]
        factors = []
        for piece in range(pieces):
            place = (slot * pieces + piece) * per_block
            total = stack[1, place : place + per_block]
            logs[piece, block] = total
            end = jnp.broadcast_to(total[:, rows - 1 :], (per_block, rows))
            weight[piece, block] = jnp.exp(end - total) * docs[1, piece : piece + 1, :]
            passed = jnp.broadcast_to(docs[2, piece : piece + 1, rows - 1 :], (per_block, rows))
            factors.append(jnp.exp(end) * passed)
        through = []
        for c in range(chips):
            product = factors[c * cores]
            for u in range(1, cores):
                product = product * factors[c * cores + u]
            through.append(product)
        one, zero = jnp.ones_like(through[0]), jnp.zeros_like(through[0])

        def between(low, high):
            product = one
            for c in range(low, high):
                product = product * through[c]
            return product

        to_start = pick(chip, [between(0, c) for c in range(chips)])
        coef[at["to_start"], block] = to_start
        coef[at["to_end"], block] = pick(chip, [between(0, c + 1) for c in range(chips)])
        coef[at["first"], block] = pick(chip, [factors[c * cores] for c in range(chips)])
        coef[at["second"], block] = pick(chip, [factors[c * cores + 1] for c in range(chips)])
        coef[at["row"], block] = between(0, chips)
        for back in range(chips):
            source = lax.rem(chip - back + chips, chips)
            coef[back, block] = pick(source, [between(c + 1, chips) for c in range(chips)])
            before = pick(
                chip,
                [between(c - back + 1, c) if 0 <= c - back < c else zero for c in range(chips)],
            )
            coef[chips + back, block] = before
            coef[2 * chips + back, block] = jnp.where(
                (source < chip) & (back > 0), before, to_start
            )


def states_a_body(chips, cores, *refs):
    decays, (docs, own, far) = refs[:chips], refs[chips : chips + 3]
    state_x, state_0, logs, coef, weight, stack = refs[chips + 3 :]
    tables(chips, cores, decays, docs, logs, coef, weight, stack)
    for i in range(chips // 2):

        def keep(c, first, state):
            state_0[i, c] = first
            state_x[i, c] = state.astype(BF16)

        states_of(chips, weight, coef, own, far, i, i, keep)


def states_b_body(chips, weight, coef, own, far, state_b, state_z, state_0):
    mid = chips // 2
    for n in range(mid):
        i = n + mid

        def keep(c, first, state):
            state_0[n, c] = first
            state_b[n, c] = state.astype(BF16)
            state_z[n, c] = (coef[0, i, c : c + 1, :] * state).astype(BF16)

        states_of(chips, weight, coef, own, far, n, i, keep)


def within_body(cores, far, blocks, logs, docs, q, kv, out, carry):
    core = lax.axis_index("sub")
    piece = lax.axis_index("head") * cores + core
    core = 1 - core if far else core
    per_block, rows = logs.shape[2], logs.shape[3]
    docs_here = jnp.broadcast_to(docs[0, pl.ds(piece, 1), :], (rows, rows))
    t = lax.broadcasted_iota(jnp.int32, (rows, rows), 0)
    s = lax.broadcasted_iota(jnp.int32, (rows, rows), 1)
    linked = (docs_here.T == docs_here) & (t >= s)
    carries = column(docs[2, pl.ds(piece, 1), :], rows)
    shift_ = blocks[0] if far else 0

    def heads_of(i):
        for c in range(per_block):
            here = slice(c * rows, (c + 1) * rows)
            row = logs[piece, i, c : c + 1, :]
            down = column(row, rows)
            damping = jnp.exp(jnp.where(linked, down - row, -1e30))
            scores = lax.dot_general(
                q[:, cols(i * cores + core, c, (per_block, rows))],
                kv[0, i - shift_, :, here],
                (((1,), (1,)), ((), ())),
                preferred_element_type=F32,
            )
            out[i - blocks[0], :, here] = jnp.dot(
                (scores * damping).astype(BF16), kv[1, i - shift_, :, here], preferred_element_type=F32
            )
            carry[i - blocks[0], :, here] = jnp.exp(down) * carries

    each(*blocks, heads_of)


def row_total_body(chips, coef, state_x, *refs):
    from_x, total = refs[:-1], refs[-1]

    def join(i):
        for c in range(state_x.shape[1]):
            sum_ = coef[0, i, c : c + 1, :] * state_x[i, c].astype(F32)
            for back in range(1, chips):
                sum_ = sum_ + coef[back, i, c : c + 1, :] * from_x[back - 1][i, c].astype(F32)
            total[i, c] = sum_.astype(BF16)

    each(0, chips // 2, join)


def messages_body(chips, parts, coef, state_b, *refs):
    past_b, messages = refs[:parts], refs[parts:]
    chip = lax.axis_index("head")
    mid = chips // 2

    def join(i):
        for c in range(state_b.shape[1]):
            past = of_core(past_b, i, c)
            factor = coef[places(chips)["to_end"], i + mid, c : c + 1, :]
            ahead = (state_b[i, c].astype(F32) + factor * past.astype(F32)).astype(BF16)
            for back in range(1, chips):
                messages[back - 1][i, c] = jnp.where(chip + back < chips, ahead, past)

    each(0, mid, join)


def entering_body(chips, half, parts, coef, first, *refs):
    past, others = refs[:parts], refs[parts:-2]
    keep, send = refs[-2:]
    is_first = lax.axis_index("sub") == 0
    at = places(chips)
    mid = chips // 2
    base = (1 + half) * chips

    def join(i):
        for c in range(keep.shape[1]):

            def factor(place):
                return coef[place, i + half * mid, c : c + 1, :]

            entering = factor(at["to_start"]) * of_core(past, i, c).astype(F32)
            for back in range(1, chips):
                entering = entering + factor(base + back) * others[back - 1][i, c].astype(F32)
            later = first[i, c] + factor(at["first"]) * entering
            keep[i, c] = jnp.where(is_first, entering, later).astype(BF16)
            send[i, c] = jnp.where(is_first, later, entering).astype(BF16)

    each(0, mid, join)


def finish_heads(chips, cores, far, half, logs, q, within, carry, state, n, put):
    core = lax.axis_index("sub")
    core = 1 - core if far else core
    i = n + half * (chips // 2)
    per_block, rows = logs.shape[2:]
    gain = logs[chips * cores, i]
    for c in range(per_block):
        here = slice(c * rows, (c + 1) * rows)
        result = within[n, :, here] + carry[n, :, here] * jnp.dot(
            q[:, cols(i * cores + core, c, (per_block, rows))],
            state[n, c],
            preferred_element_type=F32,
        )
        mean_square = jnp.mean(result * result, axis=1, keepdims=True)
        put(here, (result * lax.rsqrt(mean_square + 1e-06) * gain[c : c + 1, :]).astype(BF16))


def finish_body(chips, cores, half, logs, q, within, carry, state, out):

    def block(n):
        def put(here, value):
            out[n, :, here] = value

        finish_heads(chips, cores, False, half, logs, q, within, carry, state, n, put)

    each(0, chips // 2, block)


def last_body(chips, cores, half, done, logs, q, within, carry, state, *refs):
    finished = refs[:done]
    out, buffer, sem, done_sem = refs[-4:]
    core = lax.axis_index("sub")
    mid = chips // 2
    width = buffer.shape[2]

    def copy(source, i, place, sem):
        target = out.at[:, cols(i * cores + place, 0, (1, width))]
        return pltpu.make_async_copy(source, target, sem)

    copies = []
    for k in range(done):
        for n in range(mid):
            copies.append(copy(finished[k].at[n], n + k * mid, core, done_sem.at[k, n]))
            copies[-1].start()
    for n in range(mid):

        def put(here, value):
            buffer[n, :, here] = value

        finish_heads(chips, cores, True, half, logs, q, within, carry, state, n, put)
        copies.append(copy(buffer.at[n], n + half * mid, 1 - core, sem.at[n]))
        copies[-1].start()
    for one in copies:
        one.wait()


def block_copies(cores, core, blocks, sources, target, sems):
    width = target.shape[3]
    return [
        pltpu.make_async_copy(
            source.at[:, cols(i * cores + core, 0, (1, width))],
            target.at[n, i - blocks[0]],
            sems.at[n, i - blocks[0]],
        )
        for n, source in enumerate(sources)
        for i in range(*blocks)
    ]


def slice_body(chips, cores, k_all, v_all, send, sems):
    core = 1 - lax.axis_index("sub")
    copies = block_copies(cores, core, (0, chips // 2), (k_all, v_all), send, sems)
    for copy in copies:
        copy.start()
    for copy in copies:
        copy.wait()


def pack_body(log_decay, gain, packed):
    packed[:, : log_decay.shape[1]] = log_decay[...]
    packed[:, log_decay.shape[1] :] = gain[...]


def prepare_body(chips, cores, lengths_all, k_all, v_all, send, own, docs, *scratch):
    lengths, send_sems, own_sems, length_sem = scratch
    core = lax.axis_index("sub")
    both = (k_all, v_all)
    copies = block_copies(cores, 1 - core, (chips // 2, chips), both, send, send_sems)
    copies += block_copies(cores, core, (0, chips), both, own, own_sems)
    lengths_copy = pltpu.make_async_copy(lengths_all, lengths, length_sem)
    lengths_copy.start()
    for copy in copies:
        copy.start()
    lengths_copy.wait()
    pieces, rows = docs.shape[1:]
    piece = lax.broadcasted_iota(jnp.int32, (pieces, rows), 0)
    lane = lax.broadcasted_iota(jnp.int32, (pieces, rows), 1)
    first = (lax.axis_index("seq") * pieces + piece) * rows
    here, before = jnp.zeros((pieces, rows), F32), jnp.zeros((pieces, rows), F32)
    start = 0
    for n in range(lengths.shape[0]):
        here += jnp.where(start <= first + lane, 1.0, 0.0)
        before += jnp.where(start < first, 1.0, 0.0)
        start = start + lengths[n]
    end = jnp.broadcast_to(here[:, rows - 1 :], (pieces, rows))
    docs[0] = here
    docs[1] = jnp.where(here == end, 1.0, 0.0)
    docs[2] = jnp.where(here == before, 1.0, 0.0)
    for copy in copies:
        copy.wait()


def earlier_rows(value, row_factor, blocks, reach):
    if reach == 1:
        return fold(value)
    total, step = value, 1
    factor = row_factor[blocks] if reach > 1 else None
    while step < reach:
        before = shift(total, "seq", step).astype(F32)
        total = (total.astype(F32) + factor[:, :, None, :] * before).astype(BF16)
        factor = factor * shift(factor, "seq", step)
        step *= 2
    return [shift(total, "seq", 1)]


def per_device(query, key, value, log_decay, gain, doc_lengths):
    rows, width = query.shape
    per_block, row_tokens = log_decay.shape
    head_width = gain.shape[1]
    chips, cores, depth = lax.axis_size("head"), lax.axis_size("sub"), lax.axis_size("seq")
    assert cores == 2 and chips % 2 == 0 and rows == head_width
    pieces = chips * cores
    others = chips - 1
    mid = chips // 2
    reach = max(1, -(-depth // 4))

    def sds(shape, kind):
        return jax.ShapeDtypeStruct(shape, kind)

    square = (per_block, head_width, head_width)
    area = per_block * head_width * head_width
    block = (chips, rows, per_block * head_width)
    half = sds((mid,) + square, BF16)
    half_wide = sds((mid,) + square, F32)
    log_shape = (pieces + 1, chips, per_block, rows)
    coef_shape = (3 * chips + 5, chips, per_block, rows)

    half_kv = sds((2, mid) + block[1:], BF16)
    send_low = call(
        functools.partial(slice_body, chips, cores),
        half_kv,
        [HBM] * 2,
        VMEM,
        [pltpu.SemaphoreType.DMA((2, mid))],
        moved=4 * rows * width,
        vmem=67043328 - SLICE_ROOM * rows * width,
    )(key, value)
    far_low = rotate(send_low, "sub", 1)
    packed = call(
        pack_body,
        sds((per_block, row_tokens + head_width), F32),
        [VMEM] * 2,
        VMEM,
    )(log_decay, gain)
    decays = [packed] + [rotate(packed, "head", k) for k in range(1, chips)]
    send_high, own, docs = call(
        functools.partial(prepare_body, chips, cores),
        [half_kv, sds((2,) + block, BF16), sds((3, pieces, rows), F32)],
        [HBM] * 3,
        [VMEM] * 3,
        [
            pltpu.SMEM(doc_lengths.shape, jnp.int32),
            pltpu.SemaphoreType.DMA((2, mid)),
            pltpu.SemaphoreType.DMA((2, chips)),
            pltpu.SemaphoreType.DMA(()),
        ],
        moved=12 * rows * width,
        vmem=67043328 - PREPARE_ROOM * rows * width,
    )(doc_lengths, key, value)
    far_high = rotate(send_high, "sub", 1)

    state_x, first_a, logs, coef, weight = call(
        functools.partial(states_a_body, chips, cores),
        [half, half_wide]
        + [sds(log_shape, F32), sds(coef_shape, F32), sds((pieces,) + log_shape[1:], F32)],
        [VMEM] * (chips + 3),
        [VMEM] * 5,
        [pltpu.VMEM((2, chips * pieces * per_block, rows), F32)],
        flops=2 * rows * chips * area,
        moved=8 * chips * area,
    )(*decays, docs, own, far_low)
    from_x = [rotate(state_x, "head", k) for k in range(1, chips)]
    state_b, state_z, first_b = call(
        functools.partial(states_b_body, chips),
        [half, half, half_wide],
        [VMEM] * 4,
        [VMEM] * 3,
        flops=2 * rows * chips * area,
        moved=8 * chips * area,
    )(weight, coef, own, far_high)
    row_factor = coef[places(chips)["row"]] if reach > 1 else None
    past_b = earlier_rows(state_z, row_factor, slice(mid, chips), reach)
    logs_far = rotate(logs, "sub", 1)

    def within(far, blocks, *args):
        return call(
            functools.partial(within_body, cores, far, blocks),
            [sds((mid,) + block[1:], F32)] * 2,
            [VMEM] * 4,
            [VMEM] * 2,
            flops=rows * rows * width,
            moved=4 * rows * width,
        )(*args)

    low, high = (0, mid), (mid, chips)
    own_a = within(False, low, logs, docs, query, own)

    total = call(
        functools.partial(row_total_body, chips),
        half,
        [VMEM] * (2 + others),
        VMEM,
        moved=6 * mid * area,
    )(coef, state_x, *from_x)
    past_a = earlier_rows(total, row_factor, slice(0, mid), reach)

    messages = call(
        functools.partial(messages_body, chips, len(past_b)),
        [half] * others,
        [VMEM] * (2 + len(past_b)),
        [VMEM] * others,
        moved=6 * mid * area,
    )(coef, state_b, *past_b)
    from_b = [rotate(messages[k - 1], "head", k) for k in range(1, chips)]

    own_b = within(False, high, logs, docs, query, own)
    other_a = within(True, low, logs_far, docs, query, send_low)
    other_b = within(True, high, logs_far, docs, query, send_high)

    def entering(which, first, past, arrived):
        return call(
            functools.partial(entering_body, chips, which, len(past)),
            [half] * 2,
            [VMEM] * (2 + len(past) + others),
            [VMEM] * 2,
            moved=8 * mid * area,
        )(coef, first, *past, *arrived)

    def finish(which, local, state):
        return call(
            functools.partial(finish_body, chips, cores, which),
            sds((mid,) + block[1:], BF16),
            [VMEM] * 5,
            VMEM,
            flops=rows * head_width * width // 2,
            moved=3 * rows * width,
        )(logs, query, *local, state)

    def last(which, local, state, finished, earlier):
        done = len(finished)
        return call(
            functools.partial(last_body, chips, cores, which, done),
            sds((rows, width), BF16),
            [VMEM] * (5 + done) + [ANY] * len(earlier),
            ANY,
            [
                pltpu.VMEM((mid,) + block[1:], BF16),
                pltpu.SemaphoreType.DMA((mid,)),
                pltpu.SemaphoreType.DMA((max(done, 1), mid)),
            ],
            flops=rows * head_width * width // 2,
            moved=4 * rows * width,
            aliases={5 + done: 0} if earlier else None,
        )(logs_far, query, *local, state, *finished, *earlier)

    keep_a, send_a = entering(0, first_a, past_a, from_x)
    far_a = rotate(send_a, "sub", 1)
    out_a = finish(0, own_a, keep_a)
    keep_b, send_b = entering(1, first_b, past_b, from_b)
    far_b = rotate(send_b, "sub", 1)
    out_b = finish(1, own_b, keep_b)
    out = last(0, other_a, far_a, (out_a, out_b), ())
    return last(1, other_b, far_b, (), (out,))


SLICE_ROOM = 21
PREPARE_ROOM = 24


def solution(mesh):
    rows = P(("groups", "seq", "head", "sub"), None)

    return jax.shard_map(
        per_device,
        mesh=mesh,
        in_specs=(
            rows,
            rows,
            rows,
            P(("head", "sub"), ("groups", "seq")),
            P(("head", "sub"), None),
            P("groups"),
        ),
        out_specs=rows,
        check_vma=False,
    )
```

```python
import functools

import jax
import jax.numpy as jnp
from jax import lax
from jax.experimental import pallas as pl
from jax.experimental.pallas import tpu as pltpu
from jax.sharding import PartitionSpec as P

BF16 = jnp.bfloat16
F32 = jnp.float32
ANY = pl.BlockSpec(memory_space=pl.ANY)
HBM = pl.BlockSpec(memory_space=pltpu.HBM)
VMEM = pl.BlockSpec(memory_space=pltpu.VMEM)
SMEM = pl.BlockSpec(memory_space=pltpu.SMEM)


def rotate(x, axis, step):
    size = lax.axis_size(axis)
    return lax.ppermute(x, axis, [(i, (i + step) % size) for i in range(size)])


def shift(x, axis, step):
    size = lax.axis_size(axis)
    return lax.ppermute(x, axis, [(i, i + step) for i in range(size - step)])


def fold(x):
    depth = lax.axis_size("seq")
    results = []
    for up in range(2):
        down = 1 - up
        pairs = []
        for z in range(depth):
            pairs.append((2 * z + up, 2 * (z + 1) + up if z < depth - 1 else 2 * z + down))
            pairs.append((2 * z + down, 2 * (z - 1) + down if z > 0 else 2 * z + up))
        results.append(lax.ppermute(x, ("seq", "sub"), pairs))
    return results


def of_core(refs, *index):
    if len(refs) == 1:
        return refs[0][index]
    return jnp.where(lax.axis_index("sub") == 0, refs[0][index], refs[1][index])


def column(row, rows):
    return jnp.broadcast_to(row, (rows, row.shape[1])).T


def call(body, out_shape, in_specs, out_specs, scratch=(), flops=0, moved=0, aliases=None, vmem=8 << 20):
    return pl.pallas_call(
        body,
        out_shape=out_shape,
        in_specs=in_specs,
        out_specs=out_specs,
        scratch_shapes=list(scratch),
        input_output_aliases=aliases or {},
        cost_estimate=pl.CostEstimate(flops=flops, bytes_accessed=moved, transcendentals=0),
        compiler_params=pltpu.CompilerParams(vmem_limit_bytes=vmem),
    )


def each(low, high, body):
    if high - low == 1:
        body(low)
    elif high > low:
        lax.fori_loop(low, high, lambda i, _: (body(i), 0)[1], 0)


def cols(place, c, width, count=1):
    start = (place * width[0] + c) * width[1]
    start = start if isinstance(start, int) else pl.multiple_of(start, width[1])
    return pl.ds(start, count * width[1])


def places(chips):
    base = 3 * chips
    return dict(to_start=base, to_end=base + 1, first=base + 2, row=base + 3, second=base + 4)


def pick(index, options):
    result = options[-1]
    for c in range(len(options) - 2, -1, -1):
        result = jnp.where(index == c, options[c], result)
    return result


def states_of(chips, weight, coef, own, far, n, i, keep):
    cores = 2
    core, chip = lax.axis_index("sub"), lax.axis_index("head")
    per_block, rows = weight.shape[2:]
    for c in range(per_block):
        here = slice(c * rows, (c + 1) * rows)
        sums = []
        for ref, block, place in ((own, i, core), (far, n, 1 - core)):
            keys = ref[0, block, :, here].T.astype(F32)
            keys = keys * weight[chip * cores + place, i, c : c + 1, :]
            values = ref[1, block, :, here]
            sums.append(jnp.dot(keys.astype(BF16), values, preferred_element_type=F32))
        first = jnp.where(core == 0, sums[0], sums[1])
        last = jnp.where(core == 0, sums[1], sums[0])
        keep(c, first, last + coef[places(chips)["second"], i, c : c + 1, :] * first)


def tables(chips, cores, decays, docs, logs, coef, weight, stack):
    chip = lax.axis_index("head")
    pieces = chips * cores
    per_block, rows = logs.shape[2:]
    at = places(chips)
    for slot in range(chips):
        for piece in range(pieces):
            place = (slot * pieces + piece) * per_block
            stack[0, place : place + per_block] = decays[slot][:, piece * rows : (piece + 1) * rows]
    earlier = lax.broadcasted_iota(jnp.int32, (rows, rows), 0)
    later = lax.broadcasted_iota(jnp.int32, (rows, rows), 1)
    stack[1] = jnp.dot(
        stack[0],
        jnp.where(earlier <= later, 1.0, 0.0),
        precision=lax.Precision.HIGHEST,
        preferred_element_type=F32,
    )
    for slot in range(chips):
        block = lax.rem(chip - slot + chips, chips)
        logs[pieces, block] = decays[slot][:, pieces * rows :]
        factors = []
        for piece in range(pieces):
            place = (slot * pieces + piece) * per_block
            total = stack[1, place : place + per_block]
            logs[piece, block] = total
            end = jnp.broadcast_to(total[:, rows - 1 :], (per_block, rows))
            weight[piece, block] = jnp.exp(end - total) * docs[1, piece : piece + 1, :]
            passed = jnp.broadcast_to(docs[2, piece : piece + 1, rows - 1 :], (per_block, rows))
            factors.append(jnp.exp(end) * passed)
        through = []
        for c in range(chips):
            product = factors[c * cores]
            for u in range(1, cores):
                product = product * factors[c * cores + u]
            through.append(product)
        one, zero = jnp.ones_like(through[0]), jnp.zeros_like(through[0])

        def between(low, high):
            product = one
            for c in range(low, high):
                product = product * through[c]
            return product

        to_start = pick(chip, [between(0, c) for c in range(chips)])
        coef[at["to_start"], block] = to_start
        coef[at["to_end"], block] = pick(chip, [between(0, c + 1) for c in range(chips)])
        coef[at["first"], block] = pick(chip, [factors[c * cores] for c in range(chips)])
        coef[at["second"], block] = pick(chip, [factors[c * cores + 1] for c in range(chips)])
        coef[at["row"], block] = between(0, chips)
        for back in range(chips):
            source = lax.rem(chip - back + chips, chips)
            coef[back, block] = pick(source, [between(c + 1, chips) for c in range(chips)])
            before = pick(
                chip,
                [between(c - back + 1, c) if 0 <= c - back < c else zero for c in range(chips)],
            )
            coef[chips + back, block] = before
            coef[2 * chips + back, block] = jnp.where(
                (source < chip) & (back > 0), before, to_start
            )


def states_a_body(chips, cores, *refs):
    decays, (docs, own, far) = refs[:chips], refs[chips : chips + 3]
    state_x, state_0, logs, coef, weight, stack = refs[chips + 3 :]
    tables(chips, cores, decays, docs, logs, coef, weight, stack)
    for i in range(chips // 2):

        def keep(c, first, state):
            state_0[i, c] = first
            state_x[i, c] = state.astype(BF16)

        states_of(chips, weight, coef, own, far, i, i, keep)


def states_b_body(chips, weight, coef, own, far, state_b, state_z, state_0):
    mid = chips // 2
    for n in range(mid):
        i = n + mid

        def keep(c, first, state):
            state_0[n, c] = first
            state_b[n, c] = state.astype(BF16)
            state_z[n, c] = (coef[0, i, c : c + 1, :] * state).astype(BF16)

        states_of(chips, weight, coef, own, far, n, i, keep)


def within_body(cores, far, blocks, logs, docs, q, kv, out, carry):
    core = lax.axis_index("sub")
    piece = lax.axis_index("head") * cores + core
    core = 1 - core if far else core
    per_block, rows = logs.shape[2], logs.shape[3]
    docs_here = jnp.broadcast_to(docs[0, pl.ds(piece, 1), :], (rows, rows))
    t = lax.broadcasted_iota(jnp.int32, (rows, rows), 0)
    s = lax.broadcasted_iota(jnp.int32, (rows, rows), 1)
    linked = (docs_here.T == docs_here) & (t >= s)
    carries = column(docs[2, pl.ds(piece, 1), :], rows)
    shift_ = blocks[0] if far else 0

    def heads_of(i):
        for c in range(per_block):
            here = slice(c * rows, (c + 1) * rows)
            row = logs[piece, i, c : c + 1, :]
            down = column(row, rows)
            damping = jnp.exp(jnp.where(linked, down - row, -1e30))
            scores = lax.dot_general(
                q[:, cols(i * cores + core, c, (per_block, rows))],
                kv[0, i - shift_, :, here],
                (((1,), (1,)), ((), ())),
                preferred_element_type=F32,
            )
            out[i - blocks[0], :, here] = jnp.dot(
                (scores * damping).astype(BF16), kv[1, i - shift_, :, here], preferred_element_type=F32
            )
            carry[i - blocks[0], :, here] = jnp.exp(down) * carries

    each(*blocks, heads_of)


def row_total_body(chips, coef, state_x, *refs):
    from_x, total = refs[:-1], refs[-1]

    def join(i):
        for c in range(state_x.shape[1]):
            sum_ = coef[0, i, c : c + 1, :] * state_x[i, c].astype(F32)
            for back in range(1, chips):
                sum_ = sum_ + coef[back, i, c : c + 1, :] * from_x[back - 1][i, c].astype(F32)
            total[i, c] = sum_.astype(BF16)

    each(0, chips // 2, join)


def messages_body(chips, parts, coef, state_b, *refs):
    past_b, messages = refs[:parts], refs[parts:]
    chip = lax.axis_index("head")
    mid = chips // 2

    def join(i):
        for c in range(state_b.shape[1]):
            past = of_core(past_b, i, c)
            factor = coef[places(chips)["to_end"], i + mid, c : c + 1, :]
            ahead = (state_b[i, c].astype(F32) + factor * past.astype(F32)).astype(BF16)
            for back in range(1, chips):
                messages[back - 1][i, c] = jnp.where(chip + back < chips, ahead, past)

    each(0, mid, join)


def entering_body(chips, half, parts, coef, first, *refs):
    past, others = refs[:parts], refs[parts:-2]
    keep, send = refs[-2:]
    is_first = lax.axis_index("sub") == 0
    at = places(chips)
    mid = chips // 2
    base = (1 + half) * chips

    def join(i):
        for c in range(keep.shape[1]):

            def factor(place):
                return coef[place, i + half * mid, c : c + 1, :]

            entering = factor(at["to_start"]) * of_core(past, i, c).astype(F32)
            for back in range(1, chips):
                entering = entering + factor(base + back) * others[back - 1][i, c].astype(F32)
            later = first[i, c] + factor(at["first"]) * entering
            keep[i, c] = jnp.where(is_first, entering, later).astype(BF16)
            send[i, c] = jnp.where(is_first, later, entering).astype(BF16)

    each(0, mid, join)


def finish_heads(chips, cores, far, half, logs, q, within, carry, state, n, put):
    core = lax.axis_index("sub")
    core = 1 - core if far else core
    i = n + half * (chips // 2)
    per_block, rows = logs.shape[2:]
    gain = logs[chips * cores, i]
    for c in range(per_block):
        here = slice(c * rows, (c + 1) * rows)
        result = within[n, :, here] + carry[n, :, here] * jnp.dot(
            q[:, cols(i * cores + core, c, (per_block, rows))],
            state[n, c],
            preferred_element_type=F32,
        )
        mean_square = jnp.mean(result * result, axis=1, keepdims=True)
        put(here, (result * lax.rsqrt(mean_square + 1e-06) * gain[c : c + 1, :]).astype(BF16))


def finish_body(chips, cores, half, logs, q, within, carry, state, out):

    def block(n):
        def put(here, value):
            out[n, :, here] = value

        finish_heads(chips, cores, False, half, logs, q, within, carry, state, n, put)

    each(0, chips // 2, block)


def last_body(chips, cores, half, done, logs, q, within, carry, state, *refs):
    finished = refs[:done]
    out, buffer, sem, done_sem = refs[-4:]
    core = lax.axis_index("sub")
    mid = chips // 2
    rows, width = buffer.shape[1:]

    def copy(source, i, place, sem):
        target = out.at[:, cols(i * cores + place, 0, (1, width))]
        return pltpu.make_async_copy(source, target, sem)

    copies = []
    for k in range(done):
        for n in range(mid):
            copies.append(copy(finished[k].at[n], n + k * mid, core, done_sem.at[k, n]))
            copies[-1].start()
    for n in range(mid):

        def put(here, value):
            buffer[n, :, here] = value
            c = here.stop // rows - 1
            if c % 2 == 1:
                pair = slice(here.stop - 2 * rows, here.stop)
                place = cols((n + half * mid) * cores + 1 - core, c - 1, (width // rows, rows), 2)
                copies.append(
                    pltpu.make_async_copy(
                        buffer.at[n, :, pair], out.at[:, place], sem.at[n, c // 2]
                    )
                )
                copies[-1].start()

        finish_heads(chips, cores, True, half, logs, q, within, carry, state, n, put)
    for one in copies:
        one.wait()


def block_copies(cores, core, blocks, sources, target, sems):
    width = target.shape[3]
    parts = sems.shape[2]
    rows = target.shape[2] // parts
    return [
        pltpu.make_async_copy(
            source.at[part * rows : (part + 1) * rows, cols(i * cores + core, 0, (1, width))],
            target.at[n, i - blocks[0], part * rows : (part + 1) * rows],
            sems.at[n, i - blocks[0], part],
        )
        for n, source in enumerate(sources)
        for i in range(*blocks)
        for part in range(parts)
    ]


def slice_body(chips, cores, k_all, v_all, send, sems):
    core = 1 - lax.axis_index("sub")
    copies = block_copies(cores, core, (0, chips // 2), (k_all, v_all), send, sems)
    for copy in copies:
        copy.start()
    for copy in copies:
        copy.wait()


def pack_body(log_decay, gain, packed):
    packed[:, : log_decay.shape[1]] = log_decay[...]
    packed[:, log_decay.shape[1] :] = gain[...]


def prepare_body(chips, cores, lengths_all, k_all, v_all, send, own, docs, *scratch):
    lengths, send_sems, own_sems, length_sem = scratch
    core = lax.axis_index("sub")
    both = (k_all, v_all)
    copies = block_copies(cores, 1 - core, (chips // 2, chips), both, send, send_sems)
    copies += block_copies(cores, core, (0, chips), both, own, own_sems)
    lengths_copy = pltpu.make_async_copy(lengths_all, lengths, length_sem)
    lengths_copy.start()
    for copy in copies:
        copy.start()
    lengths_copy.wait()
    pieces, rows = docs.shape[1:]
    piece = lax.broadcasted_iota(jnp.int32, (pieces, rows), 0)
    lane = lax.broadcasted_iota(jnp.int32, (pieces, rows), 1)
    first = (lax.axis_index("seq") * pieces + piece) * rows
    here, before = jnp.zeros((pieces, rows), F32), jnp.zeros((pieces, rows), F32)
    start = 0
    for n in range(lengths.shape[0]):
        here += jnp.where(start <= first + lane, 1.0, 0.0)
        before += jnp.where(start < first, 1.0, 0.0)
        start = start + lengths[n]
    end = jnp.broadcast_to(here[:, rows - 1 :], (pieces, rows))
    docs[0] = here
    docs[1] = jnp.where(here == end, 1.0, 0.0)
    docs[2] = jnp.where(here == before, 1.0, 0.0)
    for copy in copies:
        copy.wait()


def earlier_rows(value, row_factor, blocks, reach):
    if reach == 1:
        return fold(value)
    total, step = value, 1
    factor = row_factor[blocks] if reach > 1 else None
    while step < reach:
        before = shift(total, "seq", step).astype(F32)
        total = (total.astype(F32) + factor[:, :, None, :] * before).astype(BF16)
        factor = factor * shift(factor, "seq", step)
        step *= 2
    return [shift(total, "seq", 1)]


def per_device(query, key, value, log_decay, gain, doc_lengths):
    rows, width = query.shape
    per_block, row_tokens = log_decay.shape
    head_width = gain.shape[1]
    chips, cores, depth = lax.axis_size("head"), lax.axis_size("sub"), lax.axis_size("seq")
    assert cores == 2 and chips % 2 == 0 and rows == head_width
    pieces = chips * cores
    others = chips - 1
    mid = chips // 2
    reach = max(1, -(-depth // 4))

    def sds(shape, kind):
        return jax.ShapeDtypeStruct(shape, kind)

    square = (per_block, head_width, head_width)
    area = per_block * head_width * head_width
    block = (chips, rows, per_block * head_width)
    half = sds((mid,) + square, BF16)
    half_wide = sds((mid,) + square, F32)
    log_shape = (pieces + 1, chips, per_block, rows)
    coef_shape = (3 * chips + 5, chips, per_block, rows)

    half_kv = sds((2, mid) + block[1:], BF16)
    send_low = call(
        functools.partial(slice_body, chips, cores),
        half_kv,
        [HBM] * 2,
        VMEM,
        [pltpu.SemaphoreType.DMA((2, mid, CUTS))],
        moved=4 * rows * width,
        vmem=67043328 - SLICE_ROOM * rows * width,
    )(key, value)
    far_low = rotate(send_low, "sub", 1)
    packed = call(
        pack_body,
        sds((per_block, row_tokens + head_width), F32),
        [VMEM] * 2,
        VMEM,
    )(log_decay, gain)
    decays = [packed] + [rotate(packed, "head", k) for k in range(1, chips)]
    send_high, own, docs = call(
        functools.partial(prepare_body, chips, cores),
        [half_kv, sds((2,) + block, BF16), sds((3, pieces, rows), F32)],
        [HBM] * 3,
        [VMEM] * 3,
        [
            pltpu.SMEM(doc_lengths.shape, jnp.int32),
            pltpu.SemaphoreType.DMA((2, mid, CUTS)),
            pltpu.SemaphoreType.DMA((2, chips, CUTS)),
            pltpu.SemaphoreType.DMA(()),
        ],
        moved=12 * rows * width,
        vmem=67043328 - PREPARE_ROOM * rows * width,
    )(doc_lengths, key, value)
    far_high = rotate(send_high, "sub", 1)

    state_x, first_a, logs, coef, weight = call(
        functools.partial(states_a_body, chips, cores),
        [half, half_wide]
        + [sds(log_shape, F32), sds(coef_shape, F32), sds((pieces,) + log_shape[1:], F32)],
        [VMEM] * (chips + 3),
        [VMEM] * 5,
        [pltpu.VMEM((2, chips * pieces * per_block, rows), F32)],
        flops=2 * rows * chips * area,
        moved=8 * chips * area,
    )(*decays, docs, own, far_low)
    from_x = [rotate(state_x, "head", k) for k in range(1, chips)]
    state_b, state_z, first_b = call(
        functools.partial(states_b_body, chips),
        [half, half, half_wide],
        [VMEM] * 4,
        [VMEM] * 3,
        flops=2 * rows * chips * area,
        moved=8 * chips * area,
    )(weight, coef, own, far_high)
    row_factor = coef[places(chips)["row"]] if reach > 1 else None
    past_b = earlier_rows(state_z, row_factor, slice(mid, chips), reach)
    logs_far = rotate(logs, "sub", 1)

    def within(far, blocks, *args):
        return call(
            functools.partial(within_body, cores, far, blocks),
            [sds((mid,) + block[1:], F32)] * 2,
            [VMEM] * 4,
            [VMEM] * 2,
            flops=rows * rows * width,
            moved=4 * rows * width,
        )(*args)

    low, high = (0, mid), (mid, chips)
    own_a = within(False, low, logs, docs, query, own)

    total = call(
        functools.partial(row_total_body, chips),
        half,
        [VMEM] * (2 + others),
        VMEM,
        moved=6 * mid * area,
    )(coef, state_x, *from_x)
    past_a = earlier_rows(total, row_factor, slice(0, mid), reach)

    messages = call(
        functools.partial(messages_body, chips, len(past_b)),
        [half] * others,
        [VMEM] * (2 + len(past_b)),
        [VMEM] * others,
        moved=6 * mid * area,
    )(coef, state_b, *past_b)
    from_b = [rotate(messages[k - 1], "head", k) for k in range(1, chips)]

    own_b = within(False, high, logs, docs, query, own)
    other_a = within(True, low, logs_far, docs, query, send_low)
    other_b = within(True, high, logs_far, docs, query, send_high)

    def entering(which, first, past, arrived):
        return call(
            functools.partial(entering_body, chips, which, len(past)),
            [half] * 2,
            [VMEM] * (2 + len(past) + others),
            [VMEM] * 2,
            moved=8 * mid * area,
        )(coef, first, *past, *arrived)

    def finish(which, local, state):
        return call(
            functools.partial(finish_body, chips, cores, which),
            sds((mid,) + block[1:], BF16),
            [VMEM] * 5,
            VMEM,
            flops=rows * head_width * width // 2,
            moved=3 * rows * width,
        )(logs, query, *local, state)

    def last(which, local, state, finished, earlier):
        done = len(finished)
        return call(
            functools.partial(last_body, chips, cores, which, done),
            sds((rows, width), BF16),
            [VMEM] * (5 + done) + [ANY] * len(earlier),
            ANY,
            [
                pltpu.VMEM((mid,) + block[1:], BF16),
                pltpu.SemaphoreType.DMA((mid, per_block // 2)),
                pltpu.SemaphoreType.DMA((max(done, 1), mid)),
            ],
            flops=rows * head_width * width // 2,
            moved=4 * rows * width,
            aliases={5 + done: 0} if earlier else None,
        )(logs_far, query, *local, state, *finished, *earlier)

    keep_a, send_a = entering(0, first_a, past_a, from_x)
    far_a = rotate(send_a, "sub", 1)
    out_a = finish(0, own_a, keep_a)
    keep_b, send_b = entering(1, first_b, past_b, from_b)
    far_b = rotate(send_b, "sub", 1)
    out_b = finish(1, own_b, keep_b)
    out = last(0, other_a, far_a, (out_a, out_b), ())
    return last(1, other_b, far_b, (), (out,))


CUTS = 1
SLICE_ROOM = 21
PREPARE_ROOM = 24


def solution(mesh):
    rows = P(("groups", "seq", "head", "sub"), None)

    return jax.shard_map(
        per_device,
        mesh=mesh,
        in_specs=(
            rows,
            rows,
            rows,
            P(("head", "sub"), ("groups", "seq")),
            P(("head", "sub"), None),
            P("groups"),
        ),
        out_specs=rows,
        check_vma=False,
    )
```

```python
import functools

import jax
import jax.numpy as jnp
from jax import lax
from jax.experimental import pallas as pl
from jax.experimental.pallas import tpu as pltpu
from jax.sharding import PartitionSpec as P

BF16 = jnp.bfloat16
F32 = jnp.float32
ANY = pl.BlockSpec(memory_space=pl.ANY)
HBM = pl.BlockSpec(memory_space=pltpu.HBM)
VMEM = pl.BlockSpec(memory_space=pltpu.VMEM)
SMEM = pl.BlockSpec(memory_space=pltpu.SMEM)


def rotate(x, axis, step):
    size = lax.axis_size(axis)
    return lax.ppermute(x, axis, [(i, (i + step) % size) for i in range(size)])


def shift(x, axis, step):
    size = lax.axis_size(axis)
    return lax.ppermute(x, axis, [(i, i + step) for i in range(size - step)])


def fold(x):
    depth = lax.axis_size("seq")
    results = []
    for up in range(2):
        down = 1 - up
        pairs = []
        for z in range(depth):
            pairs.append((2 * z + up, 2 * (z + 1) + up if z < depth - 1 else 2 * z + down))
            pairs.append((2 * z + down, 2 * (z - 1) + down if z > 0 else 2 * z + up))
        results.append(lax.ppermute(x, ("seq", "sub"), pairs))
    return results


def of_core(refs, *index):
    if len(refs) == 1:
        return refs[0][index]
    return jnp.where(lax.axis_index("sub") == 0, refs[0][index], refs[1][index])


def column(row, rows):
    return jnp.broadcast_to(row, (rows, row.shape[1])).T


def call(body, out_shape, in_specs, out_specs, scratch=(), flops=0, moved=0, aliases=None, vmem=8 << 20):
    return pl.pallas_call(
        body,
        out_shape=out_shape,
        in_specs=in_specs,
        out_specs=out_specs,
        scratch_shapes=list(scratch),
        input_output_aliases=aliases or {},
        cost_estimate=pl.CostEstimate(flops=flops, bytes_accessed=moved, transcendentals=0),
        compiler_params=pltpu.CompilerParams(vmem_limit_bytes=vmem),
    )


def each(low, high, body):
    if high - low == 1:
        body(low)
    elif high > low:
        lax.fori_loop(low, high, lambda i, _: (body(i), 0)[1], 0)


def cols(place, c, width, count=1):
    start = (place * width[0] + c) * width[1]
    start = start if isinstance(start, int) else pl.multiple_of(start, width[1])
    return pl.ds(start, count * width[1])


def places(chips):
    base = 3 * chips
    return dict(to_start=base, to_end=base + 1, first=base + 2, row=base + 3, second=base + 4)


def pick(index, options):
    result = options[-1]
    for c in range(len(options) - 2, -1, -1):
        result = jnp.where(index == c, options[c], result)
    return result


def part(kv, n, block, here):
    return kv[0][n, block, :, here] if len(kv) == 1 else kv[n][block, :, here]


def states_of(chips, weight, coef, own, far, n, i, keep):
    cores = 2
    core, chip = lax.axis_index("sub"), lax.axis_index("head")
    per_block, rows = weight.shape[2:]
    for c in range(per_block):
        here = slice(c * rows, (c + 1) * rows)
        sums = []
        for ref, block, place in ((own, i, core), (far, n, 1 - core)):
            keys = part(ref, 0, block, here).T.astype(F32)
            keys = keys * weight[chip * cores + place, i, c : c + 1, :]
            values = part(ref, 1, block, here)
            sums.append(jnp.dot(keys.astype(BF16), values, preferred_element_type=F32))
        first = jnp.where(core == 0, sums[0], sums[1])
        last = jnp.where(core == 0, sums[1], sums[0])
        keep(c, first, last + coef[places(chips)["second"], i, c : c + 1, :] * first)


def tables(chips, cores, decays, docs, logs, coef, weight, stack):
    chip = lax.axis_index("head")
    pieces = chips * cores
    per_block, rows = logs.shape[2:]
    at = places(chips)
    for slot in range(chips):
        for piece in range(pieces):
            place = (slot * pieces + piece) * per_block
            stack[0, place : place + per_block] = decays[slot][:, piece * rows : (piece + 1) * rows]
    earlier = lax.broadcasted_iota(jnp.int32, (rows, rows), 0)
    later = lax.broadcasted_iota(jnp.int32, (rows, rows), 1)
    stack[1] = jnp.dot(
        stack[0],
        jnp.where(earlier <= later, 1.0, 0.0),
        precision=lax.Precision.HIGHEST,
        preferred_element_type=F32,
    )
    for slot in range(chips):
        block = lax.rem(chip - slot + chips, chips)
        logs[pieces, block] = decays[slot][:, pieces * rows :]
        factors = []
        for piece in range(pieces):
            place = (slot * pieces + piece) * per_block
            total = stack[1, place : place + per_block]
            logs[piece, block] = total
            end = jnp.broadcast_to(total[:, rows - 1 :], (per_block, rows))
            weight[piece, block] = jnp.exp(end - total) * docs[1, piece : piece + 1, :]
            passed = jnp.broadcast_to(docs[2, piece : piece + 1, rows - 1 :], (per_block, rows))
            factors.append(jnp.exp(end) * passed)
        through = []
        for c in range(chips):
            product = factors[c * cores]
            for u in range(1, cores):
                product = product * factors[c * cores + u]
            through.append(product)
        one, zero = jnp.ones_like(through[0]), jnp.zeros_like(through[0])

        def between(low, high):
            product = one
            for c in range(low, high):
                product = product * through[c]
            return product

        to_start = pick(chip, [between(0, c) for c in range(chips)])
        coef[at["to_start"], block] = to_start
        coef[at["to_end"], block] = pick(chip, [between(0, c + 1) for c in range(chips)])
        coef[at["first"], block] = pick(chip, [factors[c * cores] for c in range(chips)])
        coef[at["second"], block] = pick(chip, [factors[c * cores + 1] for c in range(chips)])
        coef[at["row"], block] = between(0, chips)
        for back in range(chips):
            source = lax.rem(chip - back + chips, chips)
            coef[back, block] = pick(source, [between(c + 1, chips) for c in range(chips)])
            before = pick(
                chip,
                [between(c - back + 1, c) if 0 <= c - back < c else zero for c in range(chips)],
            )
            coef[chips + back, block] = before
            coef[2 * chips + back, block] = jnp.where(
                (source < chip) & (back > 0), before, to_start
            )


def states_a_body(chips, cores, *refs):
    decays, (docs, own, *far) = refs[:chips], refs[chips : chips + 4]
    state_x, state_0, logs, coef, weight, stack = refs[chips + 4 :]
    tables(chips, cores, decays, docs, logs, coef, weight, stack)
    for i in range(chips // 2):

        def keep(c, first, state):
            state_0[i, c] = first
            state_x[i, c] = state.astype(BF16)

        states_of(chips, weight, coef, (own,), far, i, i, keep)


def states_b_body(chips, weight, coef, own, far, state_b, state_z, state_0):
    mid = chips // 2
    for n in range(mid):
        i = n + mid

        def keep(c, first, state):
            state_0[n, c] = first
            state_b[n, c] = state.astype(BF16)
            state_z[n, c] = (coef[0, i, c : c + 1, :] * state).astype(BF16)

        states_of(chips, weight, coef, (own,), (far,), n, i, keep)


def within_body(cores, far, blocks, logs, docs, q, *refs):
    kv, (out, carry) = refs[:-2], refs[-2:]
    core = lax.axis_index("sub")
    piece = lax.axis_index("head") * cores + core
    core = 1 - core if far else core
    per_block, rows = logs.shape[2], logs.shape[3]
    docs_here = jnp.broadcast_to(docs[0, pl.ds(piece, 1), :], (rows, rows))
    t = lax.broadcasted_iota(jnp.int32, (rows, rows), 0)
    s = lax.broadcasted_iota(jnp.int32, (rows, rows), 1)
    linked = (docs_here.T == docs_here) & (t >= s)
    carries = column(docs[2, pl.ds(piece, 1), :], rows)
    shift_ = blocks[0] if far else 0

    def heads_of(i):
        for c in range(per_block):
            here = slice(c * rows, (c + 1) * rows)
            row = logs[piece, i, c : c + 1, :]
            down = column(row, rows)
            damping = jnp.exp(jnp.where(linked, down - row, -1e30))
            scores = lax.dot_general(
                q[:, cols(i * cores + core, c, (per_block, rows))],
                part(kv, 0, i - shift_, here),
                (((1,), (1,)), ((), ())),
                preferred_element_type=F32,
            )
            out[i - blocks[0], :, here] = jnp.dot(
                (scores * damping).astype(BF16), part(kv, 1, i - shift_, here), preferred_element_type=F32
            )
            carry[i - blocks[0], :, here] = jnp.exp(down) * carries

    each(*blocks, heads_of)


def row_total_body(chips, coef, state_x, *refs):
    from_x, total = refs[:-1], refs[-1]

    def join(i):
        for c in range(state_x.shape[1]):
            sum_ = coef[0, i, c : c + 1, :] * state_x[i, c].astype(F32)
            for back in range(1, chips):
                sum_ = sum_ + coef[back, i, c : c + 1, :] * from_x[back - 1][i, c].astype(F32)
            total[i, c] = sum_.astype(BF16)

    each(0, chips // 2, join)


def messages_body(chips, parts, coef, state_b, *refs):
    past_b, messages = refs[:parts], refs[parts:]
    chip = lax.axis_index("head")
    mid = chips // 2

    def join(i):
        for c in range(state_b.shape[1]):
            past = of_core(past_b, i, c)
            factor = coef[places(chips)["to_end"], i + mid, c : c + 1, :]
            ahead = (state_b[i, c].astype(F32) + factor * past.astype(F32)).astype(BF16)
            for back in range(1, chips):
                messages[back - 1][i, c] = jnp.where(chip + back < chips, ahead, past)

    each(0, mid, join)


def entering_body(chips, half, parts, coef, first, *refs):
    past, others = refs[:parts], refs[parts:-2]
    keep, send = refs[-2:]
    is_first = lax.axis_index("sub") == 0
    at = places(chips)
    mid = chips // 2
    base = (1 + half) * chips

    def join(i):
        for c in range(keep.shape[1]):

            def factor(place):
                return coef[place, i + half * mid, c : c + 1, :]

            entering = factor(at["to_start"]) * of_core(past, i, c).astype(F32)
            for back in range(1, chips):
                entering = entering + factor(base + back) * others[back - 1][i, c].astype(F32)
            later = first[i, c] + factor(at["first"]) * entering
            keep[i, c] = jnp.where(is_first, entering, later).astype(BF16)
            send[i, c] = jnp.where(is_first, later, entering).astype(BF16)

    each(0, mid, join)


def finish_heads(chips, cores, far, half, logs, q, within, carry, state, n, put):
    core = lax.axis_index("sub")
    core = 1 - core if far else core
    i = n + half * (chips // 2)
    per_block, rows = logs.shape[2:]
    gain = logs[chips * cores, i]
    for c in range(per_block):
        here = slice(c * rows, (c + 1) * rows)
        result = within[n, :, here] + carry[n, :, here] * jnp.dot(
            q[:, cols(i * cores + core, c, (per_block, rows))],
            state[n, c],
            preferred_element_type=F32,
        )
        mean_square = jnp.mean(result * result, axis=1, keepdims=True)
        put(here, (result * lax.rsqrt(mean_square + 1e-06) * gain[c : c + 1, :]).astype(BF16))


def finish_body(chips, cores, far, half, logs, q, within, carry, state, out):

    def block(n):
        def put(here, value):
            out[n, :, here] = value

        finish_heads(chips, cores, far, half, logs, q, within, carry, state, n, put)

    each(0, chips // 2, block)


def last_body(chips, cores, logs, q, within, carry, state, *refs):
    finished = refs[:3]
    out, buffer, sem, done_sem = refs[3:]
    core = lax.axis_index("sub")
    mid = chips // 2
    half = 1
    rows, width = buffer.shape[1:]

    def copy(source, i, place, sem):
        target = out.at[:, cols(i * cores + place, 0, (1, width))]
        return pltpu.make_async_copy(source, target, sem)

    copies = []
    for k, (which, place) in enumerate(((0, core), (1, core), (0, 1 - core))):
        for n in range(mid):
            copies.append(copy(finished[k].at[n], n + which * mid, place, done_sem.at[k, n]))
            copies[-1].start()
    for n in range(mid):

        def put(here, value):
            buffer[n, :, here] = value
            c = here.stop // rows - 1
            if c % 2 == 1:
                pair = slice(here.stop - 2 * rows, here.stop)
                place = cols((n + half * mid) * cores + 1 - core, c - 1, (width // rows, rows), 2)
                copies.append(
                    pltpu.make_async_copy(
                        buffer.at[n, :, pair], out.at[:, place], sem.at[n, c // 2]
                    )
                )
                copies[-1].start()

        finish_heads(chips, cores, True, half, logs, q, within, carry, state, n, put)
    for one in copies:
        one.wait()


def block_copies(cores, core, blocks, sources, targets, sems):
    rows, width = targets[0].shape[-2:]
    parts = sems.shape[2]
    rows = rows // parts
    return [
        pltpu.make_async_copy(
            source.at[cut * rows : (cut + 1) * rows, cols(i * cores + core, 0, (1, width))],
            targets[n].at[i - blocks[0], cut * rows : (cut + 1) * rows],
            sems.at[n, i - blocks[0], cut],
        )
        for n, source in enumerate(sources)
        for i in range(*blocks)
        for cut in range(parts)
    ]


def slice_body(chips, cores, k_all, v_all, k, v, sems):
    core = 1 - lax.axis_index("sub")
    copies = block_copies(cores, core, (0, chips // 2), (k_all, v_all), (k, v), sems)
    for copy in copies:
        copy.start()
    for copy in copies:
        copy.wait()


def pack_body(log_decay, gain, packed):
    packed[:, : log_decay.shape[1]] = log_decay[...]
    packed[:, log_decay.shape[1] :] = gain[...]


def prepare_body(chips, cores, lengths_all, k_all, v_all, send, own, docs, *scratch):
    lengths, send_sems, own_sems, length_sem = scratch
    core = lax.axis_index("sub")
    both = (k_all, v_all)
    copies = block_copies(cores, 1 - core, (chips // 2, chips), both, (send.at[0], send.at[1]), send_sems)
    copies += block_copies(cores, core, (0, chips), both, (own.at[0], own.at[1]), own_sems)
    lengths_copy = pltpu.make_async_copy(lengths_all, lengths, length_sem)
    lengths_copy.start()
    for copy in copies:
        copy.start()
    lengths_copy.wait()
    pieces, rows = docs.shape[1:]
    piece = lax.broadcasted_iota(jnp.int32, (pieces, rows), 0)
    lane = lax.broadcasted_iota(jnp.int32, (pieces, rows), 1)
    first = (lax.axis_index("seq") * pieces + piece) * rows
    here, before = jnp.zeros((pieces, rows), F32), jnp.zeros((pieces, rows), F32)
    start = 0
    for n in range(lengths.shape[0]):
        here += jnp.where(start <= first + lane, 1.0, 0.0)
        before += jnp.where(start < first, 1.0, 0.0)
        start = start + lengths[n]
    end = jnp.broadcast_to(here[:, rows - 1 :], (pieces, rows))
    docs[0] = here
    docs[1] = jnp.where(here == end, 1.0, 0.0)
    docs[2] = jnp.where(here == before, 1.0, 0.0)
    for copy in copies:
        copy.wait()


def earlier_rows(value, row_factor, blocks, reach):
    if reach == 1:
        return fold(value)
    total, step = value, 1
    factor = row_factor[blocks] if reach > 1 else None
    while step < reach:
        before = shift(total, "seq", step).astype(F32)
        total = (total.astype(F32) + factor[:, :, None, :] * before).astype(BF16)
        factor = factor * shift(factor, "seq", step)
        step *= 2
    return [shift(total, "seq", 1)]


def per_device(query, key, value, log_decay, gain, doc_lengths):
    rows, width = query.shape
    per_block, row_tokens = log_decay.shape
    head_width = gain.shape[1]
    chips, cores, depth = lax.axis_size("head"), lax.axis_size("sub"), lax.axis_size("seq")
    assert cores == 2 and chips % 2 == 0 and rows == head_width
    pieces = chips * cores
    others = chips - 1
    mid = chips // 2
    reach = max(1, -(-depth // 4))

    def sds(shape, kind):
        return jax.ShapeDtypeStruct(shape, kind)

    square = (per_block, head_width, head_width)
    area = per_block * head_width * head_width
    block = (chips, rows, per_block * head_width)
    half = sds((mid,) + square, BF16)
    half_wide = sds((mid,) + square, F32)
    log_shape = (pieces + 1, chips, per_block, rows)
    coef_shape = (3 * chips + 5, chips, per_block, rows)

    half_kv = sds((2, mid) + block[1:], BF16)
    send_low = call(
        functools.partial(slice_body, chips, cores),
        [sds((mid,) + block[1:], BF16)] * 2,
        [HBM] * 2,
        [VMEM] * 2,
        [pltpu.SemaphoreType.DMA((2, mid, CUTS))],
        moved=4 * rows * width,
        vmem=67043328 - SLICE_ROOM * rows * width,
    )(key, value)
    far_k = rotate(send_low[0], "sub", 1)
    far_v = rotate(send_low[1], "sub", 1)
    packed = call(
        pack_body,
        sds((per_block, row_tokens + head_width), F32),
        [VMEM] * 2,
        VMEM,
    )(log_decay, gain)
    decays = [packed] + [rotate(packed, "head", k) for k in range(1, chips)]
    send_high, own, docs = call(
        functools.partial(prepare_body, chips, cores),
        [half_kv, sds((2,) + block, BF16), sds((3, pieces, rows), F32)],
        [HBM] * 3,
        [VMEM] * 3,
        [
            pltpu.SMEM(doc_lengths.shape, jnp.int32),
            pltpu.SemaphoreType.DMA((2, mid, CUTS)),
            pltpu.SemaphoreType.DMA((2, chips, CUTS)),
            pltpu.SemaphoreType.DMA(()),
        ],
        moved=12 * rows * width,
        vmem=67043328 - PREPARE_ROOM * rows * width,
    )(doc_lengths, key, value)
    far_high = rotate(send_high, "sub", 1)

    state_x, first_a, logs, coef, weight = call(
        functools.partial(states_a_body, chips, cores),
        [half, half_wide]
        + [sds(log_shape, F32), sds(coef_shape, F32), sds((pieces,) + log_shape[1:], F32)],
        [VMEM] * (chips + 4),
        [VMEM] * 5,
        [pltpu.VMEM((2, chips * pieces * per_block, rows), F32)],
        flops=2 * rows * chips * area,
        moved=8 * chips * area,
    )(*decays, docs, own, far_k, far_v)
    from_x = [rotate(state_x, "head", k) for k in range(1, chips)]
    state_b, state_z, first_b = call(
        functools.partial(states_b_body, chips),
        [half, half, half_wide],
        [VMEM] * 4,
        [VMEM] * 3,
        flops=2 * rows * chips * area,
        moved=8 * chips * area,
    )(weight, coef, own, far_high)
    row_factor = coef[places(chips)["row"]] if reach > 1 else None
    past_b = earlier_rows(state_z, row_factor, slice(mid, chips), reach)
    logs_far = rotate(logs, "sub", 1)

    def within(far, blocks, *args):
        return call(
            functools.partial(within_body, cores, far, blocks),
            [sds((mid,) + block[1:], F32)] * 2,
            [VMEM] * len(args),
            [VMEM] * 2,
            flops=rows * rows * width,
            moved=4 * rows * width,
        )(*args)

    low, high = (0, mid), (mid, chips)
    own_a = within(False, low, logs, docs, query, own)

    total = call(
        functools.partial(row_total_body, chips),
        half,
        [VMEM] * (2 + others),
        VMEM,
        moved=6 * mid * area,
    )(coef, state_x, *from_x)
    past_a = earlier_rows(total, row_factor, slice(0, mid), reach)

    messages = call(
        functools.partial(messages_body, chips, len(past_b)),
        [half] * others,
        [VMEM] * (2 + len(past_b)),
        [VMEM] * others,
        moved=6 * mid * area,
    )(coef, state_b, *past_b)
    from_b = [rotate(messages[k - 1], "head", k) for k in range(1, chips)]

    own_b = within(False, high, logs, docs, query, own)
    other_a = within(True, low, logs_far, docs, query, *send_low)
    other_b = within(True, high, logs_far, docs, query, send_high)

    def entering(which, first, past, arrived):
        return call(
            functools.partial(entering_body, chips, which, len(past)),
            [half] * 2,
            [VMEM] * (2 + len(past) + others),
            [VMEM] * 2,
            moved=8 * mid * area,
        )(coef, first, *past, *arrived)

    def finish(far, which, logs_used, local, state):
        return call(
            functools.partial(finish_body, chips, cores, far, which),
            sds((mid,) + block[1:], BF16),
            [VMEM] * 5,
            VMEM,
            flops=rows * head_width * width // 2,
            moved=3 * rows * width,
        )(logs_used, query, *local, state)

    keep_a, send_a = entering(0, first_a, past_a, from_x)
    far_a = rotate(send_a, "sub", 1)
    out_a = finish(False, 0, logs, own_a, keep_a)
    keep_b, send_b = entering(1, first_b, past_b, from_b)
    far_b = rotate(send_b, "sub", 1)
    out_b = finish(False, 1, logs, own_b, keep_b)
    out_far = finish(True, 0, logs_far, other_a, far_a)
    return call(
        functools.partial(last_body, chips, cores),
        sds((rows, width), BF16),
        [VMEM] * 8,
        ANY,
        [
            pltpu.VMEM((mid,) + block[1:], BF16),
            pltpu.SemaphoreType.DMA((mid, per_block // 2)),
            pltpu.SemaphoreType.DMA((3, mid)),
        ],
        flops=rows * head_width * width // 2,
        moved=4 * rows * width,
    )(logs_far, query, *other_b, far_b, out_a, out_b, out_far)


CUTS = 1
SLICE_ROOM = 21
PREPARE_ROOM = 24


def solution(mesh):
    rows = P(("groups", "seq", "head", "sub"), None)

    return jax.shard_map(
        per_device,
        mesh=mesh,
        in_specs=(
            rows,
            rows,
            rows,
            P(("head", "sub"), ("groups", "seq")),
            P(("head", "sub"), None),
            P("groups"),
        ),
        out_specs=rows,
        check_vma=False,
    )
```

```python
import functools

import jax
import jax.numpy as jnp
from jax import lax
from jax.experimental import pallas as pl
from jax.experimental.pallas import tpu as pltpu
from jax.sharding import PartitionSpec as P

BF16 = jnp.bfloat16
F32 = jnp.float32
ANY = pl.BlockSpec(memory_space=pl.ANY)
HBM = pl.BlockSpec(memory_space=pltpu.HBM)
VMEM = pl.BlockSpec(memory_space=pltpu.VMEM)
SMEM = pl.BlockSpec(memory_space=pltpu.SMEM)


def rotate(x, axis, step):
    size = lax.axis_size(axis)
    return lax.ppermute(x, axis, [(i, (i + step) % size) for i in range(size)])


def shift(x, axis, step):
    size = lax.axis_size(axis)
    return lax.ppermute(x, axis, [(i, i + step) for i in range(size - step)])


def fold(x):
    depth = lax.axis_size("seq")
    results = []
    for up in range(2):
        down = 1 - up
        pairs = []
        for z in range(depth):
            pairs.append((2 * z + up, 2 * (z + 1) + up if z < depth - 1 else 2 * z + down))
            pairs.append((2 * z + down, 2 * (z - 1) + down if z > 0 else 2 * z + up))
        results.append(lax.ppermute(x, ("seq", "sub"), pairs))
    return results


def of_core(refs, *index):
    if len(refs) == 1:
        return refs[0][index]
    return jnp.where(lax.axis_index("sub") == 0, refs[0][index], refs[1][index])


def column(row, rows):
    return jnp.broadcast_to(row, (rows, row.shape[1])).T


def call(body, out_shape, in_specs, out_specs, scratch=(), flops=0, moved=0, aliases=None, vmem=8 << 20):
    return pl.pallas_call(
        body,
        out_shape=out_shape,
        in_specs=in_specs,
        out_specs=out_specs,
        scratch_shapes=list(scratch),
        input_output_aliases=aliases or {},
        cost_estimate=pl.CostEstimate(flops=flops, bytes_accessed=moved, transcendentals=0),
        compiler_params=pltpu.CompilerParams(vmem_limit_bytes=vmem),
    )


def each(low, high, body):
    if high - low == 1:
        body(low)
    elif high > low:
        lax.fori_loop(low, high, lambda i, _: (body(i), 0)[1], 0)


def cols(place, c, width, count=1):
    start = (place * width[0] + c) * width[1]
    start = start if isinstance(start, int) else pl.multiple_of(start, width[1])
    return pl.ds(start, count * width[1])


def places(chips):
    base = 3 * chips
    return dict(to_start=base, to_end=base + 1, first=base + 2, row=base + 3, second=base + 4)


def pick(index, options):
    result = options[-1]
    for c in range(len(options) - 2, -1, -1):
        result = jnp.where(index == c, options[c], result)
    return result


def states_of(chips, weight, coef, own, far, n, i, keep):
    cores = 2
    core, chip = lax.axis_index("sub"), lax.axis_index("head")
    per_block, rows = weight.shape[2:]
    for c in range(per_block):
        here = slice(c * rows, (c + 1) * rows)
        sums = []
        for ref, block, place in ((own, i, core), (far, n, 1 - core)):
            keys = ref[0, block, :, here].T.astype(F32)
            keys = keys * weight[chip * cores + place, i, c : c + 1, :]
            values = ref[1, block, :, here]
            sums.append(jnp.dot(keys.astype(BF16), values, preferred_element_type=F32))
        first = jnp.where(core == 0, sums[0], sums[1])
        last = jnp.where(core == 0, sums[1], sums[0])
        keep(c, first, last + coef[places(chips)["second"], i, c : c + 1, :] * first)


def tables(chips, cores, decays, docs, logs, coef, weight, stack):
    chip = lax.axis_index("head")
    pieces = chips * cores
    per_block, rows = logs.shape[2:]
    at = places(chips)
    for slot in range(chips):
        for piece in range(pieces):
            place = (slot * pieces + piece) * per_block
            stack[0, place : place + per_block] = decays[slot][:, piece * rows : (piece + 1) * rows]
    earlier = lax.broadcasted_iota(jnp.int32, (rows, rows), 0)
    later = lax.broadcasted_iota(jnp.int32, (rows, rows), 1)
    stack[1] = jnp.dot(
        stack[0],
        jnp.where(earlier <= later, 1.0, 0.0),
        precision=lax.Precision.HIGHEST,
        preferred_element_type=F32,
    )
    for slot in range(chips):
        block = lax.rem(chip - slot + chips, chips)
        logs[pieces, block] = decays[slot][:, pieces * rows :]
        factors = []
        for piece in range(pieces):
            place = (slot * pieces + piece) * per_block
            total = stack[1, place : place + per_block]
            logs[piece, block] = total
            end = jnp.broadcast_to(total[:, rows - 1 :], (per_block, rows))
            weight[piece, block] = jnp.exp(end - total) * docs[1, piece : piece + 1, :]
            passed = jnp.broadcast_to(docs[2, piece : piece + 1, rows - 1 :], (per_block, rows))
            factors.append(jnp.exp(end) * passed)
        through = []
        for c in range(chips):
            product = factors[c * cores]
            for u in range(1, cores):
                product = product * factors[c * cores + u]
            through.append(product)
        one, zero = jnp.ones_like(through[0]), jnp.zeros_like(through[0])

        def between(low, high):
            product = one
            for c in range(low, high):
                product = product * through[c]
            return product

        to_start = pick(chip, [between(0, c) for c in range(chips)])
        coef[at["to_start"], block] = to_start
        coef[at["to_end"], block] = pick(chip, [between(0, c + 1) for c in range(chips)])
        coef[at["first"], block] = pick(chip, [factors[c * cores] for c in range(chips)])
        coef[at["second"], block] = pick(chip, [factors[c * cores + 1] for c in range(chips)])
        coef[at["row"], block] = between(0, chips)
        for back in range(chips):
            source = lax.rem(chip - back + chips, chips)
            coef[back, block] = pick(source, [between(c + 1, chips) for c in range(chips)])
            before = pick(
                chip,
                [between(c - back + 1, c) if 0 <= c - back < c else zero for c in range(chips)],
            )
            coef[chips + back, block] = before
            coef[2 * chips + back, block] = jnp.where(
                (source < chip) & (back > 0), before, to_start
            )


def states_a_body(chips, cores, *refs):
    decays, (docs, own, far) = refs[:chips], refs[chips : chips + 3]
    state_x, state_0, logs, coef, weight, stack = refs[chips + 3 :]
    tables(chips, cores, decays, docs, logs, coef, weight, stack)
    for i in range(chips // 2):

        def keep(c, first, state):
            state_0[i, c] = first
            state_x[i, c] = state.astype(BF16)

        states_of(chips, weight, coef, own, far, i, i, keep)


def states_b_body(chips, weight, coef, own, far, state_b, state_z, state_0):
    mid = chips // 2
    for n in range(mid):
        i = n + mid

        def keep(c, first, state):
            state_0[n, c] = first
            state_b[n, c] = state.astype(BF16)
            state_z[n, c] = (coef[0, i, c : c + 1, :] * state).astype(BF16)

        states_of(chips, weight, coef, own, far, n, i, keep)


def within_body(cores, far, blocks, logs, docs, q, kv, out, carry):
    core = lax.axis_index("sub")
    piece = lax.axis_index("head") * cores + core
    core = 1 - core if far else core
    per_block, rows = logs.shape[2], logs.shape[3]
    docs_here = jnp.broadcast_to(docs[0, pl.ds(piece, 1), :], (rows, rows))
    t = lax.broadcasted_iota(jnp.int32, (rows, rows), 0)
    s = lax.broadcasted_iota(jnp.int32, (rows, rows), 1)
    linked = (docs_here.T == docs_here) & (t >= s)
    carries = column(docs[2, pl.ds(piece, 1), :], rows)
    shift_ = blocks[0] if far else 0

    def heads_of(i):
        for c in range(per_block):
            here = slice(c * rows, (c + 1) * rows)
            row = logs[piece, i, c : c + 1, :]
            down = column(row, rows)
            damping = jnp.exp(jnp.where(linked, down - row, -1e30))
            scores = lax.dot_general(
                q[:, cols(i * cores + core, c, (per_block, rows))],
                kv[0, i - shift_, :, here],
                (((1,), (1,)), ((), ())),
                preferred_element_type=F32,
            )
            out[i - blocks[0], :, here] = jnp.dot(
                (scores * damping).astype(BF16), kv[1, i - shift_, :, here], preferred_element_type=F32
            )
            carry[i - blocks[0], :, here] = jnp.exp(down) * carries

    each(*blocks, heads_of)


def row_total_body(chips, coef, state_x, *refs):
    from_x, total = refs[:-1], refs[-1]

    def join(i):
        for c in range(state_x.shape[1]):
            sum_ = coef[0, i, c : c + 1, :] * state_x[i, c].astype(F32)
            for back in range(1, chips):
                sum_ = sum_ + coef[back, i, c : c + 1, :] * from_x[back - 1][i, c].astype(F32)
            total[i, c] = sum_.astype(BF16)

    each(0, chips // 2, join)


def messages_body(chips, parts, coef, state_b, *refs):
    past_b, messages = refs[:parts], refs[parts:]
    chip = lax.axis_index("head")
    mid = chips // 2

    def join(i):
        for c in range(state_b.shape[1]):
            past = of_core(past_b, i, c)
            factor = coef[places(chips)["to_end"], i + mid, c : c + 1, :]
            ahead = (state_b[i, c].astype(F32) + factor * past.astype(F32)).astype(BF16)
            for back in range(1, chips):
                messages[back - 1][i, c] = jnp.where(chip + back < chips, ahead, past)

    each(0, mid, join)


def entering_body(chips, half, parts, start, coef, first, *refs):
    past, others = refs[:parts], refs[parts:-2]
    keep, send = refs[-2:]
    is_first = lax.axis_index("sub") == 0
    at = places(chips)
    mid = chips // 2
    base = (1 + half) * chips

    def join(i):
        for n in range(keep.shape[1]):
            c = n + start

            def factor(place):
                return coef[place, i + half * mid, c : c + 1, :]

            entering = factor(at["to_start"]) * of_core(past, i, c).astype(F32)
            for back in range(1, chips):
                entering = entering + factor(base + back) * others[back - 1][i, c].astype(F32)
            later = first[i, c] + factor(at["first"]) * entering
            keep[i, n] = jnp.where(is_first, entering, later).astype(BF16)
            send[i, n] = jnp.where(is_first, later, entering).astype(BF16)

    each(0, mid, join)


def finish_heads(chips, cores, far, half, start, logs, q, within, carry, state, n, put):
    core = lax.axis_index("sub")
    core = 1 - core if far else core
    i = n + half * (chips // 2)
    per_block, rows = logs.shape[2:]
    gain = logs[chips * cores, i]
    for k in range(state.shape[1]):
        c = start + k
        here = slice(c * rows, (c + 1) * rows)
        result = within[n, :, here] + carry[n, :, here] * jnp.dot(
            q[:, cols(i * cores + core, c, (per_block, rows))],
            state[n, k],
            preferred_element_type=F32,
        )
        mean_square = jnp.mean(result * result, axis=1, keepdims=True)
        put(k, (result * lax.rsqrt(mean_square + 1e-06) * gain[c : c + 1, :]).astype(BF16))


def finish_body(chips, cores, far, half, start, logs, q, within, carry, state, out):
    rows = q.shape[0]

    def block(n):
        def put(k, value):
            out[n, :, k * rows : (k + 1) * rows] = value

        finish_heads(chips, cores, far, half, start, logs, q, within, carry, state, n, put)

    each(0, chips // 2, block)


def last_body(chips, cores, start, finished, logs, q, within, carry, state, *refs):
    done = refs[: len(finished)]
    out, buffer, sem, done_sem = refs[len(finished) :]
    core = lax.axis_index("sub")
    mid = chips // 2
    per_block, rows = logs.shape[2:]

    def target(far, half, n, c, count):
        block = (n + half * mid) * cores + (1 - core if far else core)
        return out.at[:, cols(block, c, (per_block, rows), count)]

    copies = []
    for k, (far, half, first) in enumerate(finished):
        for n in range(mid):
            place = target(far, half, n, first, done[k].shape[2] // rows)
            copies.append(pltpu.make_async_copy(done[k].at[n], place, done_sem.at[k, n]))
            copies[-1].start()
    for n in range(mid):

        def put(k, value):
            buffer[n, :, k * rows : (k + 1) * rows] = value
            if k % 2 == 1:
                source = buffer.at[n, :, (k - 1) * rows : (k + 1) * rows]
                place = target(True, 1, n, start + k - 1, 2)
                copies.append(pltpu.make_async_copy(source, place, sem.at[n, k // 2]))
                copies[-1].start()

        finish_heads(chips, cores, True, 1, start, logs, q, within, carry, state, n, put)
    for one in copies:
        one.wait()


def block_copies(cores, core, blocks, sources, target, sems):
    width = target.shape[3]
    parts = sems.shape[2]
    rows = target.shape[2] // parts
    return [
        pltpu.make_async_copy(
            source.at[part * rows : (part + 1) * rows, cols(i * cores + core, 0, (1, width))],
            target.at[n, i - blocks[0], part * rows : (part + 1) * rows],
            sems.at[n, i - blocks[0], part],
        )
        for n, source in enumerate(sources)
        for i in range(*blocks)
        for part in range(parts)
    ]


def slice_body(chips, cores, k_all, v_all, send, sems):
    core = 1 - lax.axis_index("sub")
    copies = block_copies(cores, core, (0, chips // 2), (k_all, v_all), send, sems)
    for copy in copies:
        copy.start()
    for copy in copies:
        copy.wait()


def pack_body(log_decay, gain, packed):
    packed[:, : log_decay.shape[1]] = log_decay[...]
    packed[:, log_decay.shape[1] :] = gain[...]


def prepare_body(chips, cores, lengths_all, k_all, v_all, send, own, docs, *scratch):
    lengths, send_sems, own_sems, length_sem = scratch
    core = lax.axis_index("sub")
    both = (k_all, v_all)
    copies = block_copies(cores, 1 - core, (chips // 2, chips), both, send, send_sems)
    copies += block_copies(cores, core, (0, chips), both, own, own_sems)
    lengths_copy = pltpu.make_async_copy(lengths_all, lengths, length_sem)
    lengths_copy.start()
    for copy in copies:
        copy.start()
    lengths_copy.wait()
    pieces, rows = docs.shape[1:]
    piece = lax.broadcasted_iota(jnp.int32, (pieces, rows), 0)
    lane = lax.broadcasted_iota(jnp.int32, (pieces, rows), 1)
    first = (lax.axis_index("seq") * pieces + piece) * rows
    here, before = jnp.zeros((pieces, rows), F32), jnp.zeros((pieces, rows), F32)
    start = 0
    for n in range(lengths.shape[0]):
        here += jnp.where(start <= first + lane, 1.0, 0.0)
        before += jnp.where(start < first, 1.0, 0.0)
        start = start + lengths[n]
    end = jnp.broadcast_to(here[:, rows - 1 :], (pieces, rows))
    docs[0] = here
    docs[1] = jnp.where(here == end, 1.0, 0.0)
    docs[2] = jnp.where(here == before, 1.0, 0.0)
    for copy in copies:
        copy.wait()


def earlier_rows(value, row_factor, blocks, reach):
    if reach == 1:
        return fold(value)
    total, step = value, 1
    factor = row_factor[blocks] if reach > 1 else None
    while step < reach:
        before = shift(total, "seq", step).astype(F32)
        total = (total.astype(F32) + factor[:, :, None, :] * before).astype(BF16)
        factor = factor * shift(factor, "seq", step)
        step *= 2
    return [shift(total, "seq", 1)]


def per_device(query, key, value, log_decay, gain, doc_lengths):
    rows, width = query.shape
    per_block, row_tokens = log_decay.shape
    head_width = gain.shape[1]
    chips, cores, depth = lax.axis_size("head"), lax.axis_size("sub"), lax.axis_size("seq")
    assert cores == 2 and chips % 2 == 0 and rows == head_width
    pieces = chips * cores
    others = chips - 1
    mid = chips // 2
    reach = max(1, -(-depth // 4))

    def sds(shape, kind):
        return jax.ShapeDtypeStruct(shape, kind)

    square = (per_block, head_width, head_width)
    area = per_block * head_width * head_width
    block = (chips, rows, per_block * head_width)
    half = sds((mid,) + square, BF16)
    half_wide = sds((mid,) + square, F32)
    log_shape = (pieces + 1, chips, per_block, rows)
    coef_shape = (3 * chips + 5, chips, per_block, rows)

    half_kv = sds((2, mid) + block[1:], BF16)
    send_low = call(
        functools.partial(slice_body, chips, cores),
        half_kv,
        [HBM] * 2,
        VMEM,
        [pltpu.SemaphoreType.DMA((2, mid, CUTS))],
        moved=4 * rows * width,
        vmem=67043328 - SLICE_ROOM * rows * width,
    )(key, value)
    far_low = rotate(send_low, "sub", 1)
    packed = call(
        pack_body,
        sds((per_block, row_tokens + head_width), F32),
        [VMEM] * 2,
        VMEM,
    )(log_decay, gain)
    decays = [packed] + [rotate(packed, "head", k) for k in range(1, chips)]
    send_high, own, docs = call(
        functools.partial(prepare_body, chips, cores),
        [half_kv, sds((2,) + block, BF16), sds((3, pieces, rows), F32)],
        [HBM] * 3,
        [VMEM] * 3,
        [
            pltpu.SMEM(doc_lengths.shape, jnp.int32),
            pltpu.SemaphoreType.DMA((2, mid, CUTS)),
            pltpu.SemaphoreType.DMA((2, chips, CUTS)),
            pltpu.SemaphoreType.DMA(()),
        ],
        moved=12 * rows * width,
        vmem=67043328 - PREPARE_ROOM * rows * width,
    )(doc_lengths, key, value)
    far_high = rotate(send_high, "sub", 1)

    state_x, first_a, logs, coef, weight = call(
        functools.partial(states_a_body, chips, cores),
        [half, half_wide]
        + [sds(log_shape, F32), sds(coef_shape, F32), sds((pieces,) + log_shape[1:], F32)],
        [VMEM] * (chips + 3),
        [VMEM] * 5,
        [pltpu.VMEM((2, chips * pieces * per_block, rows), F32)],
        flops=2 * rows * chips * area,
        moved=8 * chips * area,
    )(*decays, docs, own, far_low)
    from_x = [rotate(state_x, "head", k) for k in range(1, chips)]
    state_b, state_z, first_b = call(
        functools.partial(states_b_body, chips),
        [half, half, half_wide],
        [VMEM] * 4,
        [VMEM] * 3,
        flops=2 * rows * chips * area,
        moved=8 * chips * area,
    )(weight, coef, own, far_high)
    row_factor = coef[places(chips)["row"]] if reach > 1 else None
    past_b = earlier_rows(state_z, row_factor, slice(mid, chips), reach)
    logs_far = rotate(logs, "sub", 1)

    def within(far, blocks, *args):
        return call(
            functools.partial(within_body, cores, far, blocks),
            [sds((mid,) + block[1:], F32)] * 2,
            [VMEM] * 4,
            [VMEM] * 2,
            flops=rows * rows * width,
            moved=4 * rows * width,
        )(*args)

    low, high = (0, mid), (mid, chips)
    own_a = within(False, low, logs, docs, query, own)

    total = call(
        functools.partial(row_total_body, chips),
        half,
        [VMEM] * (2 + others),
        VMEM,
        moved=6 * mid * area,
    )(coef, state_x, *from_x)
    past_a = earlier_rows(total, row_factor, slice(0, mid), reach)

    messages = call(
        functools.partial(messages_body, chips, len(past_b)),
        [half] * others,
        [VMEM] * (2 + len(past_b)),
        [VMEM] * others,
        moved=6 * mid * area,
    )(coef, state_b, *past_b)
    from_b = [rotate(messages[k - 1], "head", k) for k in range(1, chips)]

    own_b = within(False, high, logs, docs, query, own)
    other_a = within(True, low, logs_far, docs, query, send_low)
    other_b = within(True, high, logs_far, docs, query, send_high)

    def entering(which, start, count, first, past, arrived):
        return call(
            functools.partial(entering_body, chips, which, len(past), start),
            [sds((mid, count) + square[1:], BF16)] * 2,
            [VMEM] * (2 + len(past) + others),
            [VMEM] * 2,
            moved=count * mid * area,
        )(coef, first, *past, *arrived)

    def finish(far, which, start, logs_used, local, state):
        return call(
            functools.partial(finish_body, chips, cores, far, which, start),
            sds((mid, rows, state.shape[1] * rows), BF16),
            [VMEM] * 5,
            VMEM,
            flops=rows * head_width * width // 2,
            moved=3 * rows * width,
        )(logs_used, query, *local, state)

    pair = per_block // 2
    keep_a, send_a = entering(0, 0, per_block, first_a, past_a, from_x)
    far_a = rotate(send_a, "sub", 1)
    keep_b, send_b = entering(1, 0, pair, first_b, past_b, from_b)
    far_b = rotate(send_b, "sub", 1)
    keep_c, send_c = entering(1, pair, pair, first_b, past_b, from_b)
    far_c = rotate(send_c, "sub", 1)
    out_a = finish(False, 0, 0, logs, own_a, keep_a)
    out_b = finish(False, 1, 0, logs, own_b, keep_b)
    out_c = finish(False, 1, pair, logs, own_b, keep_c)
    out_d = finish(True, 0, 0, logs_far, other_a, far_a)
    out_e = finish(True, 1, 0, logs_far, other_b, far_b)
    finished = (
        (False, 0, 0),
        (False, 1, 0),
        (False, 1, pair),
        (True, 0, 0),
        (True, 1, 0),
    )
    return call(
        functools.partial(last_body, chips, cores, pair, finished),
        sds((rows, width), BF16),
        [VMEM] * (5 + len(finished)),
        ANY,
        [
            pltpu.VMEM((mid, rows, pair * rows), BF16),
            pltpu.SemaphoreType.DMA((mid, max(1, pair // 2))),
            pltpu.SemaphoreType.DMA((len(finished), mid)),
        ],
        flops=rows * head_width * width // 2,
        moved=4 * rows * width,
    )(logs_far, query, *other_b, far_c, out_a, out_b, out_c, out_d, out_e)


CUTS = 1
SLICE_ROOM = 21
PREPARE_ROOM = 24


def solution(mesh):
    rows = P(("groups", "seq", "head", "sub"), None)

    return jax.shard_map(
        per_device,
        mesh=mesh,
        in_specs=(
            rows,
            rows,
            rows,
            P(("head", "sub"), ("groups", "seq")),
            P(("head", "sub"), None),
            P("groups"),
        ),
        out_specs=rows,
        check_vma=False,
    )
```

```python
import functools

import jax
import jax.numpy as jnp
from jax import lax
from jax.experimental import pallas as pl
from jax.experimental.pallas import tpu as pltpu
from jax.sharding import PartitionSpec as P

BF16 = jnp.bfloat16
F32 = jnp.float32
ANY = pl.BlockSpec(memory_space=pl.ANY)
HBM = pl.BlockSpec(memory_space=pltpu.HBM)
VMEM = pl.BlockSpec(memory_space=pltpu.VMEM)
SMEM = pl.BlockSpec(memory_space=pltpu.SMEM)


def rotate(x, axis, step):
    size = lax.axis_size(axis)
    return lax.ppermute(x, axis, [(i, (i + step) % size) for i in range(size)])


def shift(x, axis, step):
    size = lax.axis_size(axis)
    return lax.ppermute(x, axis, [(i, i + step) for i in range(size - step)])


def fold(x):
    depth = lax.axis_size("seq")
    results = []
    for up in range(2):
        down = 1 - up
        pairs = []
        for z in range(depth):
            pairs.append((2 * z + up, 2 * (z + 1) + up if z < depth - 1 else 2 * z + down))
            pairs.append((2 * z + down, 2 * (z - 1) + down if z > 0 else 2 * z + up))
        results.append(lax.ppermute(x, ("seq", "sub"), pairs))
    return results


def of_core(refs, *index):
    if len(refs) == 1:
        return refs[0][index]
    return jnp.where(lax.axis_index("sub") == 0, refs[0][index], refs[1][index])


def column(row, rows):
    return jnp.broadcast_to(row, (rows, row.shape[1])).T


def call(body, out_shape, in_specs, out_specs, scratch=(), flops=0, moved=0, aliases=None, vmem=8 << 20):
    return pl.pallas_call(
        body,
        out_shape=out_shape,
        in_specs=in_specs,
        out_specs=out_specs,
        scratch_shapes=list(scratch),
        input_output_aliases=aliases or {},
        cost_estimate=pl.CostEstimate(flops=flops, bytes_accessed=moved, transcendentals=0),
        compiler_params=pltpu.CompilerParams(vmem_limit_bytes=vmem),
    )


def each(low, high, body):
    if high - low == 1:
        body(low)
    elif high > low:
        lax.fori_loop(low, high, lambda i, _: (body(i), 0)[1], 0)


def cols(place, c, width, count=1):
    start = (place * width[0] + c) * width[1]
    start = start if isinstance(start, int) else pl.multiple_of(start, width[1])
    return pl.ds(start, count * width[1])


def places(chips):
    base = 3 * chips
    return dict(to_start=base, to_end=base + 1, first=base + 2, row=base + 3, second=base + 4)


def pick(index, options):
    result = options[-1]
    for c in range(len(options) - 2, -1, -1):
        result = jnp.where(index == c, options[c], result)
    return result


def states_of(chips, weight, coef, own, far, n, i, keep):
    cores = 2
    core, chip = lax.axis_index("sub"), lax.axis_index("head")
    per_block, rows = weight.shape[2:]
    for c in range(per_block):
        here = slice(c * rows, (c + 1) * rows)
        sums = []
        for ref, block, place in ((own, i, core), (far, n, 1 - core)):
            keys = ref[0, block, :, here].T.astype(F32)
            keys = keys * weight[chip * cores + place, i, c : c + 1, :]
            values = ref[1, block, :, here]
            sums.append(jnp.dot(keys.astype(BF16), values, preferred_element_type=F32))
        first = jnp.where(core == 0, sums[0], sums[1])
        last = jnp.where(core == 0, sums[1], sums[0])
        keep(c, first, last + coef[places(chips)["second"], i, c : c + 1, :] * first)


def tables(chips, cores, decays, docs, logs, coef, weight, stack):
    chip = lax.axis_index("head")
    pieces = chips * cores
    per_block, rows = logs.shape[2:]
    at = places(chips)
    for slot in range(chips):
        for piece in range(pieces):
            place = (slot * pieces + piece) * per_block
            stack[0, place : place + per_block] = decays[slot][:, piece * rows : (piece + 1) * rows]
    earlier = lax.broadcasted_iota(jnp.int32, (rows, rows), 0)
    later = lax.broadcasted_iota(jnp.int32, (rows, rows), 1)
    stack[1] = jnp.dot(
        stack[0],
        jnp.where(earlier <= later, 1.0, 0.0),
        precision=lax.Precision.HIGHEST,
        preferred_element_type=F32,
    )
    for slot in range(chips):
        block = lax.rem(chip - slot + chips, chips)
        logs[pieces, block] = decays[slot][:, pieces * rows :]
        factors = []
        for piece in range(pieces):
            place = (slot * pieces + piece) * per_block
            total = stack[1, place : place + per_block]
            logs[piece, block] = total
            end = jnp.broadcast_to(total[:, rows - 1 :], (per_block, rows))
            weight[piece, block] = jnp.exp(end - total) * docs[1, piece : piece + 1, :]
            passed = jnp.broadcast_to(docs[2, piece : piece + 1, rows - 1 :], (per_block, rows))
            factors.append(jnp.exp(end) * passed)
        through = []
        for c in range(chips):
            product = factors[c * cores]
            for u in range(1, cores):
                product = product * factors[c * cores + u]
            through.append(product)
        one, zero = jnp.ones_like(through[0]), jnp.zeros_like(through[0])

        def between(low, high):
            product = one
            for c in range(low, high):
                product = product * through[c]
            return product

        to_start = pick(chip, [between(0, c) for c in range(chips)])
        coef[at["to_start"], block] = to_start
        coef[at["to_end"], block] = pick(chip, [between(0, c + 1) for c in range(chips)])
        coef[at["first"], block] = pick(chip, [factors[c * cores] for c in range(chips)])
        coef[at["second"], block] = pick(chip, [factors[c * cores + 1] for c in range(chips)])
        coef[at["row"], block] = between(0, chips)
        for back in range(chips):
            source = lax.rem(chip - back + chips, chips)
            coef[back, block] = pick(source, [between(c + 1, chips) for c in range(chips)])
            before = pick(
                chip,
                [between(c - back + 1, c) if 0 <= c - back < c else zero for c in range(chips)],
            )
            coef[chips + back, block] = before
            coef[2 * chips + back, block] = jnp.where(
                (source < chip) & (back > 0), before, to_start
            )


def states_a_body(chips, cores, *refs):
    decays, (docs, own, far) = refs[:chips], refs[chips : chips + 3]
    state_x, state_0, logs, coef, weight, stack = refs[chips + 3 :]
    tables(chips, cores, decays, docs, logs, coef, weight, stack)
    for i in range(chips // 2):

        def keep(c, first, state):
            state_0[i, c] = first
            state_x[i, c] = state.astype(BF16)

        states_of(chips, weight, coef, own, far, i, i, keep)


def states_b_body(chips, weight, coef, own, far, state_b, state_z, state_0):
    mid = chips // 2
    for n in range(mid):
        i = n + mid

        def keep(c, first, state):
            state_0[n, c] = first
            state_b[n, c] = state.astype(BF16)
            state_z[n, c] = (coef[0, i, c : c + 1, :] * state).astype(BF16)

        states_of(chips, weight, coef, own, far, n, i, keep)


def within_body(cores, far, blocks, logs, docs, q, kv, out, carry):
    core = lax.axis_index("sub")
    piece = lax.axis_index("head") * cores + core
    core = 1 - core if far else core
    per_block, rows = logs.shape[2], logs.shape[3]
    docs_here = jnp.broadcast_to(docs[0, pl.ds(piece, 1), :], (rows, rows))
    t = lax.broadcasted_iota(jnp.int32, (rows, rows), 0)
    s = lax.broadcasted_iota(jnp.int32, (rows, rows), 1)
    linked = (docs_here.T == docs_here) & (t >= s)
    carries = column(docs[2, pl.ds(piece, 1), :], rows)
    shift_ = blocks[0] if far else 0

    def heads_of(i):
        for c in range(per_block):
            here = slice(c * rows, (c + 1) * rows)
            row = logs[piece, i, c : c + 1, :]
            down = column(row, rows)
            damping = jnp.exp(jnp.where(linked, down - row, -1e30))
            scores = lax.dot_general(
                q[:, cols(i * cores + core, c, (per_block, rows))],
                kv[0, i - shift_, :, here],
                (((1,), (1,)), ((), ())),
                preferred_element_type=F32,
            )
            out[i - blocks[0], :, here] = jnp.dot(
                (scores * damping).astype(BF16), kv[1, i - shift_, :, here], preferred_element_type=F32
            )
            carry[i - blocks[0], :, here] = jnp.exp(down) * carries

    each(*blocks, heads_of)


def row_total_body(chips, coef, state_x, *refs):
    from_x, total = refs[:-1], refs[-1]

    def join(i):
        for c in range(state_x.shape[1]):
            sum_ = coef[0, i, c : c + 1, :] * state_x[i, c].astype(F32)
            for back in range(1, chips):
                sum_ = sum_ + coef[back, i, c : c + 1, :] * from_x[back - 1][i, c].astype(F32)
            total[i, c] = sum_.astype(BF16)

    each(0, chips // 2, join)


def messages_body(chips, parts, coef, state_b, *refs):
    past_b, messages = refs[:parts], refs[parts:]
    chip = lax.axis_index("head")
    mid = chips // 2

    def join(i):
        for c in range(state_b.shape[1]):
            past = of_core(past_b, i, c)
            factor = coef[places(chips)["to_end"], i + mid, c : c + 1, :]
            ahead = (state_b[i, c].astype(F32) + factor * past.astype(F32)).astype(BF16)
            for back in range(1, chips):
                messages[back - 1][i, c] = jnp.where(chip + back < chips, ahead, past)

    each(0, mid, join)


def entering_body(chips, half, parts, wanted, coef, first, *refs):
    past, others = refs[:parts], refs[parts : -len(wanted)]
    results = refs[-len(wanted) :]
    is_first = lax.axis_index("sub") == 0
    at = places(chips)
    mid = chips // 2
    base = (1 + half) * chips

    def join(i):
        for c in range(first.shape[1]):

            def factor(place):
                return coef[place, i + half * mid, c : c + 1, :]

            entering = factor(at["to_start"]) * of_core(past, i, c).astype(F32)
            for back in range(1, chips):
                entering = entering + factor(base + back) * others[back - 1][i, c].astype(F32)
            later = first[i, c] + factor(at["first"]) * entering
            for sent, result in zip(wanted, results):
                here, there = (later, entering) if sent else (entering, later)
                result[i, c] = jnp.where(is_first, here, there).astype(BF16)

    each(0, mid, join)


def finish_heads(chips, cores, far, half, logs, q, within, carry, state, n, put):
    core = lax.axis_index("sub")
    core = 1 - core if far else core
    i = n + half * (chips // 2)
    per_block, rows = logs.shape[2:]
    gain = logs[chips * cores, i]
    for c in range(per_block):
        here = slice(c * rows, (c + 1) * rows)
        result = within[n, :, here] + carry[n, :, here] * jnp.dot(
            q[:, cols(i * cores + core, c, (per_block, rows))],
            state[n, c],
            preferred_element_type=F32,
        )
        mean_square = jnp.mean(result * result, axis=1, keepdims=True)
        put(here, (result * lax.rsqrt(mean_square + 1e-06) * gain[c : c + 1, :]).astype(BF16))


def finish_body(chips, cores, far, half, logs, q, within, carry, state, out):

    def block(n):
        def put(here, value):
            out[n, :, here] = value

        finish_heads(chips, cores, far, half, logs, q, within, carry, state, n, put)

    each(0, chips // 2, block)


def last_body(chips, cores, logs, q, within, carry, state, *refs):
    finished = refs[:3]
    out, buffer, sem, done_sem = refs[3:]
    core = lax.axis_index("sub")
    mid = chips // 2
    half = 1
    rows, width = buffer.shape[1:]

    def copy(source, i, place, sem):
        target = out.at[:, cols(i * cores + place, 0, (1, width))]
        return pltpu.make_async_copy(source, target, sem)

    copies = []
    for k, (which, place) in enumerate(((0, core), (1, core), (0, 1 - core))):
        for n in range(mid):
            copies.append(copy(finished[k].at[n], n + which * mid, place, done_sem.at[k, n]))
            copies[-1].start()
    for n in range(mid):

        def put(here, value):
            buffer[n, :, here] = value
            c = here.stop // rows - 1
            if c % 2 == 1:
                pair = slice(here.stop - 2 * rows, here.stop)
                place = cols((n + half * mid) * cores + 1 - core, c - 1, (width // rows, rows), 2)
                copies.append(
                    pltpu.make_async_copy(
                        buffer.at[n, :, pair], out.at[:, place], sem.at[n, c // 2]
                    )
                )
                copies[-1].start()

        finish_heads(chips, cores, True, half, logs, q, within, carry, state, n, put)
    for one in copies:
        one.wait()


def block_copies(cores, core, blocks, sources, target, sems):
    width = target.shape[3]
    parts = sems.shape[2]
    rows = target.shape[2] // parts
    return [
        pltpu.make_async_copy(
            source.at[part * rows : (part + 1) * rows, cols(i * cores + core, 0, (1, width))],
            target.at[n, i - blocks[0], part * rows : (part + 1) * rows],
            sems.at[n, i - blocks[0], part],
        )
        for n, source in enumerate(sources)
        for i in range(*blocks)
        for part in range(parts)
    ]


def slice_body(chips, cores, k_all, v_all, send, sems):
    core = 1 - lax.axis_index("sub")
    copies = block_copies(cores, core, (0, chips // 2), (k_all, v_all), send, sems)
    for copy in copies:
        copy.start()
    for copy in copies:
        copy.wait()


def pack_body(log_decay, gain, packed):
    packed[:, : log_decay.shape[1]] = log_decay[...]
    packed[:, log_decay.shape[1] :] = gain[...]


def prepare_body(chips, cores, lengths_all, k_all, v_all, send, own, docs, *scratch):
    lengths, send_sems, own_sems, length_sem = scratch
    core = lax.axis_index("sub")
    both = (k_all, v_all)
    copies = block_copies(cores, 1 - core, (chips // 2, chips), both, send, send_sems)
    copies += block_copies(cores, core, (0, chips), both, own, own_sems)
    lengths_copy = pltpu.make_async_copy(lengths_all, lengths, length_sem)
    lengths_copy.start()
    for copy in copies:
        copy.start()
    lengths_copy.wait()
    pieces, rows = docs.shape[1:]
    piece = lax.broadcasted_iota(jnp.int32, (pieces, rows), 0)
    lane = lax.broadcasted_iota(jnp.int32, (pieces, rows), 1)
    first = (lax.axis_index("seq") * pieces + piece) * rows
    here, before = jnp.zeros((pieces, rows), F32), jnp.zeros((pieces, rows), F32)
    start = 0
    for n in range(lengths.shape[0]):
        here += jnp.where(start <= first + lane, 1.0, 0.0)
        before += jnp.where(start < first, 1.0, 0.0)
        start = start + lengths[n]
    end = jnp.broadcast_to(here[:, rows - 1 :], (pieces, rows))
    docs[0] = here
    docs[1] = jnp.where(here == end, 1.0, 0.0)
    docs[2] = jnp.where(here == before, 1.0, 0.0)
    for copy in copies:
        copy.wait()


def earlier_rows(value, row_factor, blocks, reach):
    if reach == 1:
        return fold(value)
    total, step = value, 1
    factor = row_factor[blocks] if reach > 1 else None
    while step < reach:
        before = shift(total, "seq", step).astype(F32)
        total = (total.astype(F32) + factor[:, :, None, :] * before).astype(BF16)
        factor = factor * shift(factor, "seq", step)
        step *= 2
    return [shift(total, "seq", 1)]


def per_device(query, key, value, log_decay, gain, doc_lengths):
    rows, width = query.shape
    per_block, row_tokens = log_decay.shape
    head_width = gain.shape[1]
    chips, cores, depth = lax.axis_size("head"), lax.axis_size("sub"), lax.axis_size("seq")
    assert cores == 2 and chips % 2 == 0 and rows == head_width
    pieces = chips * cores
    others = chips - 1
    mid = chips // 2
    reach = max(1, -(-depth // 4))

    def sds(shape, kind):
        return jax.ShapeDtypeStruct(shape, kind)

    square = (per_block, head_width, head_width)
    area = per_block * head_width * head_width
    block = (chips, rows, per_block * head_width)
    half = sds((mid,) + square, BF16)
    half_wide = sds((mid,) + square, F32)
    log_shape = (pieces + 1, chips, per_block, rows)
    coef_shape = (3 * chips + 5, chips, per_block, rows)

    half_kv = sds((2, mid) + block[1:], BF16)
    send_low = call(
        functools.partial(slice_body, chips, cores),
        half_kv,
        [HBM] * 2,
        VMEM,
        [pltpu.SemaphoreType.DMA((2, mid, CUTS))],
        moved=4 * rows * width,
        vmem=67043328 - SLICE_ROOM * rows * width,
    )(key, value)
    far_low = rotate(send_low, "sub", 1)
    packed = call(
        pack_body,
        sds((per_block, row_tokens + head_width), F32),
        [VMEM] * 2,
        VMEM,
    )(log_decay, gain)
    decays = [packed] + [rotate(packed, "head", k) for k in range(1, chips)]
    send_high, own, docs = call(
        functools.partial(prepare_body, chips, cores),
        [half_kv, sds((2,) + block, BF16), sds((3, pieces, rows), F32)],
        [HBM] * 3,
        [VMEM] * 3,
        [
            pltpu.SMEM(doc_lengths.shape, jnp.int32),
            pltpu.SemaphoreType.DMA((2, mid, CUTS)),
            pltpu.SemaphoreType.DMA((2, chips, CUTS)),
            pltpu.SemaphoreType.DMA(()),
        ],
        moved=12 * rows * width,
        vmem=67043328 - PREPARE_ROOM * rows * width,
    )(doc_lengths, key, value)
    far_high = rotate(send_high, "sub", 1)

    state_x, first_a, logs, coef, weight = call(
        functools.partial(states_a_body, chips, cores),
        [half, half_wide]
        + [sds(log_shape, F32), sds(coef_shape, F32), sds((pieces,) + log_shape[1:], F32)],
        [VMEM] * (chips + 3),
        [VMEM] * 5,
        [pltpu.VMEM((2, chips * pieces * per_block, rows), F32)],
        flops=2 * rows * chips * area,
        moved=8 * chips * area,
    )(*decays, docs, own, far_low)
    from_x = [rotate(state_x, "head", k) for k in range(1, chips)]
    state_b, state_z, first_b = call(
        functools.partial(states_b_body, chips),
        [half, half, half_wide],
        [VMEM] * 4,
        [VMEM] * 3,
        flops=2 * rows * chips * area,
        moved=8 * chips * area,
    )(weight, coef, own, far_high)
    row_factor = coef[places(chips)["row"]] if reach > 1 else None
    past_b = earlier_rows(state_z, row_factor, slice(mid, chips), reach)
    logs_far = rotate(logs, "sub", 1)

    def within(far, blocks, *args):
        return call(
            functools.partial(within_body, cores, far, blocks),
            [sds((mid,) + block[1:], F32)] * 2,
            [VMEM] * 4,
            [VMEM] * 2,
            flops=rows * rows * width,
            moved=4 * rows * width,
        )(*args)

    low, high = (0, mid), (mid, chips)
    own_a = within(False, low, logs, docs, query, own)

    total = call(
        functools.partial(row_total_body, chips),
        half,
        [VMEM] * (2 + others),
        VMEM,
        moved=6 * mid * area,
    )(coef, state_x, *from_x)
    past_a = earlier_rows(total, row_factor, slice(0, mid), reach)

    messages = call(
        functools.partial(messages_body, chips, len(past_b)),
        [half] * others,
        [VMEM] * (2 + len(past_b)),
        [VMEM] * others,
        moved=6 * mid * area,
    )(coef, state_b, *past_b)
    from_b = [rotate(messages[k - 1], "head", k) for k in range(1, chips)]

    own_b = within(False, high, logs, docs, query, own)
    other_a = within(True, low, logs_far, docs, query, send_low)
    other_b = within(True, high, logs_far, docs, query, send_high)

    def entering(which, wanted, first, past, arrived):
        return call(
            functools.partial(entering_body, chips, which, len(past), wanted),
            [half] * len(wanted),
            [VMEM] * (2 + len(past) + others),
            [VMEM] * len(wanted),
            moved=8 * mid * area,
        )(coef, first, *past, *arrived)

    def finish(far, which, logs_used, local, state):
        return call(
            functools.partial(finish_body, chips, cores, far, which),
            sds((mid,) + block[1:], BF16),
            [VMEM] * 5,
            VMEM,
            flops=rows * head_width * width // 2,
            moved=3 * rows * width,
        )(logs_used, query, *local, state)

    keep_a, send_a = entering(0, (False, True), first_a, past_a, from_x)
    far_a = rotate(send_a, "sub", 1)
    out_a = finish(False, 0, logs, own_a, keep_a)
    (send_b,) = entering(1, (True,), first_b, past_b, from_b)
    far_b = rotate(send_b, "sub", 1)
    (keep_b,) = entering(1, (False,), first_b, past_b, from_b)
    out_b = finish(False, 1, logs, own_b, keep_b)
    out_far = finish(True, 0, logs_far, other_a, far_a)
    return call(
        functools.partial(last_body, chips, cores),
        sds((rows, width), BF16),
        [VMEM] * 8,
        ANY,
        [
            pltpu.VMEM((mid,) + block[1:], BF16),
            pltpu.SemaphoreType.DMA((mid, per_block // 2)),
            pltpu.SemaphoreType.DMA((3, mid)),
        ],
        flops=rows * head_width * width // 2,
        moved=4 * rows * width,
    )(logs_far, query, *other_b, far_b, out_a, out_b, out_far)


CUTS = 1
SLICE_ROOM = 21
PREPARE_ROOM = 24


def solution(mesh):
    rows = P(("groups", "seq", "head", "sub"), None)

    return jax.shard_map(
        per_device,
        mesh=mesh,
        in_specs=(
            rows,
            rows,
            rows,
            P(("head", "sub"), ("groups", "seq")),
            P(("head", "sub"), None),
            P("groups"),
        ),
        out_specs=rows,
        check_vma=False,
    )
```

```python
import functools

import jax
import jax.numpy as jnp
from jax import lax
from jax.experimental import pallas as pl
from jax.experimental.pallas import tpu as pltpu
from jax.sharding import PartitionSpec as P

BF16 = jnp.bfloat16
F32 = jnp.float32
ANY = pl.BlockSpec(memory_space=pl.ANY)
HBM = pl.BlockSpec(memory_space=pltpu.HBM)
VMEM = pl.BlockSpec(memory_space=pltpu.VMEM)
SMEM = pl.BlockSpec(memory_space=pltpu.SMEM)


def rotate(x, axis, step):
    size = lax.axis_size(axis)
    return lax.ppermute(x, axis, [(i, (i + step) % size) for i in range(size)])


def shift(x, axis, step):
    size = lax.axis_size(axis)
    return lax.ppermute(x, axis, [(i, i + step) for i in range(size - step)])


def fold(x):
    depth = lax.axis_size("seq")
    results = []
    for up in range(2):
        down = 1 - up
        pairs = []
        for z in range(depth):
            pairs.append((2 * z + up, 2 * (z + 1) + up if z < depth - 1 else 2 * z + down))
            pairs.append((2 * z + down, 2 * (z - 1) + down if z > 0 else 2 * z + up))
        results.append(lax.ppermute(x, ("seq", "sub"), pairs))
    return results


def of_core(refs, *index):
    if len(refs) == 1:
        return refs[0][index]
    return jnp.where(lax.axis_index("sub") == 0, refs[0][index], refs[1][index])


def column(row, rows):
    return jnp.broadcast_to(row, (rows, row.shape[1])).T


def call(body, out_shape, in_specs, out_specs, scratch=(), flops=0, moved=0, aliases=None, vmem=8 << 20):
    return pl.pallas_call(
        body,
        out_shape=out_shape,
        in_specs=in_specs,
        out_specs=out_specs,
        scratch_shapes=list(scratch),
        input_output_aliases=aliases or {},
        cost_estimate=pl.CostEstimate(flops=flops, bytes_accessed=moved, transcendentals=0),
        compiler_params=pltpu.CompilerParams(vmem_limit_bytes=vmem),
    )


def each(low, high, body):
    if high - low == 1:
        body(low)
    elif high > low:
        lax.fori_loop(low, high, lambda i, _: (body(i), 0)[1], 0)


def cols(place, c, width, count=1):
    start = (place * width[0] + c) * width[1]
    start = start if isinstance(start, int) else pl.multiple_of(start, width[1])
    return pl.ds(start, count * width[1])


def places(chips):
    base = 3 * chips
    return dict(to_start=base, to_end=base + 1, first=base + 2, row=base + 3, second=base + 4)


def pick(index, options):
    result = options[-1]
    for c in range(len(options) - 2, -1, -1):
        result = jnp.where(index == c, options[c], result)
    return result


def states_of(chips, weight, coef, own, far, n, i, keep):
    cores = 2
    core, chip = lax.axis_index("sub"), lax.axis_index("head")
    per_block, rows = weight.shape[2:]
    for c in range(per_block):
        here = slice(c * rows, (c + 1) * rows)
        sums = []
        for ref, block, place in ((own, i, core), (far, n, 1 - core)):
            keys = ref[0, block, :, here].T.astype(F32)
            keys = keys * weight[chip * cores + place, i, c : c + 1, :]
            values = ref[1, block, :, here]
            sums.append(jnp.dot(keys.astype(BF16), values, preferred_element_type=F32))
        first = jnp.where(core == 0, sums[0], sums[1])
        last = jnp.where(core == 0, sums[1], sums[0])
        keep(c, first, last + coef[places(chips)["second"], i, c : c + 1, :] * first)


def tables(chips, cores, decays, docs, logs, coef, weight, stack):
    chip = lax.axis_index("head")
    pieces = chips * cores
    per_block, rows = logs.shape[2:]
    at = places(chips)
    for slot in range(chips):
        for piece in range(pieces):
            place = (slot * pieces + piece) * per_block
            stack[0, place : place + per_block] = decays[slot][:, piece * rows : (piece + 1) * rows]
    earlier = lax.broadcasted_iota(jnp.int32, (rows, rows), 0)
    later = lax.broadcasted_iota(jnp.int32, (rows, rows), 1)
    stack[1] = jnp.dot(
        stack[0],
        jnp.where(earlier <= later, 1.0, 0.0),
        precision=lax.Precision.HIGHEST,
        preferred_element_type=F32,
    )
    for slot in range(chips):
        block = lax.rem(chip - slot + chips, chips)
        logs[pieces, block] = decays[slot][:, pieces * rows :]
        factors = []
        for piece in range(pieces):
            place = (slot * pieces + piece) * per_block
            total = stack[1, place : place + per_block]
            logs[piece, block] = total
            end = jnp.broadcast_to(total[:, rows - 1 :], (per_block, rows))
            weight[piece, block] = jnp.exp(end - total) * docs[1, piece : piece + 1, :]
            passed = jnp.broadcast_to(docs[2, piece : piece + 1, rows - 1 :], (per_block, rows))
            factors.append(jnp.exp(end) * passed)
        through = []
        for c in range(chips):
            product = factors[c * cores]
            for u in range(1, cores):
                product = product * factors[c * cores + u]
            through.append(product)
        one, zero = jnp.ones_like(through[0]), jnp.zeros_like(through[0])

        def between(low, high):
            product = one
            for c in range(low, high):
                product = product * through[c]
            return product

        to_start = pick(chip, [between(0, c) for c in range(chips)])
        coef[at["to_start"], block] = to_start
        coef[at["to_end"], block] = pick(chip, [between(0, c + 1) for c in range(chips)])
        coef[at["first"], block] = pick(chip, [factors[c * cores] for c in range(chips)])
        coef[at["second"], block] = pick(chip, [factors[c * cores + 1] for c in range(chips)])
        coef[at["row"], block] = between(0, chips)
        for back in range(chips):
            source = lax.rem(chip - back + chips, chips)
            coef[back, block] = pick(source, [between(c + 1, chips) for c in range(chips)])
            before = pick(
                chip,
                [between(c - back + 1, c) if 0 <= c - back < c else zero for c in range(chips)],
            )
            coef[chips + back, block] = before
            coef[2 * chips + back, block] = jnp.where(
                (source < chip) & (back > 0), before, to_start
            )


def states_a_body(chips, cores, *refs):
    decays, (docs, own, far) = refs[:chips], refs[chips : chips + 3]
    state_x, state_0, logs, coef, weight, stack = refs[chips + 3 :]
    tables(chips, cores, decays, docs, logs, coef, weight, stack)
    for i in range(chips // 2):

        def keep(c, first, state):
            state_0[i, c] = first
            state_x[i, c] = state.astype(BF16)

        states_of(chips, weight, coef, own, far, i, i, keep)


def states_b_body(chips, weight, coef, own, far, state_b, state_z, state_0):
    mid = chips // 2
    for n in range(mid):
        i = n + mid

        def keep(c, first, state):
            state_0[n, c] = first
            state_b[n, c] = state.astype(BF16)
            state_z[n, c] = (coef[0, i, c : c + 1, :] * state).astype(BF16)

        states_of(chips, weight, coef, own, far, n, i, keep)


def within_body(cores, far, blocks, logs, docs, q, kv, out, carry):
    core = lax.axis_index("sub")
    piece = lax.axis_index("head") * cores + core
    core = 1 - core if far else core
    per_block, rows = logs.shape[2], logs.shape[3]
    docs_here = jnp.broadcast_to(docs[0, pl.ds(piece, 1), :], (rows, rows))
    t = lax.broadcasted_iota(jnp.int32, (rows, rows), 0)
    s = lax.broadcasted_iota(jnp.int32, (rows, rows), 1)
    linked = (docs_here.T == docs_here) & (t >= s)
    carries = column(docs[2, pl.ds(piece, 1), :], rows)
    shift_ = blocks[0] if far else 0

    def heads_of(i):
        for c in range(per_block):
            here = slice(c * rows, (c + 1) * rows)
            row = logs[piece, i, c : c + 1, :]
            down = column(row, rows)
            damping = jnp.exp(jnp.where(linked, down - row, -1e30))
            scores = lax.dot_general(
                q[:, cols(i * cores + core, c, (per_block, rows))],
                kv[0, i - shift_, :, here],
                (((1,), (1,)), ((), ())),
                preferred_element_type=F32,
            )
            out[i - blocks[0], :, here] = jnp.dot(
                (scores * damping).astype(BF16), kv[1, i - shift_, :, here], preferred_element_type=F32
            )
            carry[i - blocks[0], :, here] = jnp.exp(down) * carries

    each(*blocks, heads_of)


def row_total_body(chips, coef, state_x, *refs):
    from_x, total = refs[:-1], refs[-1]

    def join(i):
        for c in range(state_x.shape[1]):
            sum_ = coef[0, i, c : c + 1, :] * state_x[i, c].astype(F32)
            for back in range(1, chips):
                sum_ = sum_ + coef[back, i, c : c + 1, :] * from_x[back - 1][i, c].astype(F32)
            total[i, c] = sum_.astype(BF16)

    each(0, chips // 2, join)


def messages_body(chips, parts, coef, state_b, *refs):
    past_b, messages = refs[:parts], refs[parts:]
    chip = lax.axis_index("head")
    mid = chips // 2

    def join(i):
        for c in range(state_b.shape[1]):
            past = of_core(past_b, i, c)
            factor = coef[places(chips)["to_end"], i + mid, c : c + 1, :]
            ahead = (state_b[i, c].astype(F32) + factor * past.astype(F32)).astype(BF16)
            for back in range(1, chips):
                messages[back - 1][i, c] = jnp.where(chip + back < chips, ahead, past)

    each(0, mid, join)


def entering_body(chips, half, parts, coef, first, *refs):
    past, others = refs[:parts], refs[parts:-2]
    keep, send = refs[-2:]
    is_first = lax.axis_index("sub") == 0
    at = places(chips)
    mid = chips // 2
    base = (1 + half) * chips

    def join(i):
        for c in range(keep.shape[1]):

            def factor(place):
                return coef[place, i + half * mid, c : c + 1, :]

            entering = factor(at["to_start"]) * of_core(past, i, c).astype(F32)
            for back in range(1, chips):
                entering = entering + factor(base + back) * others[back - 1][i, c].astype(F32)
            later = first[i, c] + factor(at["first"]) * entering
            keep[i, c] = jnp.where(is_first, entering, later).astype(BF16)
            send[i, c] = jnp.where(is_first, later, entering).astype(BF16)

    each(0, mid, join)


def finish_heads(chips, cores, far, half, logs, q, within, carry, state, n, put):
    core = lax.axis_index("sub")
    core = 1 - core if far else core
    i = n + half * (chips // 2)
    per_block, rows = logs.shape[2:]
    gain = logs[chips * cores, i]
    for c in range(per_block):
        here = slice(c * rows, (c + 1) * rows)
        result = within[n, :, here] + carry[n, :, here] * jnp.dot(
            q[:, cols(i * cores + core, c, (per_block, rows))],
            state[n, c],
            preferred_element_type=F32,
        )
        mean_square = jnp.mean(result * result, axis=1, keepdims=True)
        put(here, (result * lax.rsqrt(mean_square + 1e-06) * gain[c : c + 1, :]).astype(BF16))


def finish_body(chips, cores, far, half, logs, q, within, carry, state, out):

    def block(n):
        def put(here, value):
            out[n, :, here] = value

        finish_heads(chips, cores, far, half, logs, q, within, carry, state, n, put)

    each(0, chips // 2, block)


def last_body(chips, cores, logs, q, within, carry, state, *refs):
    finished = refs[:3]
    out, buffer, sem, done_sem = refs[3:]
    core = lax.axis_index("sub")
    mid = chips // 2
    half = 1
    rows, width = buffer.shape[1:]

    def copy(source, i, place, sem):
        target = out.at[:, cols(i * cores + place, 0, (1, width))]
        return pltpu.make_async_copy(source, target, sem)

    copies = []
    for k, (which, place) in enumerate(((0, core), (1, core), (0, 1 - core))):
        for n in range(mid):
            copies.append(copy(finished[k].at[n], n + which * mid, place, done_sem.at[k, n]))
            copies[-1].start()
    for n in range(mid):

        def put(here, value):
            buffer[n, :, here] = value
            c = here.stop // rows - 1
            if c % 2 == 1:
                pair = slice(here.stop - 2 * rows, here.stop)
                place = cols((n + half * mid) * cores + 1 - core, c - 1, (width // rows, rows), 2)
                copies.append(
                    pltpu.make_async_copy(
                        buffer.at[n, :, pair], out.at[:, place], sem.at[n, c // 2]
                    )
                )
                copies[-1].start()

        finish_heads(chips, cores, True, half, logs, q, within, carry, state, n, put)
    for one in copies:
        one.wait()


def block_copies(cores, core, blocks, sources, target, sems):
    width = target.shape[3]
    parts = sems.shape[2]
    rows = target.shape[2] // parts
    return [
        pltpu.make_async_copy(
            source.at[part * rows : (part + 1) * rows, cols(i * cores + core, 0, (1, width))],
            target.at[n, i - blocks[0], part * rows : (part + 1) * rows],
            sems.at[n, i - blocks[0], part],
        )
        for n, source in enumerate(sources)
        for i in range(*blocks)
        for part in range(parts)
    ]


def slice_body(chips, cores, k_all, v_all, send, sems):
    core = 1 - lax.axis_index("sub")
    copies = block_copies(cores, core, (0, chips // 2), (k_all, v_all), send, sems)
    for copy in copies:
        copy.start()
    for copy in copies:
        copy.wait()


def pack_body(log_decay, gain, packed):
    packed[:, : log_decay.shape[1]] = log_decay[...]
    packed[:, log_decay.shape[1] :] = gain[...]


def prepare_body(chips, cores, lengths_all, k_all, v_all, send, own, docs, *scratch):
    lengths, send_sems, own_sems, length_sem = scratch
    core = lax.axis_index("sub")
    both = (k_all, v_all)
    copies = block_copies(cores, 1 - core, (chips // 2, chips), both, send, send_sems)
    copies += block_copies(cores, core, (0, chips), both, own, own_sems)
    lengths_copy = pltpu.make_async_copy(lengths_all, lengths, length_sem)
    lengths_copy.start()
    for copy in copies:
        copy.start()
    lengths_copy.wait()
    pieces, rows = docs.shape[1:]
    piece = lax.broadcasted_iota(jnp.int32, (pieces, rows), 0)
    lane = lax.broadcasted_iota(jnp.int32, (pieces, rows), 1)
    first = (lax.axis_index("seq") * pieces + piece) * rows
    here, before = jnp.zeros((pieces, rows), F32), jnp.zeros((pieces, rows), F32)
    start = 0
    for n in range(lengths.shape[0]):
        here += jnp.where(start <= first + lane, 1.0, 0.0)
        before += jnp.where(start < first, 1.0, 0.0)
        start = start + lengths[n]
    end = jnp.broadcast_to(here[:, rows - 1 :], (pieces, rows))
    docs[0] = here
    docs[1] = jnp.where(here == end, 1.0, 0.0)
    docs[2] = jnp.where(here == before, 1.0, 0.0)
    for copy in copies:
        copy.wait()


def earlier_rows(value, row_factor, blocks, reach):
    if reach == 1:
        return fold(value)
    total, step = value, 1
    factor = row_factor[blocks] if reach > 1 else None
    while step < reach:
        before = shift(total, "seq", step).astype(F32)
        total = (total.astype(F32) + factor[:, :, None, :] * before).astype(BF16)
        factor = factor * shift(factor, "seq", step)
        step *= 2
    return [shift(total, "seq", 1)]


def per_device(query, key, value, log_decay, gain, doc_lengths):
    rows, width = query.shape
    per_block, row_tokens = log_decay.shape
    head_width = gain.shape[1]
    chips, cores, depth = lax.axis_size("head"), lax.axis_size("sub"), lax.axis_size("seq")
    assert cores == 2 and chips % 2 == 0 and rows == head_width
    pieces = chips * cores
    others = chips - 1
    mid = chips // 2
    reach = max(1, -(-depth // 4))

    def sds(shape, kind):
        return jax.ShapeDtypeStruct(shape, kind)

    square = (per_block, head_width, head_width)
    area = per_block * head_width * head_width
    block = (chips, rows, per_block * head_width)
    half = sds((mid,) + square, BF16)
    half_wide = sds((mid,) + square, F32)
    log_shape = (pieces + 1, chips, per_block, rows)
    coef_shape = (3 * chips + 5, chips, per_block, rows)

    half_kv = sds((2, mid) + block[1:], BF16)
    send_low = call(
        functools.partial(slice_body, chips, cores),
        half_kv,
        [HBM] * 2,
        VMEM,
        [pltpu.SemaphoreType.DMA((2, mid, CUTS))],
        moved=4 * rows * width,
        vmem=67043328 - SLICE_ROOM * rows * width,
    )(key, value)
    far_low = rotate(send_low, "sub", 1)
    packed = call(
        pack_body,
        sds((per_block, row_tokens + head_width), F32),
        [VMEM] * 2,
        VMEM,
    )(log_decay, gain)
    decays = [packed] + [rotate(packed, "head", k) for k in range(1, chips)]
    send_high, own, docs = call(
        functools.partial(prepare_body, chips, cores),
        [half_kv, sds((2,) + block, BF16), sds((3, pieces, rows), F32)],
        [HBM] * 3,
        [VMEM] * 3,
        [
            pltpu.SMEM(doc_lengths.shape, jnp.int32),
            pltpu.SemaphoreType.DMA((2, mid, CUTS)),
            pltpu.SemaphoreType.DMA((2, chips, CUTS)),
            pltpu.SemaphoreType.DMA(()),
        ],
        moved=12 * rows * width,
        vmem=67043328 - PREPARE_ROOM * rows * width,
    )(doc_lengths, key, value)
    far_high = rotate(send_high, "sub", 1)

    state_x, first_a, logs, coef, weight = call(
        functools.partial(states_a_body, chips, cores),
        [half, half_wide]
        + [sds(log_shape, F32), sds(coef_shape, F32), sds((pieces,) + log_shape[1:], F32)],
        [VMEM] * (chips + 3),
        [VMEM] * 5,
        [pltpu.VMEM((2, chips * pieces * per_block, rows), F32)],
        flops=2 * rows * chips * area,
        moved=8 * chips * area,
    )(*decays, docs, own, far_low)
    from_x = [rotate(state_x, "head", k) for k in range(1, chips)]
    state_b, state_z, first_b = call(
        functools.partial(states_b_body, chips),
        [half, half, half_wide],
        [VMEM] * 4,
        [VMEM] * 3,
        flops=2 * rows * chips * area,
        moved=8 * chips * area,
    )(weight, coef, own, far_high)
    row_factor = coef[places(chips)["row"]] if reach > 1 else None
    past_b = earlier_rows(state_z, row_factor, slice(mid, chips), reach)
    logs_far = rotate(logs, "sub", 1)

    def within(far, blocks, *args):
        return call(
            functools.partial(within_body, cores, far, blocks),
            [sds((mid,) + block[1:], F32)] * 2,
            [VMEM] * 4,
            [VMEM] * 2,
            flops=rows * rows * width,
            moved=4 * rows * width,
        )(*args)

    low, high = (0, mid), (mid, chips)
    own_a = within(False, low, logs, docs, query, own)

    total = call(
        functools.partial(row_total_body, chips),
        half,
        [VMEM] * (2 + others),
        VMEM,
        moved=6 * mid * area,
    )(coef, state_x, *from_x)
    past_a = earlier_rows(total, row_factor, slice(0, mid), reach)

    messages = call(
        functools.partial(messages_body, chips, len(past_b)),
        [half] * others,
        [VMEM] * (2 + len(past_b)),
        [VMEM] * others,
        moved=6 * mid * area,
    )(coef, state_b, *past_b)
    from_b = [rotate(messages[k - 1], "head", k) for k in range(1, chips)]

    own_b = within(False, high, logs, docs, query, own)
    other_a = within(True, low, logs_far, docs, query, send_low)
    other_b = within(True, high, logs_far, docs, query, send_high)

    def entering(which, first, past, arrived):
        return call(
            functools.partial(entering_body, chips, which, len(past)),
            [half] * 2,
            [VMEM] * (2 + len(past) + others),
            [VMEM] * 2,
            moved=8 * mid * area,
        )(coef, first, *past, *arrived)

    def finish(far, which, logs_used, local, state):
        return call(
            functools.partial(finish_body, chips, cores, far, which),
            sds((mid,) + block[1:], BF16),
            [VMEM] * 5,
            VMEM,
            flops=rows * head_width * width // 2,
            moved=3 * rows * width,
        )(logs_used, query, *local, state)

    keep_a, send_a = entering(0, first_a, past_a, from_x)
    far_a = rotate(send_a, "sub", 1)
    out_a = finish(False, 0, logs, own_a, keep_a)
    keep_b, send_b = entering(1, first_b, past_b, from_b)
    far_b = rotate(send_b, "sub", 1)
    out_b = finish(False, 1, logs, own_b, keep_b)
    out_far = finish(True, 0, logs_far, other_a, far_a)
    return call(
        functools.partial(last_body, chips, cores),
        sds((rows, width), BF16),
        [VMEM] * 8,
        ANY,
        [
            pltpu.VMEM((mid,) + block[1:], BF16),
            pltpu.SemaphoreType.DMA((mid, per_block // 2)),
            pltpu.SemaphoreType.DMA((3, mid)),
        ],
        flops=rows * head_width * width // 2,
        moved=4 * rows * width,
    )(logs_far, query, *other_b, far_b, out_a, out_b, out_far)


CUTS = 1
SLICE_ROOM = 21
PREPARE_ROOM = 24


def solution(mesh):
    rows = P(("groups", "seq", "head", "sub"), None)

    return jax.shard_map(
        per_device,
        mesh=mesh,
        in_specs=(
            rows,
            rows,
            rows,
            P(("head", "sub"), ("groups", "seq")),
            P(("head", "sub"), None),
            P("groups"),
        ),
        out_specs=rows,
        check_vma=False,
    )
```
